32 devices in a mesh: dp: 4 (over x, core), expert: 8 (over z, y).
Axes of the slice: x: 2, y: 2, z: 4, core: 2. Of those that a mesh axis runs over, the one named last changes fastest.
Arguments:
- tokens: bfloat16 [2, 32, 256, 1024], P(None, ('dp', 'expert')), may hold values from -6 to 6
- parents: int32 [2, 32, 13], P(None, ('dp', 'expert')), may hold values from 0 to 4, as said below
- routes: int32 [2, 32, 256, 8], P(None, ('dp', 'expert')), may hold values from 0 to 31, all different within a row; in each aligned block of 256 rows (0 to 255, 256 to 511, ..., all dimensions but the last counted through in order) at most 72 rows name the same one
- gain_attn: float32 [1024], replicated, may hold values from 0.5 to 1.5
- w_query: bfloat16 [1024, 1024], P('dp'), may hold values from -2 to 2
- key_matrix: bfloat16 [1024, 512], P('dp'), may hold values from -0.1875 to 0.1875
- value_matrix: bfloat16 [1024, 512], P('dp'), may hold values from -0.1875 to 0.1875
- w_out: bfloat16 [1024, 1024], P(None, 'dp'), may hold values from -3 to 3
- gain_moe: float32 [1024], replicated, may hold values from 0.5 to 1.5
- router: bfloat16 [1024, 32], P('dp'), may hold values from -0.09375 to 0.09375
- expert_gate_up: bfloat16 [32, 1024, 1024], P('expert', 'dp'), may hold values from -0.1875 to 0.1875
- expert_down: bfloat16 [32, 512, 1024], P('expert', None, 'dp'), may hold values from -4 to 4
- cotangent: bfloat16 [2, 32, 256, 1024], P(None, ('dp', 'expert')), may hold values from -6 to 6
Outputs:
- output: bfloat16 [2, 32, 256, 1024], P(None, ('dp', 'expert'))
- grad_tokens: float32 [2, 32, 256, 1024], P(None, ('dp', 'expert'))
- grad_gain_attn: float32 [1024], P(('dp', 'expert'))
- grad_w_query: float32 [1024, 1024], P(('dp', 'expert'))
- grad_w_key: float32 [1024, 512], P(('dp', 'expert'))
- grad_w_value: float32 [1024, 512], P(('dp', 'expert'))
- grad_w_out: float32 [1024, 1024], P(None, ('dp', 'expert'))
- grad_gain_moe: float32 [1024], P(('dp', 'expert'))
- grad_router: float32 [1024, 32], P(('dp', 'expert'))
- grad_expert_gate_up: float32 [32, 1024, 1024], P('expert', 'dp')
- grad_expert_down: float32 [32, 512, 1024], P('expert', None, 'dp')
The draws below stay inside these ranges and needn't reach their ends.
Inputs may be any that keep to these rules, and one draw needn't show every extreme that they name: `parents`: in every tree the entries 0 to 4 are 0; each of the last 8 entries names a branch, 1 to 4. `routes`: each token names 8 different experts. Within one tree (the 256 tokens of one micro-batch on one device) no expert is named by more than 72 tokens, a bound that some block reaches.
All inputs are finite; a program needn't handle non-finite values.
Results may differ from the reference program's by a relative error of at most 0.015.
The reference program's roundings to bfloat16 on the way count: a program that leaves them out, or rounds other values in their place, can miss the bound.
Values may be sent and summed in bfloat16 or wider, within the bound.
No kernel may reach another device: no remote copies, remote signals or barrier semaphores. Data moves between devices by JAX's collectives and lax.ppermute only.
A program may use at most 256 MiB of HBM per device.

```python
import math
import jax
import jax.numpy as jnp
import numpy as np
from jax import lax

D = 1024
QUERY_HEADS = 16
KEY_VALUE_HEADS = 8
HEAD_SIZE = 64
FFE = 512
EXPERTS = 32
TOP = 8
SEG_LEN = 16
BRANCHES = 4
LEAVES = 8
MB = 2
TRUNK = 64
NSEG = 13
TREE_TOKENS = 256
QD = 1024
KD = 512
CAP = 72
TREES = 32


def draw_parents(key, part):
    leaf_parent = jax.random.randint(key, (MB, TREES, LEAVES), 1, BRANCHES + 1).astype(jnp.int32)
    upper_rows = jnp.zeros((MB, TREES, 1 + BRANCHES), jnp.int32)
    return jnp.concatenate([upper_rows, leaf_parent], axis=2)


def strengthened(values, stream_key, source, target, parts, factor):
    def block_of(axis_at):
        return (jnp.arange(values.shape[axis_at]) // (values.shape[axis_at] // parts)).reshape((-1,) + (1,) * (values.ndim - 1 - axis_at))

    near = jax.random.permutation(stream_key, parts)[block_of(target)]
    other_side = (block_of(target) + parts // 2) % parts
    return jnp.where((block_of(source) == near) | (block_of(source) == other_side), factor * values, values)


def shard_levels(own_key, extent, cuts, low, high):
    def one(axis_at, blocks):
        steps = jax.random.uniform(jax.random.fold_in(jax.random.fold_in(own_key, 6), axis_at), (blocks,), jnp.float32, low / len(cuts), high / len(cuts))
        return jnp.repeat(jnp.exp(steps), extent[axis_at] // blocks).reshape((-1,) + (1,) * (len(extent) - axis_at - 1))

    level = one(*cuts[0])
    for cut in cuts[1:]:
        level = level * one(*cut)
    return level


def routed_block(rng, own, number, rows, number_of, top, bound, skew):
    sequence = jax.random.permutation(rng, number_of)
    packed, common = load_shares(number_of, rows * top, bound, skew, True), load_shares(number_of, rows * top, bound, skew, False)
    places = jnp.arange(number_of)

    def named(sizes, rotation):
        used = int((sizes > 0).sum())
        fixed = max(1, used // 4)
        passed = fixed + (places - fixed + rotation * (used - fixed)) % max(1, number_of - fixed)
        return jnp.zeros((number_of,), jnp.int32).at[sequence[jnp.where(places < fixed, places, passed)]].set(jnp.asarray(sizes, jnp.int32))

    sizes = jnp.where(number % 4 == 0, named(packed, number // 4), named(common, number - number // 4 - 1))
    mixed = jax.random.permutation(jax.random.fold_in(own, 3), number_of)
    giver, sink = mixed[0:number_of // 2 * 2:2], mixed[1:number_of // 2 * 2:2]
    margin = jnp.minimum(sizes[giver] - 1, bound - sizes[sink]) // 2
    margin = jnp.where((giver == sequence[0]) | (sink == sequence[0]) | (sizes[sink] == 0), 0, jnp.maximum(margin, 0))
    passed = jax.random.randint(jax.random.fold_in(own, 4), (number_of // 2,), 0, 1 << 20) % (margin + 1)
    sizes = sizes.at[giver].add(-passed).at[sink].add(passed)
    members = jnp.searchsorted(jnp.cumsum(sizes), jnp.arange(rows * top), side="right").astype(jnp.int32)
    listing = members.reshape(top, rows).T
    listing = listing[jax.random.permutation(jax.random.fold_in(own, 1), rows)]
    rotation = jax.random.randint(jax.random.fold_in(own, 2), (rows, 1), 0, top)
    return jnp.take_along_axis(listing, (jnp.arange(top)[None, :] + rotation) % top, axis=1)


def load_shares(number_of, total, most, slope, full):
    weights = [(1 << 20) // math.isqrt(rank ** slope) + 1 for rank in range(1, number_of + 1)]
    largest = most if full else min(most, max(-(-total // number_of), total * weights[0] // sum(weights)))
    least = 1 if total - largest >= number_of - 1 else 0
    given, spare = [largest] + [least] * (number_of - 1), total - largest - least * (number_of - 1)
    while spare > 0:
        candidates = [i for i in range(1, number_of) if given[i] < largest] or [i for i in range(1, number_of) if given[i] < most]
        whole, remaining = sum([weights[i] for i in candidates]), spare
        for i in candidates:
            extra = min(most - given[i], max(1, remaining * weights[i] // whole), spare)
            given[i] = given[i] + extra
            spare = spare - extra
    return np.array(given)


def gaussian(stream_key, shape, spread, limit, pieces=(), kind=jnp.bfloat16):
    factor_of = shard_levels(stream_key, shape, pieces, -0.22, 0.18) if pieces else 1.0
    values = jax.random.normal(stream_key, shape, jnp.float32) * spread * factor_of
    return jnp.minimum(jnp.maximum(values, -limit), limit).astype(kind)


def bell_draw_with(own_key, extent, spread, bound, cuts, heavy, kind=jnp.bfloat16):
    entries = spread * jax.random.normal(own_key, extent, jnp.float32)
    if cuts:
        entries = entries * shard_levels(own_key, extent, cuts, -0.22, 0.18)
    return jnp.clip(strengthened(entries, jax.random.fold_in(own_key, 3), *heavy), -bound, bound).astype(kind)


def setup_inputs(seed: int = 0) -> dict:
    streams_of = jax.random.split(jax.random.key(seed), 14)
    tokens = gaussian(streams_of[0], (MB, TREES, TREE_TOKENS, D), 1.0, 6.0, ((1, 32),))
    parents = draw_parents(jax.random.fold_in(streams_of[13], 71), 0)
    routes_keys = jax.random.split(jax.random.fold_in(streams_of[2], 1), MB * TREES * TREE_TOKENS // TREE_TOKENS)
    routes_turns = jax.random.permutation(jax.random.fold_in(streams_of[2], 3), MB * TREES * TREE_TOKENS // TREE_TOKENS)
    routes = jax.vmap(lambda own, number: routed_block(jax.random.fold_in(streams_of[2], 2), own, number, TREE_TOKENS, EXPERTS, TOP, CAP, 2))(routes_keys, routes_turns).reshape((MB, TREES, TREE_TOKENS, TOP))
    gain_attn = jnp.clip(1.0 + 0.1 * jax.random.normal(streams_of[3], (D,), jnp.float32), 0.5, 1.5)
    w_query = gaussian(streams_of[4], (D, QD), (D // 128) ** -0.5, 2.0, ((0, 4),))
    key_matrix = gaussian(streams_of[5], (D, KD), D ** -0.5, 0.1875, ((0, 4),))
    value_matrix = gaussian(streams_of[6], (D, KD), D ** -0.5, 0.1875, ((0, 4),))
    w_out = gaussian(streams_of[7], (QD, D), (D // 256) ** -0.5, 3.0, ((1, 4),))
    gain_moe = jnp.clip(1.0 + 0.1 * jax.random.normal(streams_of[8], (D,), jnp.float32), 0.5, 1.5)
    router = gaussian(streams_of[9], (D, EXPERTS), (4 * D) ** -0.5, 0.09375, ((0, 4),))
    expert_gate_up = gaussian(streams_of[10], (EXPERTS, D, 2 * FFE), D ** -0.5, 0.1875, ((0, 8), (1, 4)))
    expert_down = gaussian(streams_of[11], (EXPERTS, FFE, D), (max(FFE // 256, 1)) ** -0.5, 4.0, ((0, 8), (2, 4)))
    cotangent = bell_draw_with(streams_of[12], (MB, TREES, TREE_TOKENS, D), 1.0, 6.0, ((1, 32),), (1, 3, 32, 2.75))
    return dict(tokens=tokens, parents=parents, routes=routes, gain_attn=gain_attn, w_query=w_query, key_matrix=key_matrix, value_matrix=value_matrix, w_out=w_out, gain_moe=gain_moe, router=router, expert_gate_up=expert_gate_up, expert_down=expert_down, cotangent=cotangent)


@jax.custom_vjp
def reduced_precision(v):
    return lax.optimization_barrier(v.astype(jnp.bfloat16)).astype(jnp.float32)

@jax.custom_vjp
def reduced_backward(v):
    return v

def low_keep(v):
    return (reduced_precision(v), None)

def low_pass(kept, grad):
    return (grad,)

def back_keep(v):
    return (v, None)

def back_low(kept, grad):
    return (reduced_precision(grad),)
reduced_precision.defvjp(low_keep, low_pass)
reduced_backward.defvjp(back_keep, back_low)
epsilon = 1e-06
attn_mult = 0.015625
resid_mult = 0.22
theta_base = 10000.0
neg_fill = -1e+30
highest_precision = lax.Precision.HIGHEST

def tree_layout():
    row_index = jnp.arange(TREE_TOKENS, dtype=jnp.int32)
    branch_rest = row_index - TRUNK
    leaf_rest = branch_rest - BRANCHES * SEG_LEN
    in_trunk = row_index < TRUNK
    in_branch = branch_rest < BRANCHES * SEG_LEN
    segment = jnp.where(in_trunk, 0, jnp.where(in_branch, 1 + branch_rest // SEG_LEN, 1 + BRANCHES + leaf_rest // SEG_LEN))
    position = jnp.where(in_trunk, row_index, jnp.where(in_branch, TRUNK + branch_rest % SEG_LEN, TRUNK + SEG_LEN + leaf_rest % SEG_LEN))
    return (segment.astype(jnp.int32), position.astype(jnp.int32))

def rope_tables(position):
    half_width = HEAD_SIZE // 2
    inverse_freq = theta_base ** (-2.0 * jnp.arange(half_width, dtype=jnp.float32) / HEAD_SIZE)
    angles = position.astype(jnp.float32)[:, None] * inverse_freq[None, :]
    cosine_table = jnp.concatenate([jnp.cos(angles), jnp.cos(angles)], axis=1)
    sine_table = jnp.concatenate([jnp.sin(angles), jnp.sin(angles)], axis=1)
    return (cosine_table, sine_table)

def apply_rotary(vector, cosine_table, sine_table):
    half_width = vector.shape[-1] // 2
    turned = jnp.concatenate([-vector[..., half_width:], vector[..., :half_width]], axis=-1)
    return vector * cosine_table[:, None, :] + turned * sine_table[:, None, :]

def path_mask(parent_row, segment):
    seg_ids = jnp.arange(NSEG, dtype=jnp.int32)
    parent_hot = (parent_row[:, None] == seg_ids[None, :]).astype(jnp.float32)
    ancestor = jnp.eye(NSEG, dtype=jnp.float32) + parent_hot + jnp.dot(parent_hot, parent_hot, precision=highest_precision)
    seg_hot = (segment[:, None] == seg_ids[None, :]).astype(jnp.float32)
    reach = jnp.dot(jnp.dot(seg_hot, ancestor, precision=highest_precision), seg_hot.T, precision=highest_precision)
    row_index = jnp.arange(TREE_TOKENS, dtype=jnp.int32)
    return (reach > 0.5) & (row_index[None, :] <= row_index[:, None])

def slot_index(route_rows):
    flat_routes = route_rows.reshape(-1).astype(jnp.int32)
    expert_hot = (flat_routes[:, None] == jnp.arange(EXPERTS, dtype=jnp.int32)[None, :]).astype(jnp.int32)
    slot_rank = lax.optimization_barrier(jnp.sum(jnp.cumsum(expert_hot, axis=0) * expert_hot, axis=1)) - 1
    slot_ids = (flat_routes * CAP + slot_rank).astype(jnp.int32)
    token_ids = (jnp.arange(TREE_TOKENS * TOP, dtype=jnp.int32) // TOP).astype(jnp.int32)
    slot_owner = jnp.full((EXPERTS * CAP,), TREE_TOKENS, jnp.int32).at[slot_ids].set(token_ids)
    return (slot_ids, slot_owner)

def tree_forward(params, tokens_in, parent_row, route_rows):
    gain_attn, w_query, key_matrix, value_matrix, w_out, gain_moe, router, gate_up, down_proj = params
    segment, position = tree_layout()
    allowed = path_mask(parent_row, segment)
    cosine_table, sine_table = rope_tables(position)
    scale_one = lax.rsqrt(lax.optimization_barrier(jnp.mean(tokens_in * tokens_in, axis=1, keepdims=True)) + epsilon)
    first_normed = reduced_precision(tokens_in * scale_one * gain_attn)
    query_rows = reduced_backward(jnp.dot(first_normed, w_query, precision=highest_precision)).reshape(TREE_TOKENS, QUERY_HEADS, HEAD_SIZE)
    key_unrotated = reduced_backward(jnp.dot(first_normed, key_matrix, precision=highest_precision)).reshape(TREE_TOKENS, KEY_VALUE_HEADS, HEAD_SIZE)
    value_reduced = reduced_precision(reduced_backward(jnp.dot(first_normed, value_matrix, precision=highest_precision))).reshape(TREE_TOKENS, KEY_VALUE_HEADS, HEAD_SIZE)
    query_rotated = reduced_precision(apply_rotary(query_rows, cosine_table, sine_table)).reshape(TREE_TOKENS, KEY_VALUE_HEADS, QUERY_HEADS // KEY_VALUE_HEADS, HEAD_SIZE)
    key_rot = reduced_precision(apply_rotary(key_unrotated, cosine_table, sine_table))
    scores = reduced_backward(attn_mult * jnp.einsum('tkgd,skd->kgts', query_rotated, key_rot, precision=highest_precision))
    scores = jnp.where(allowed[None, None], scores, neg_fill)
    probs = reduced_precision(jax.nn.softmax(scores, axis=-1))
    mixed = jnp.einsum('kgts,skd->tkgd', probs, value_reduced, precision=highest_precision).reshape(TREE_TOKENS, QD)
    mixed = reduced_precision(reduced_backward(mixed))
    branch = reduced_backward(jnp.dot(mixed, w_out, precision=highest_precision))
    hidden_state = tokens_in + resid_mult * branch
    scale_two = lax.rsqrt(lax.optimization_barrier(jnp.mean(hidden_state * hidden_state, axis=1, keepdims=True)) + epsilon)
    normed_two = reduced_precision(hidden_state * scale_two * gain_moe)
    logits = reduced_backward(jnp.dot(normed_two, router, precision=highest_precision))
    route_hot = (route_rows[:, :, None] == jnp.arange(EXPERTS, dtype=jnp.int32)[None, None, :]).astype(jnp.float32)
    chosen = lax.optimization_barrier(jnp.sum(route_hot * logits[:, None, :], axis=2))
    gates = jax.nn.softmax(chosen, axis=1)
    slot_ids, slot_owner = slot_index(route_rows)
    padded = jnp.concatenate([normed_two, jnp.zeros((1, D), jnp.float32)], axis=0)
    sent = reduced_backward(padded[slot_owner]).reshape(EXPERTS, CAP, D)
    both = reduced_backward(jnp.einsum('ecd,edf->ecf', sent, gate_up, precision=highest_precision))
    expert_hidden = reduced_precision(jax.nn.silu(both[..., :FFE]) * both[..., FFE:])
    expert_out = reduced_precision(reduced_backward(jnp.einsum('ecf,efd->ecd', expert_hidden, down_proj, precision=highest_precision)))
    picked = expert_out.reshape(EXPERTS * CAP, D)[slot_ids].reshape(TREE_TOKENS, TOP, D)
    moe = jnp.einsum('tk,tkd->td', gates, picked, precision=highest_precision)
    return hidden_state + resid_mult * moe

def reference(tokens, parents, routes, gain_attn, w_query, key_matrix, value_matrix, w_out, gain_moe, router, expert_gate_up, expert_down, cotangent):
    params = tuple((item.astype(jnp.float32) for item in (gain_attn, w_query, key_matrix, value_matrix, w_out, gain_moe, router, expert_gate_up, expert_down)))
    count = MB * TREES
    inputs = tokens.astype(jnp.float32).reshape(count, TREE_TOKENS, D)
    parent_rows = parents.reshape(count, NSEG)
    route_all = routes.reshape(count, TREE_TOKENS, TOP)
    checked = jax.checkpoint(tree_forward)

    def forward(weights, rows):

        def one_tree(running, block_item):
            tree_rows, parent_row, route_rows = block_item
            return (running, checked(weights, tree_rows, parent_row, route_rows))
        unused, results = lax.scan(one_tree, jnp.zeros((), jnp.float32), (rows, parent_rows, route_all))
        return results
    results, pullback = jax.vjp(forward, params, inputs)
    grad_params, grad_inputs = pullback(cotangent.astype(jnp.float32).reshape(count, TREE_TOKENS, D))
    output = results.reshape(MB, TREES, TREE_TOKENS, D).astype(jnp.bfloat16)
    grad_tokens = grad_inputs.reshape(MB, TREES, TREE_TOKENS, D).astype(jnp.float32)
    g_attn, g_query, g_key, g_value, g_out, g_moe, g_router, g_gate_up, g_down = grad_params
    return (output, grad_tokens, g_attn, g_query, g_key, g_value, g_out, g_moe, g_router, g_gate_up, g_down)
```

```python
import functools

import jax
import jax.numpy as jnp
from jax import lax
from jax.experimental import pallas as pl
from jax.experimental.pallas import tpu as pltpu
from jax.sharding import PartitionSpec as P

D = 1024
QUERY_HEADS = 16
KEY_VALUE_HEADS = 8
HEAD_SIZE = 64
FFE = 512
EXPERTS = 32
TOP = 8
SEG_LEN = 16
BRANCHES = 4
MB = 2
TRUNK = 64
NSEG = 13
TREE_TOKENS = 256
QD = 1024
KD = 512
CAP = 72
CAP_PAD = 80
QKV = QD + 2 * KD
W1 = QKV + 128
GW = QKV + D + 128
EXT = 16
PAY = TREE_TOKENS + EXT

epsilon = 1e-06
attn_mult = 0.015625
resid_mult = 0.22
theta_base = 10000.0
neg_fill = -1e30

f32 = jnp.float32
bf16 = jnp.bfloat16
VMEM_LIMIT = 60 * 1024 * 1024


def dot(a, b, ca=1, cb=0):
    return lax.dot_general(a, b, (((ca,), (cb,)), ((), ())), preferred_element_type=f32)


def lanes(shape):
    return lax.broadcasted_iota(jnp.int32, shape, len(shape) - 1)


def params(**extra):
    return pltpu.CompilerParams(vmem_limit_bytes=VMEM_LIMIT, **extra)


def whole(shape):
    return pl.BlockSpec(shape, lambda *_: (0,) * len(shape))


def cost(flops, size, exps=0):
    return pl.CostEstimate(flops=int(flops), bytes_accessed=int(size), transcendentals=int(exps))


def tree_layout():
    row_index = jnp.arange(TREE_TOKENS, dtype=jnp.int32)
    branch_rest = row_index - TRUNK
    leaf_rest = branch_rest - BRANCHES * SEG_LEN
    in_trunk = row_index < TRUNK
    in_branch = branch_rest < BRANCHES * SEG_LEN
    segment = jnp.where(
        in_trunk,
        0,
        jnp.where(in_branch, 1 + branch_rest // SEG_LEN, 1 + BRANCHES + leaf_rest // SEG_LEN),
    )
    position = jnp.where(
        in_trunk,
        row_index,
        jnp.where(in_branch, TRUNK + branch_rest % SEG_LEN, TRUNK + SEG_LEN + leaf_rest % SEG_LEN),
    )
    return (segment, position)


def rope_tables(position):
    half_width = HEAD_SIZE // 2
    inverse_freq = theta_base ** (-2.0 * jnp.arange(half_width, dtype=f32) / HEAD_SIZE)
    angles = position.astype(f32)[:, None] * inverse_freq[None, :]
    c, s = jnp.cos(angles), jnp.sin(angles)
    return jnp.concatenate([c, c, c, c], axis=1), jnp.concatenate([-s, s, -s, s], axis=1)


def mask_bias(parent_row, segment):
    seg_ids = jnp.arange(NSEG, dtype=jnp.int32)
    parent_hot = (parent_row[:, None] == seg_ids[None, :]).astype(f32)
    ancestor = jnp.eye(NSEG, dtype=f32) + parent_hot + jnp.dot(parent_hot, parent_hot)
    seg_hot = (segment[:, None] == seg_ids[None, :]).astype(f32)
    reach = jnp.dot(jnp.dot(seg_hot, ancestor), seg_hot.T)
    rows = jnp.arange(TREE_TOKENS, dtype=jnp.int32)
    allowed = (reach > 0.5) & (rows[None, :] <= rows[:, None])
    return jnp.where(allowed, 0.0, neg_fill).astype(f32)


def swap_halves(u):
    first = (lanes(u.shape) % HEAD_SIZE) < HEAD_SIZE // 2
    return jnp.where(first, pltpu.roll(u, 96, 1), pltpu.roll(u, 32, 1))


def twice(u, upper):
    low = lanes(u.shape) < HEAD_SIZE
    turned = pltpu.roll(u, HEAD_SIZE, 1)
    return jnp.where(low, turned, u) if upper else jnp.where(low, u, turned)


def split_heads(u):
    low = lanes(u.shape) < HEAD_SIZE
    zero = jnp.zeros_like(u)
    return jnp.concatenate([jnp.where(low, u, zero), jnp.where(low, zero, u)], axis=0)


def softmax_rows(scores, bias):
    s = scores.reshape(2, TREE_TOKENS, TREE_TOKENS) * attn_mult + bias[None]
    e = jnp.exp(s - jnp.max(s, axis=-1, keepdims=True))
    p = e * (1.0 / jnp.sum(e, axis=-1, keepdims=True))
    return p.reshape(2 * TREE_TOKENS, TREE_TOKENS)


def forward_kernel(n_dp, pos, *refs):
    tokens, bias, cos2, sin2, gain_a, gain_m, routes = refs[:7]
    w1 = refs[7 : 7 + n_dp]
    wo = refs[7 + n_dp : 7 + 2 * n_dp]
    xnp, hidden_out, q_out, k2_out, v2_out, mixed_out, gates_out = refs[7 + 2 * n_dp : 14 + 2 * n_dp]
    xn1, branch = refs[14 + 2 * n_dp :]
    shard = D // n_dp

    def cols(p):
        return pl.ds(pl.multiple_of(pos[p] * shard, shard), shard)

    x = tokens[...].astype(f32)
    r1 = lax.rsqrt(jnp.mean(x * x, axis=1, keepdims=True) + epsilon)
    xn1[...] = (x * r1 * gain_a[...]).astype(bf16)
    qkv = dot(xn1[:, cols(0)], w1[0][:, :QKV])
    for p in range(1, n_dp):
        qkv = qkv + dot(xn1[:, cols(p)], w1[p][:, :QKV])
    c, s = cos2[...], sin2[...]
    for m in range(KEY_VALUE_HEADS):
        u = qkv[:, 128 * m : 128 * m + 128]
        q_out[:, 128 * m : 128 * m + 128] = (u * c + swap_halves(u) * s).astype(bf16)
    for n in range(KEY_VALUE_HEADS // 2):
        u = qkv[:, QD + 128 * n : QD + 128 * n + 128]
        u = u * c + swap_halves(u) * s
        w = qkv[:, QD + KD + 128 * n : QD + KD + 128 * n + 128]
        for half in range(2):
            at = 128 * (2 * n + half)
            k2_out[:, at : at + 128] = twice(u, half).astype(bf16)
            v2_out[:, at : at + 128] = twice(w, half).astype(bf16)

    def one(m, carry):
        at = pl.ds(pl.multiple_of(m * 128, 128), 128)
        qq = split_heads(q_out[:, at])
        p = softmax_rows(dot(qq, k2_out[:, at], 1, 1), bias[...]).astype(bf16)
        o = dot(p, v2_out[:, at])
        low = lanes((TREE_TOKENS, 128)) < HEAD_SIZE
        mixed_out[:, at] = jnp.where(low, o[:TREE_TOKENS], o[TREE_TOKENS:]).astype(bf16)
        return carry

    lax.fori_loop(0, KEY_VALUE_HEADS, one, 0, unroll=2)
    for p in range(n_dp):
        branch[:, cols(p)] = dot(mixed_out[...], wo[p][...])
    h = x + resid_mult * branch[...]
    hidden_out[...] = h
    r2 = lax.rsqrt(jnp.mean(h * h, axis=1, keepdims=True) + epsilon)
    xnp[:TREE_TOKENS] = (h * r2 * gain_m[...]).astype(bf16)
    logits = dot(xnp[:TREE_TOKENS, cols(0)], w1[0][:, QKV:])
    for p in range(1, n_dp):
        logits = logits + dot(xnp[:TREE_TOKENS, cols(p)], w1[p][:, QKV:])
    lt = logits.T[:EXPERTS]
    ids = lax.broadcasted_iota(jnp.int32, (EXPERTS, TREE_TOKENS), 0)
    named = ids == routes[0:1, :]
    for k in range(1, TOP):
        named = named | (ids == routes[k : k + 1, :])
    lt = jnp.where(named, lt, neg_fill)
    e = jnp.where(named, jnp.exp(lt - jnp.max(lt, axis=0, keepdims=True)), 0.0)
    g = e / jnp.sum(e, axis=0, keepdims=True)
    gates_out[...] = g
    packed = pack_rows(g)
    hi = packed.astype(bf16)
    low_part = (packed - hi.astype(f32)).astype(bf16)
    xnp[TREE_TOKENS:] = jnp.concatenate([hi.astype(f32), low_part.astype(f32)], axis=0).astype(bf16)


def pack_rows(g):
    return jnp.concatenate([g[8 * i : 8 * i + 8] for i in range(4)], axis=1)


def unpack_rows(g):
    return jnp.concatenate([g[:, 256 * i : 256 * i + 256] for i in range(4)], axis=0)


def forward_part(pos, tokens, bias, tables, gain_a, gain_m, routes, w1, wo):
    n_dp = len(w1)
    t = TREE_TOKENS
    ins = [tokens, bias, *tables, gain_a, gain_m, routes, *w1, *wo]
    outs = [((PAY, D), bf16), ((t, D), f32)] + [((t, QD), bf16)] * 4 + [((EXPERTS, t), f32)]
    return pl.pallas_call(
        functools.partial(forward_kernel, n_dp),
        grid_spec=pltpu.PrefetchScalarGridSpec(
            num_scalar_prefetch=1,
            grid=(1,),
            in_specs=[whole(a.shape) for a in ins],
            out_specs=[whole(s) for s, _ in outs],
            scratch_shapes=[pltpu.VMEM((t, D), bf16), pltpu.VMEM((t, D), f32)],
        ),
        out_shape=[jax.ShapeDtypeStruct(s, d) for s, d in outs],
        compiler_params=params(),
        cost_estimate=cost(2 * t * D * 3200 + 4 * 16 * t * t * 128, 12e6, 16 * t * t),
        name="attention_forward",
    )(pos, *ins)


def expert_kernel(n_dp, n_blocks, local, pos, *refs):
    xs = refs[:n_blocks]
    cots = refs[n_blocks : 2 * n_blocks]
    at = 2 * n_blocks
    gu = refs[at : at + n_dp]
    dn = refs[at + n_dp : at + 2 * n_dp]
    at += 2 * n_dp
    g_outs = refs[at : at + n_blocks]
    m_outs = refs[at + n_blocks : at + 2 * n_blocks]
    at += 2 * n_blocks
    sent_out, hid_out, gboth_out, geo_out = refs[at : at + 4]
    rank_s, gate_s, gg_s, sel_s, comb_s, eo_s, gs_s = refs[at + 4 :]
    e = pl.program_id(0)
    shard = D // n_dp
    first = pos[n_dp] * local
    t = TREE_TOKENS
    ids = lax.broadcasted_iota(jnp.int32, (EXPERTS, t), 0)

    def cols(p):
        return pl.ds(pl.multiple_of(pos[p] * shard, shard), shard)

    @pl.when(e == 0)
    def _():
        rows = []
        for b in range(n_blocks):
            ext = xs[b][t:].astype(f32)
            gates = unpack_rows(ext[:8] + ext[8:16])
            rows.append(
                [
                    jnp.sum(jnp.where(ids == first + el, gates, 0.0), axis=0, keepdims=True)
                    for el in range(local)
                ]
            )
        before = lax.broadcasted_iota(jnp.int32, (t, t), 0) < lax.broadcasted_iota(jnp.int32, (t, t), 1)
        before = before.astype(f32).astype(bf16)
        pad = [jnp.zeros((8 - n_blocks, t), f32)] if n_blocks < 8 else []
        for el in range(local):
            gate = jnp.concatenate([rows[b][el] for b in range(n_blocks)] + pad, axis=0)
            used = gate > 0.0
            rank = dot(used.astype(f32).astype(bf16), before)
            gate_s[el] = gate
            rank_s[el] = jnp.where(used, rank, -1.0)
        sel_s[...] = jnp.zeros_like(sel_s)
        comb_s[...] = jnp.zeros_like(comb_s)

    gate, rank = gate_s[e], rank_s[e]
    slot = lax.broadcasted_iota(jnp.int32, (CAP, t), 0).astype(f32)
    sels, sent, cot, gate_slot = [], [], [], []
    for b in range(n_blocks):
        hit = slot == rank[b : b + 1]
        sel = jnp.where(hit, 1.0, 0.0)
        sels.append(sel)
        low = sel.astype(bf16)
        sent.append(dot(low, xs[b][:t]))
        cot.append(dot(low, cots[b][...]))
        gate_slot.append(jnp.sum(jnp.where(hit, gate[b : b + 1], 0.0), axis=1, keepdims=True))
    sent_out[0] = jnp.concatenate(sent, axis=0).astype(bf16)
    gm = jnp.concatenate(cot, axis=0) * resid_mult
    gate_slot = jnp.concatenate(gate_slot, axis=0)
    geo_out[0] = (gm * gate_slot).astype(bf16)
    both = dot(sent_out[0, :, cols(0)], gu[0][0])
    for p in range(1, n_dp):
        both = both + dot(sent_out[0, :, cols(p)], gu[p][0])
    gh, up = both[:, :FFE], both[:, FFE:]
    sigma = 1.0 / (1.0 + jnp.exp(-gh))
    hid_out[0] = (gh * sigma * up).astype(bf16)
    for p in range(n_dp):
        eo_s[:, cols(p)] = dot(hid_out[0], dn[p][0]).astype(bf16)
    grad_hidden = dot(geo_out[0, :, cols(0)], dn[0][0], 1, 1)
    for p in range(1, n_dp):
        grad_hidden = grad_hidden + dot(geo_out[0, :, cols(p)], dn[p][0], 1, 1)
    gs = grad_hidden * sigma
    gboth_out[0] = jnp.concatenate(
        [(gs * up * (1.0 + gh * (1.0 - sigma))).astype(bf16), (gs * gh).astype(bf16)], axis=1
    )
    for p in range(n_dp):
        gs_s[:, cols(p)] = dot(gboth_out[0], gu[p][0], 1, 1)
    eo = eo_s[...].astype(f32)
    gg = jnp.sum(gm * eo, axis=1, keepdims=True)
    weighted = gate_slot * eo
    ggs = []
    for b in range(n_blocks):
        part = slice(CAP * b, CAP * b + CAP)
        where = pl.ds(pl.multiple_of(e * CAP_PAD, 16), CAP)
        sel_s[b, where] = sels[b].astype(bf16)
        comb_s[b, where, :D] = gs_s[part].astype(bf16)
        comb_s[b, where, D:] = weighted[part].astype(bf16)
        ggs.append(jnp.sum(sels[b] * gg[part], axis=0, keepdims=True))
    gg_s[e] = jnp.concatenate(ggs + [jnp.zeros((8 - n_blocks, t), f32)] if n_blocks < 8 else ggs, axis=0)

    @pl.when(e == local - 1)
    def _():
        for b in range(n_blocks):
            both_parts = dot(sel_s[b], comb_s[b], 0, 0)
            g_outs[b][:t] = both_parts[:, :D].astype(g_outs[b].dtype)
            m_outs[b][...] = both_parts[:, D:].astype(m_outs[b].dtype)
            full = jnp.zeros((EXPERTS, t), f32)
            for el in range(local):
                full = full + jnp.where(ids == first + el, gg_s[el, b : b + 1], 0.0)
            packed = pack_rows(full)
            hi = packed.astype(bf16)
            rest = (packed - hi.astype(f32)).astype(bf16)
            ext = jnp.concatenate([hi.astype(f32), rest.astype(f32)], axis=0)
            g_outs[b][t:] = ext.astype(g_outs[b].dtype)


def expert_part(pos, xs, cots, gu, dn, kind):
    n_dp, n_blocks, local = len(gu), len(xs), gu[0].shape[0]
    t, shard = TREE_TOKENS, D // n_dp
    m = CAP * n_blocks
    ins = [*xs, *cots, *gu, *dn]
    in_specs = (
        [whole(a.shape) for a in (*xs, *cots)]
        + [pl.BlockSpec((1, shard, 2 * FFE), lambda e, *_: (e, 0, 0))] * n_dp
        + [pl.BlockSpec((1, FFE, shard), lambda e, *_: (e, 0, 0))] * n_dp
    )
    outs = [((PAY, D), kind)] * n_blocks + [((t, D), kind)] * n_blocks
    out_specs = [whole(s) for s, _ in outs]
    kept = [D, FFE, 2 * FFE, D]
    outs = outs + [((local, m, w), bf16) for w in kept]
    out_specs = out_specs + [pl.BlockSpec((1, m, w), lambda e, *_: (e, 0, 0)) for w in kept]
    flops = local * 2 * m * (3 * D * 2 * FFE + 2 * t * D) + n_blocks * 2 * t * local * CAP * 2 * D
    res = pl.pallas_call(
        functools.partial(expert_kernel, n_dp, n_blocks, local),
        grid_spec=pltpu.PrefetchScalarGridSpec(
            num_scalar_prefetch=1,
            grid=(local,),
            in_specs=in_specs,
            out_specs=out_specs,
            scratch_shapes=[
                pltpu.VMEM((local, 8, t), f32),
                pltpu.VMEM((local, 8, t), f32),
                pltpu.VMEM((local, 8, t), f32),
                pltpu.VMEM((n_blocks, local * CAP_PAD, t), bf16),
                pltpu.VMEM((n_blocks, local * CAP_PAD, 2 * D), bf16),
                pltpu.VMEM((m, D), bf16),
                pltpu.VMEM((m, D), f32),
            ],
        ),
        out_shape=[jax.ShapeDtypeStruct(s, d) for s, d in outs],
        compiler_params=params(),
        cost_estimate=cost(flops * 1.5, 40e6),
        name="experts",
    )(pos, *ins)
    return res[:n_blocks], res[n_blocks : 2 * n_blocks], res[2 * n_blocks :]


def expert_grad_kernel(n_dp, n_kept, pos, *refs):
    kept = [refs[4 * i : 4 * i + 4] for i in range(n_kept)]
    outs = refs[4 * n_kept :]
    shard = D // n_dp
    for p in range(n_dp):
        at = pl.ds(pl.multiple_of(pos[p] * shard, shard), shard)
        total = None
        for sent, _, gboth, _ in kept:
            part = dot(sent[0, :, at], gboth[0], 0, 0)
            total = part if total is None else total + part
        outs[p][0] = total.astype(outs[p].dtype)
        total = None
        for _, hid, _, geo in kept:
            part = dot(hid[0], geo[0, :, at], 0, 0)
            total = part if total is None else total + part
        outs[n_dp + p][0] = total.astype(outs[n_dp + p].dtype)


def expert_grads(pos, kept, n_dp):
    local, m, _ = kept[0][0].shape
    shard = D // n_dp
    flat = [a for one in kept for a in one]
    outs = [(local, shard, 2 * FFE)] * n_dp + [(local, FFE, shard)] * n_dp
    res = pl.pallas_call(
        functools.partial(expert_grad_kernel, n_dp, len(kept)),
        grid_spec=pltpu.PrefetchScalarGridSpec(
            num_scalar_prefetch=1,
            grid=(local,),
            in_specs=[pl.BlockSpec((1, *a.shape[1:]), lambda e, *_: (e, 0, 0)) for a in flat],
            out_specs=[pl.BlockSpec((1, *s[1:]), lambda e, *_: (e, 0, 0)) for s in outs],
        ),
        out_shape=[jax.ShapeDtypeStruct(s, bf16) for s in outs],
        compiler_params=params(),
        cost_estimate=cost(2 * local * m * len(kept) * 3 * D * FFE, 45e6),
        name="expert_grads",
    )(pos, *flat)
    return res[:n_dp], res[n_dp:]


def backward_kernel(n_dp, n_grads, pos, *refs):
    grads = refs[:n_grads]
    tokens, hidden, cot, gates, q, k2, v2, bias, cos2, sin2, gain_a, gain_m = refs[n_grads : n_grads + 12]
    at0 = n_grads + 12
    w1 = refs[at0 : at0 + n_dp]
    wo = refs[at0 + n_dp : at0 + 2 * n_dp]
    at0 += 2 * n_dp
    grad_tokens, xn1_out, gqkv_out, gbr_out, xn2_out, gl_out, gains_out = refs[at0 : at0 + 7]
    term, gmix = refs[at0 + 7 :]
    shard = D // n_dp
    t = TREE_TOKENS

    def cols(p):
        return pl.ds(pl.multiple_of(pos[p] * shard, shard), shard)

    total = grads[0][...].astype(f32)
    for other in grads[1:]:
        total = total + other[...].astype(f32)
    gg = unpack_rows(total[t : t + 8] + total[t + 8 : t + 16])
    g = gates[...]
    gl = g * (gg - jnp.sum(g * gg, axis=0, keepdims=True))
    gl = jnp.concatenate([gl, jnp.zeros((128 - EXPERTS, t), f32)], axis=0).T.astype(bf16)
    gl_out[...] = gl
    for p in range(n_dp):
        term[:, cols(p)] = dot(gl, w1[p][:, QKV:], 1, 1)
    gx2 = total[:t] + term[...]
    h = hidden[...]
    r2 = lax.rsqrt(jnp.mean(h * h, axis=1, keepdims=True) + epsilon)
    xn2_out[...] = (h * r2 * gain_m[...]).astype(bf16)
    u2 = gx2 * gain_m[...]
    ghs = cot[...].astype(f32) + r2 * u2 - h * (r2 * r2 * r2) * jnp.mean(u2 * h, axis=1, keepdims=True)
    gain2 = jnp.sum(gx2 * h * r2, axis=0, keepdims=True)
    gbr_out[...] = (resid_mult * ghs).astype(bf16)
    acc = dot(gbr_out[:, cols(0)], wo[0][...], 1, 1)
    for p in range(1, n_dp):
        acc = acc + dot(gbr_out[:, cols(p)], wo[p][...], 1, 1)
    gmix[...] = acc.astype(bf16)
    low = lanes((t, 128)) < HEAD_SIZE
    c, s = cos2[...], sin2[...]

    def unrotate(w):
        return w * c + swap_halves(w * s)

    def one(n, carry):
        keys, values = [], []
        for half in range(2):
            at = pl.ds(pl.multiple_of(n * 256 + 128 * half, 128), 128)
            qq = split_heads(q[:, at])
            dd = split_heads(gmix[:, at])
            kk = k2[:, at]
            pf = softmax_rows(dot(qq, kk, 1, 1), bias[...])
            gp = dot(dd, v2[:, at], 1, 1)
            gsc = (pf * (gp - jnp.sum(pf * gp, axis=1, keepdims=True))).astype(bf16)
            gq = dot(gsc, kk)
            gq = attn_mult * jnp.where(low, gq[:t], gq[t:])
            gqkv_out[:, at] = unrotate(gq).astype(bf16)
            gk = attn_mult * dot(gsc, qq, 0, 0)
            keys.append(gk + pltpu.roll(gk, HEAD_SIZE, 1))
            gv = dot(pf.astype(bf16), dd, 0, 0)
            values.append(gv + pltpu.roll(gv, HEAD_SIZE, 1))
        at = pl.ds(pl.multiple_of(QD + n * 128, 128), 128)
        gqkv_out[:, at] = unrotate(jnp.where(low, keys[0], keys[1])).astype(bf16)
        at = pl.ds(pl.multiple_of(QD + KD + n * 128, 128), 128)
        gqkv_out[:, at] = jnp.where(low, values[0], values[1]).astype(bf16)
        return carry

    lax.fori_loop(0, KEY_VALUE_HEADS // 2, one, 0)
    for p in range(n_dp):
        term[:, cols(p)] = dot(gqkv_out[...], w1[p][:, :QKV], 1, 1)
    gx1 = term[...]
    x = tokens[...].astype(f32)
    r1 = lax.rsqrt(jnp.mean(x * x, axis=1, keepdims=True) + epsilon)
    xn1_out[...] = (x * r1 * gain_a[...]).astype(bf16)
    u1 = gx1 * gain_a[...]
    grad_tokens[...] = ghs + r1 * u1 - x * (r1 * r1 * r1) * jnp.mean(u1 * x, axis=1, keepdims=True)
    gain1 = jnp.sum(gx1 * x * r1, axis=0, keepdims=True)
    gains_out[...] = jnp.concatenate([gain1, gain2, jnp.zeros((6, D), f32)], axis=0)


def backward_part(pos, grads, tokens, hidden, cot, gates, q, k2, v2, bias, tables, gain_a, gain_m, w1, wo):
    n_dp, t = len(w1), TREE_TOKENS
    ins = [*grads, tokens, hidden, cot, gates, q, k2, v2, bias, *tables, gain_a, gain_m, *w1, *wo]
    outs = [
        ((t, D), f32),
        ((t, D), bf16),
        ((t, QKV), bf16),
        ((t, D), bf16),
        ((t, D), bf16),
        ((t, 128), bf16),
        ((8, D), f32),
    ]
    return pl.pallas_call(
        functools.partial(backward_kernel, n_dp, len(grads)),
        grid_spec=pltpu.PrefetchScalarGridSpec(
            num_scalar_prefetch=1,
            grid=(1,),
            in_specs=[whole(a.shape) for a in ins],
            out_specs=[whole(s) for s, _ in outs],
            scratch_shapes=[pltpu.VMEM((t, D), f32), pltpu.VMEM((t, D), bf16)],
        ),
        out_shape=[jax.ShapeDtypeStruct(s, d) for s, d in outs],
        compiler_params=params(),
        cost_estimate=cost(2 * t * D * 3200 + 10 * 16 * t * t * 128, 15e6, 16 * t * t),
        name="attention_backward",
    )(pos, *ins)


def in_kernel(rows):
    return rows % 16 == 0


def weight_kernel(n_dp, n_exp, pos, *refs):
    per = 6
    sets = [refs[per * i : per * i + per] for i in range(MB)]
    outs = refs[per * MB :]
    shard, small = D // n_dp, D // n_dp // n_exp
    for p in range(n_dp):
        at = pl.ds(pl.multiple_of(pos[p] * shard, shard), shard)

        def product(left, right):
            total = None
            for one in sets:
                part = dot(one[left][:, at], one[right][...], 0, 0)
                total = part if total is None else total + part
            return total

        blocks = [product(0, 1), product(2, 3), product(4, 5)]
        pieces = n_exp if in_kernel(small) else 1
        size = shard // pieces
        for i in range(pieces):
            rows = slice(size * i, size * i + size)
            to = pl.ds(pl.multiple_of(pos[n_dp + 1 + i] * size, size), size) if pieces > 1 else slice(None)
            offset = 0
            for value in blocks:
                width = value.shape[1]
                outs[p][to, offset : offset + width] = value[rows].astype(outs[p].dtype)
                offset += width


def weight_part(pos, sets, n_dp, n_exp):
    flat = [a for one in sets for a in one]
    shard = D // n_dp
    return pl.pallas_call(
        functools.partial(weight_kernel, n_dp, n_exp),
        grid_spec=pltpu.PrefetchScalarGridSpec(
            num_scalar_prefetch=1,
            grid=(1,),
            in_specs=[whole(a.shape) for a in flat],
            out_specs=[whole((shard, GW))] * n_dp,
        ),
        out_shape=[jax.ShapeDtypeStruct((shard, GW), bf16)] * n_dp,
        compiler_params=params(),
        cost_estimate=cost(4 * TREE_TOKENS * D * GW, 15e6),
        name="dense_grads",
    )(pos, *flat)


class Grid:
    def __init__(self, n_dp, n_exp):
        self.n_dp, self.n_exp = n_dp, n_exp
        self.cores = 2 if n_dp % 2 == 0 else 1
        self.chips = n_dp // self.cores
        self.major = 4 if n_exp % 4 == 0 else 1
        self.minor = n_exp // self.major

    def shift(self, x, axis, by_major, by_minor):
        major, minor = (self.chips, self.cores) if axis == "dp" else (self.major, self.minor)
        pairs = []
        for i in range(major * minor):
            a, b = divmod(i, minor)
            pairs.append((i, (a + by_major) % major * minor + (b + by_minor) % minor))
        return lax.ppermute(x, axis, pairs)

    def dp_pieces(self, x):
        held = [x] + [self.shift(x, "dp", s, 0) for s in range(1, self.chips)]
        return [
            piece if c == 0 else self.shift(piece, "dp", 0, c) for piece in held for c in range(self.cores)
        ]

    def dp_places(self):
        i = lax.axis_index("dp")
        a, b = i // self.cores, i % self.cores
        return [
            (a - s) % self.chips * self.cores + (b - c) % self.cores
            for s in range(self.chips)
            for c in range(self.cores)
        ]

    def dp_sum(self, pieces):
        held = []
        for s in range(self.chips):
            total = pieces[s * self.cores].astype(f32)
            for c in range(1, self.cores):
                total = total + self.shift(pieces[s * self.cores + c], "dp", 0, -c).astype(f32)
            held.append(total)
        total = held[0]
        for s in range(1, self.chips):
            total = total + self.shift(held[s].astype(bf16), "dp", -s, 0).astype(f32)
        return total

    def spread(self, x):
        first = [x] + [self.shift(x, "expert", s, 0) for s in range(1, self.major)]
        return [first] + [[self.shift(b, "expert", 0, r) for b in first] for r in range(1, self.minor)]

    def home(self, parts):
        waiting = []
        for s in range(self.major):
            total = parts[0][s].astype(f32)
            for r in range(1, self.minor):
                total = total + self.shift(parts[r][s], "expert", 0, -r).astype(f32)
            waiting.append(total)
        return [waiting[0]] + [
            self.shift(waiting[s].astype(bf16), "expert", -s, 0) for s in range(1, self.major)
        ]

    def exp_places(self):
        i = lax.axis_index("expert")
        a, b = i // self.minor, i % self.minor
        return [
            (a - k // self.minor) % self.major * self.minor + (b - k % self.minor) % self.minor
            for k in range(self.n_exp)
        ]


def on_device(
    grid,
    tokens,
    parents,
    routes,
    gain_attn,
    w_query,
    key_matrix,
    value_matrix,
    w_out,
    gain_moe,
    router,
    expert_gate_up,
    expert_down,
    cotangent,
):
    n_dp, n_exp = grid.n_dp, grid.n_exp
    shard = D // n_dp
    small = shard // n_exp
    places = grid.dp_places()
    me = lax.axis_index("expert")
    a, b = me // grid.minor, me % grid.minor
    steps = [
        (a - i // grid.minor) % grid.major * grid.minor + (b - i % grid.minor) % grid.minor
        for i in range(n_exp)
    ]
    pos = jnp.stack([*places, me, *steps]).astype(jnp.int32)

    cots = [grid.spread(cotangent[i, 0]) for i in range(MB)]
    w1 = grid.dp_pieces(
        jnp.concatenate(
            [w_query, key_matrix, value_matrix, router, jnp.zeros((shard, 128 - EXPERTS), bf16)], axis=1
        )
    )
    wo = grid.dp_pieces(w_out)
    gu = grid.dp_pieces(expert_gate_up)
    dn = grid.dp_pieces(expert_down)

    segment, position = tree_layout()
    tables = rope_tables(position)
    gain_a, gain_m = gain_attn.reshape(1, D), gain_moe.reshape(1, D)

    saved, kept, returned, outputs = [], [], [], []
    for i in range(MB):
        bias = mask_bias(parents[i, 0], segment)
        xnp, hidden, q, k2, v2, mixed, gates = forward_part(
            pos, tokens[i, 0], bias, tables, gain_a, gain_m, routes[i, 0].T, w1, wo
        )
        saved.append((bias, hidden, q, k2, v2, mixed, gates))
        xs = grid.spread(xnp)
        g_parts, m_parts = [], []
        for r in range(grid.minor):
            g_out, m_out, keep = expert_part(pos, xs[r], cots[i][r], gu, dn, f32 if r == 0 else bf16)
            g_parts.append(g_out)
            m_parts.append(m_out)
            kept.append(keep)
        returned.append(grid.home(g_parts))
        moe = grid.home(m_parts)
        total = moe[0]
        for part in moe[1:]:
            total = total + part.astype(f32)
        outputs.append((hidden + resid_mult * total).astype(bf16))

    sets, gains, grad_rows = [], None, []
    for i in range(MB):
        bias, hidden, q, k2, v2, mixed, gates = saved[i]
        grad_tokens, xn1, gqkv, gbr, xn2, gl, gain = backward_part(
            pos, returned[i], tokens[i, 0], hidden, cotangent[i, 0], gates, q, k2, v2, bias, tables,
            gain_a, gain_m, w1, wo,
        )
        grad_rows.append(grad_tokens)
        sets.append((xn1, gqkv, gbr, mixed, xn2, gl))
        gains = gain if gains is None else gains + gain

    gu_pieces, dn_pieces = expert_grads(pos, kept, n_dp)
    grad_gate_up = grid.dp_sum(gu_pieces)
    grad_down = grid.dp_sum(dn_pieces)

    dense = grid.dp_sum(weight_part(pos, sets, n_dp, n_exp))
    dense = dense.reshape(n_exp, small, GW)
    if not in_kernel(small):
        dense = dense[jnp.stack(grid.exp_places())]
    parts = [
        [dense[s * grid.minor + r].astype(f32 if r == 0 else bf16) for s in range(grid.major)]
        for r in range(grid.minor)
    ]
    landed = grid.home(parts)
    mine = landed[0]
    for part in landed[1:]:
        mine = mine + part.astype(f32)
    gains = lax.psum_scatter(gains, ("dp", "expert"), scatter_dimension=1, tiled=True)

    return (
        jnp.stack(outputs)[:, None],
        jnp.stack(grad_rows)[:, None],
        gains[0],
        mine[:, :QD],
        mine[:, QD : QD + KD],
        mine[:, QD + KD : QKV],
        mine[:, QKV : QKV + D].T,
        gains[1],
        mine[:, QKV + D : QKV + D + EXPERTS],
        grad_gate_up,
        grad_down,
    )


def solution(mesh):
    grid = Grid(mesh.shape["dp"], mesh.shape["expert"])
    in_specs = (
        P(None, ("dp", "expert"), None, None),
        P(None, ("dp", "expert"), None),
        P(None, ("dp", "expert"), None, None),
        P(),
        P("dp", None),
        P("dp", None),
        P("dp", None),
        P(None, "dp"),
        P(),
        P("dp", None),
        P("expert", "dp", None),
        P("expert", None, "dp"),
        P(None, ("dp", "expert"), None, None),
    )
    out_specs = (
        P(None, ("dp", "expert"), None, None),
        P(None, ("dp", "expert"), None, None),
        P(("dp", "expert")),
        P(("dp", "expert"), None),
        P(("dp", "expert"), None),
        P(("dp", "expert"), None),
        P(None, ("dp", "expert")),
        P(("dp", "expert")),
        P(("dp", "expert"), None),
        P("expert", "dp", None),
        P("expert", None, "dp"),
    )
    return jax.shard_map(
        functools.partial(on_device, grid), mesh=mesh, in_specs=in_specs, out_specs=out_specs, check_vma=False
    )
```

```python
import functools

import jax
import jax.numpy as jnp
from jax import lax
from jax.experimental import pallas as pl
from jax.experimental.pallas import tpu as pltpu
from jax.sharding import PartitionSpec as P

D = 1024
QUERY_HEADS = 16
KEY_VALUE_HEADS = 8
HEAD_SIZE = 64
FFE = 512
EXPERTS = 32
TOP = 8
SEG_LEN = 16
BRANCHES = 4
MB = 2
TRUNK = 64
NSEG = 13
TREE_TOKENS = 256
QD = 1024
KD = 512
CAP = 72
CAP_PAD = 80
QKV = QD + 2 * KD
WIDE = QKV + 128 + D
WO = QKV + 128
PAIR = 3 * FFE
EXT = 16
PAY = TREE_TOKENS + EXT

epsilon = 1e-06
attn_mult = 0.015625
resid_mult = 0.22
theta_base = 10000.0
neg_fill = -1e30

f32 = jnp.float32
bf16 = jnp.bfloat16
VMEM_LIMIT = 60 * 1024 * 1024


def dot(a, b, ca=1, cb=0):
    return lax.dot_general(a, b, (((ca,), (cb,)), ((), ())), preferred_element_type=f32)


def lanes(shape):
    return lax.broadcasted_iota(jnp.int32, shape, len(shape) - 1)


def params(**extra):
    return pltpu.CompilerParams(vmem_limit_bytes=VMEM_LIMIT, **extra)


def whole(shape):
    return pl.BlockSpec(shape, lambda *_: (0,) * len(shape))


def cost(flops, size, exps=0):
    return pl.CostEstimate(flops=int(flops), bytes_accessed=int(size), transcendentals=int(exps))


def tree_layout():
    row_index = jnp.arange(TREE_TOKENS, dtype=jnp.int32)
    branch_rest = row_index - TRUNK
    leaf_rest = branch_rest - BRANCHES * SEG_LEN
    in_trunk = row_index < TRUNK
    in_branch = branch_rest < BRANCHES * SEG_LEN
    segment = jnp.where(
        in_trunk,
        0,
        jnp.where(in_branch, 1 + branch_rest // SEG_LEN, 1 + BRANCHES + leaf_rest // SEG_LEN),
    )
    position = jnp.where(
        in_trunk,
        row_index,
        jnp.where(in_branch, TRUNK + branch_rest % SEG_LEN, TRUNK + SEG_LEN + leaf_rest % SEG_LEN),
    )
    return (segment, position)


def rope_tables(position):
    half_width = HEAD_SIZE // 2
    inverse_freq = theta_base ** (-2.0 * jnp.arange(half_width, dtype=f32) / HEAD_SIZE)
    angles = position.astype(f32)[:, None] * inverse_freq[None, :]
    c, s = jnp.cos(angles), jnp.sin(angles)
    return jnp.concatenate([c, c, c, c], axis=1), jnp.concatenate([-s, s, -s, s], axis=1)


def mask_bias(parent_row, segment):
    seg_ids = jnp.arange(NSEG, dtype=jnp.int32)
    parent_hot = (parent_row[:, None] == seg_ids[None, :]).astype(f32)
    ancestor = jnp.eye(NSEG, dtype=f32) + parent_hot + jnp.dot(parent_hot, parent_hot)
    seg_hot = (segment[:, None] == seg_ids[None, :]).astype(f32)
    reach = jnp.dot(jnp.dot(seg_hot, ancestor), seg_hot.T)
    rows = jnp.arange(TREE_TOKENS, dtype=jnp.int32)
    allowed = (reach > 0.5) & (rows[None, :] <= rows[:, None])
    return jnp.where(allowed, 0.0, neg_fill).astype(f32)


def swap_halves(u):
    first = (lanes(u.shape) % HEAD_SIZE) < HEAD_SIZE // 2
    return jnp.where(first, pltpu.roll(u, 96, 1), pltpu.roll(u, 32, 1))


def twice(u, upper):
    low = lanes(u.shape) < HEAD_SIZE
    turned = pltpu.roll(u, HEAD_SIZE, 1)
    return jnp.where(low, turned, u) if upper else jnp.where(low, u, turned)


def split_heads(u):
    low = lanes(u.shape) < HEAD_SIZE
    zero = jnp.zeros_like(u)
    return jnp.concatenate([jnp.where(low, u, zero), jnp.where(low, zero, u)], axis=0)


def softmax_rows(scores, bias):
    s = scores.reshape(2, TREE_TOKENS, TREE_TOKENS) * attn_mult + bias[None]
    e = jnp.exp(s - jnp.max(s, axis=-1, keepdims=True))
    p = e * (1.0 / jnp.sum(e, axis=-1, keepdims=True))
    return p.reshape(2 * TREE_TOKENS, TREE_TOKENS)


def gather_weights(refs, offsets, to, sem, wait):
    for i, ref in enumerate(refs):
        rows = ref.shape[0]
        copy = pltpu.make_async_copy(
            ref, to.at[pl.ds(pl.multiple_of(offsets[i], rows), rows)], sem.at[i]
        )
        if wait:
            copy.wait()
        else:
            copy.start()


def forward_kernel(n_dense, offsets, *refs):
    tokens, bias, cos2, sin2, gain_a, gain_m, routes = refs[:7]
    dense = refs[7 : 7 + n_dense]
    xnp, hidden_out, q_out, k2_out, v2_out, mixed_out, gates_out = refs[7 + n_dense : 14 + n_dense]
    w, sem = refs[14 + n_dense :]
    gather_weights(dense, offsets, w, sem, False)
    x = tokens[...].astype(f32)
    r1 = lax.rsqrt(jnp.mean(x * x, axis=1, keepdims=True) + epsilon)
    xn1 = (x * r1 * gain_a[...]).astype(bf16)
    gather_weights(dense, offsets, w, sem, True)
    qkv = dot(xn1, w[:, :QKV])
    c, s = cos2[...], sin2[...]
    for m in range(KEY_VALUE_HEADS):
        u = qkv[:, 128 * m : 128 * m + 128]
        q_out[:, 128 * m : 128 * m + 128] = (u * c + swap_halves(u) * s).astype(bf16)
    for n in range(KEY_VALUE_HEADS // 2):
        u = qkv[:, QD + 128 * n : QD + 128 * n + 128]
        u = u * c + swap_halves(u) * s
        o = qkv[:, QD + KD + 128 * n : QD + KD + 128 * n + 128]
        for half in range(2):
            at = 128 * (2 * n + half)
            k2_out[:, at : at + 128] = twice(u, half).astype(bf16)
            v2_out[:, at : at + 128] = twice(o, half).astype(bf16)

    def one(m, carry):
        at = pl.ds(pl.multiple_of(m * 128, 128), 128)
        qq = split_heads(q_out[:, at])
        p = softmax_rows(dot(qq, k2_out[:, at], 1, 1), bias[...]).astype(bf16)
        o = dot(p, v2_out[:, at])
        low = lanes((TREE_TOKENS, 128)) < HEAD_SIZE
        mixed_out[:, at] = jnp.where(low, o[:TREE_TOKENS], o[TREE_TOKENS:]).astype(bf16)
        return carry

    lax.fori_loop(0, KEY_VALUE_HEADS, one, 0, unroll=2)
    h = x + resid_mult * dot(mixed_out[...], w[:, WO:], 1, 1)
    hidden_out[...] = h
    r2 = lax.rsqrt(jnp.mean(h * h, axis=1, keepdims=True) + epsilon)
    xn2 = (h * r2 * gain_m[...]).astype(bf16)
    xnp[:TREE_TOKENS] = xn2
    lt = dot(xn2, w[:, QKV:WO]).T[:EXPERTS]
    ids = lax.broadcasted_iota(jnp.int32, (EXPERTS, TREE_TOKENS), 0)
    named = ids == routes[0:1, :]
    for k in range(1, TOP):
        named = named | (ids == routes[k : k + 1, :])
    lt = jnp.where(named, lt, neg_fill)
    e = jnp.where(named, jnp.exp(lt - jnp.max(lt, axis=0, keepdims=True)), 0.0)
    g = e / jnp.sum(e, axis=0, keepdims=True)
    gates_out[...] = g
    packed = pack_rows(g)
    hi = packed.astype(bf16)
    low_part = (packed - hi.astype(f32)).astype(bf16)
    xnp[TREE_TOKENS:] = jnp.concatenate([hi.astype(f32), low_part.astype(f32)], axis=0).astype(bf16)


def pack_rows(g):
    return jnp.concatenate([g[8 * i : 8 * i + 8] for i in range(4)], axis=1)


def unpack_rows(g):
    return jnp.concatenate([g[:, 256 * i : 256 * i + 256] for i in range(4)], axis=0)


def any_space(n):
    return [pl.BlockSpec(memory_space=pl.ANY)] * n


def forward_part(offsets, tokens, bias, tables, gain_a, gain_m, routes, dense):
    t = TREE_TOKENS
    ins = [tokens, bias, *tables, gain_a, gain_m, routes]
    outs = [((PAY, D), bf16), ((t, D), f32)] + [((t, QD), bf16)] * 4 + [((EXPERTS, t), f32)]
    return pl.pallas_call(
        functools.partial(forward_kernel, len(dense)),
        grid_spec=pltpu.PrefetchScalarGridSpec(
            num_scalar_prefetch=1,
            grid=(1,),
            in_specs=[whole(a.shape) for a in ins] + any_space(len(dense)),
            out_specs=[whole(s) for s, _ in outs],
            scratch_shapes=[pltpu.VMEM((D, WIDE), bf16), pltpu.SemaphoreType.DMA((len(dense),))],
        ),
        out_shape=[jax.ShapeDtypeStruct(s, d) for s, d in outs],
        compiler_params=params(),
        cost_estimate=cost(1, 1),
        name="attention_forward",
    )(offsets, *ins, *dense)


def expert_kernel(layout, local, n_before, last, pos, *refs):
    refs = list(refs)

    def take(n):
        out = refs[:n]
        del refs[:n]
        return out

    n_dp = len(layout)
    rows_in, cots_in = take(5), take(5)
    weights = [take(len(sizes)) for sizes in layout]
    before_in = [take(3) for _ in range(n_before)]
    outs = take(8) if last else take(3)
    sent_out, hid_out, gboth_out, geo_out = take(4)
    rank_s, gate_s, x1_s, x3_s, c1_s, c3_s, w_s, w_sem = take(8)
    sel_s, comb_s, gg_s = take(3) if last else outs
    e = pl.program_id(0)
    shard = D // n_dp
    base = pos[n_dp] * local
    at_start, at_end = pos[n_dp + 1] == 0, pos[n_dp + 1] == 3
    t = TREE_TOKENS
    ids = lax.broadcasted_iota(jnp.int32, (EXPERTS, t), 0)
    xs = [rows_in[0], x1_s, rows_in[2], x3_s]
    cots = [cots_in[0], c1_s, cots_in[2], c3_s]

    def load(expert, slot):
        for p, (parts, sizes) in enumerate(zip(weights, layout)):
            to = w_s.at[slot, pl.ds(pl.multiple_of(pos[p] * shard, shard), shard)]
            offset = 0
            for part, size in zip(parts, sizes):
                if len(sizes) == 1:
                    pltpu.make_async_copy(part.at[expert], to, w_sem.at[slot, p]).start()
                else:

                    @pl.when((expert >= offset) & (expert < offset + size))
                    def _():
                        pltpu.make_async_copy(part.at[expert - offset], to, w_sem.at[slot, p]).start()

                offset += size

    def arrive(slot):
        for p in range(n_dp):
            to = w_s.at[slot, pl.ds(pl.multiple_of(pos[p] * shard, shard), shard)]
            pltpu.make_async_copy(weights[p][0].at[0], to, w_sem.at[slot, p]).wait()

    slot_now = e % 2

    @pl.when(e == 0)
    def _():
        load(0, 0)

    @pl.when(e + 1 < local)
    def _():
        load(e + 1, 1 - slot_now)

    @pl.when(e == 0)
    def _():
        for given, lower, upper in ((rows_in, x1_s, x3_s), (cots_in, c1_s, c3_s)):
            lower[...] = jnp.where(at_start, given[4][...], given[1][...])
            upper[...] = jnp.where(at_end, given[4][...], given[3][...])
        gates = []
        for b in range(4):
            ext = xs[b][t:].astype(f32)
            full = unpack_rows(ext[:8] + ext[8:16])
            gates.append(
                [
                    jnp.sum(jnp.where(ids == base + el, full, 0.0), axis=0, keepdims=True)
                    for el in range(local)
                ]
            )
        before = lax.broadcasted_iota(jnp.int32, (t, t), 0) < lax.broadcasted_iota(jnp.int32, (t, t), 1)
        before = before.astype(f32).astype(bf16)
        for el in range(local):
            gate = jnp.concatenate([gates[b][el] for b in range(4)] + [jnp.zeros((4, t), f32)], axis=0)
            used = gate > 0.0
            rank = dot(used.astype(f32).astype(bf16), before)
            gate_s[el] = gate
            rank_s[el] = jnp.where(used, rank, -1.0)
        sel_s[...] = jnp.zeros_like(sel_s)
        comb_s[...] = jnp.zeros_like(comb_s)

    gate, rank = gate_s[e], rank_s[e]
    slot = lax.broadcasted_iota(jnp.int32, (CAP, t), 0).astype(f32)
    sels, sent, cot, gate_slot = [], [], [], []
    for b in range(4):
        hit = slot == rank[b : b + 1]
        sel = jnp.where(hit, 1.0, 0.0)
        sels.append(sel)
        low = sel.astype(bf16)
        sent.append(dot(low, xs[b][:t]))
        cot.append(dot(low, cots[b][...]))
        gate_slot.append(jnp.sum(jnp.where(hit, gate[b : b + 1], 0.0), axis=1, keepdims=True))
    sent_out[0] = jnp.concatenate(sent, axis=0).astype(bf16)
    gm = jnp.concatenate(cot, axis=0) * resid_mult
    gate_slot = jnp.concatenate(gate_slot, axis=0)
    geo_out[0] = (gm * gate_slot).astype(bf16)
    arrive(slot_now)
    both = dot(sent_out[0], w_s[slot_now, :, : 2 * FFE])
    gh, up = both[:, :FFE], both[:, FFE:]
    sigma = 1.0 / (1.0 + jnp.exp(-gh))
    hid_out[0] = (gh * sigma * up).astype(bf16)
    eo = dot(hid_out[0], w_s[slot_now, :, 2 * FFE :], 1, 1).astype(bf16).astype(f32)
    gs = dot(geo_out[0], w_s[slot_now, :, 2 * FFE :]) * sigma
    gboth_out[0] = jnp.concatenate(
        [(gs * up * (1.0 + gh * (1.0 - sigma))).astype(bf16), (gs * gh).astype(bf16)], axis=1
    )
    grad_sent = dot(gboth_out[0], w_s[slot_now, :, : 2 * FFE], 1, 1)
    gg = jnp.sum(gm * eo, axis=1, keepdims=True)
    weighted = gate_slot * eo
    ggs = []
    for b in range(4):
        part = slice(CAP * b, CAP * b + CAP)
        where = pl.ds(pl.multiple_of(e * CAP_PAD, 16), CAP)
        sel_s[b, where] = sels[b].astype(bf16)
        comb_s[b, where, :D] = grad_sent[part].astype(bf16)
        comb_s[b, where, D:] = weighted[part].astype(bf16)
        ggs.append(jnp.sum(sels[b] * gg[part], axis=0, keepdims=True))
    gg_s[e] = jnp.concatenate(ggs + [jnp.zeros((4, t), f32)], axis=0)

    if not last:
        return

    @pl.when(e == local - 1)
    def _():
        for b in range(4):
            total = dot(sel_s[b], comb_s[b], 0, 0)
            full = jnp.zeros((EXPERTS, t), f32)
            for el in range(local):
                full = full + jnp.where(ids == base + el, gg_s[el, b : b + 1], 0.0)
            for i, (sel_b, comb_b, gg_b) in enumerate(before_in):
                total = total + dot(sel_b[b], comb_b[b], 0, 0)
                owner = pos[n_dp + 2 + i] * local
                for el in range(local):
                    full = full + jnp.where(ids == owner + el, gg_b[el, b : b + 1], 0.0)
            outs[b][:t] = total[:, :D].astype(outs[b].dtype)
            outs[4 + b][...] = total[:, D:].astype(outs[4 + b].dtype)
            packed = pack_rows(full)
            hi = packed.astype(bf16)
            rest = (packed - hi.astype(f32)).astype(bf16)
            ext = jnp.concatenate([hi.astype(f32), rest.astype(f32)], axis=0)
            outs[b][t:] = ext.astype(outs[b].dtype)


def expert_part(pos, rows, cots, weights, before, last):
    n_dp = len(weights)
    local = sum(part.shape[0] for part in weights[0])
    t = TREE_TOKENS
    m = CAP * 4
    layout = tuple(tuple(part.shape[0] for part in parts) for parts in weights)
    flat = [part for parts in weights for part in parts]
    earlier = [a for one in before for a in one]
    ins = [*rows, *cots, *flat, *earlier]
    in_specs = [whole(a.shape) for a in (*rows, *cots)]
    in_specs += [pl.BlockSpec(memory_space=pl.ANY)] * len(flat)
    in_specs += [whole(a.shape) for a in earlier]
    passed = [
        ((4, local * CAP_PAD, t), bf16),
        ((4, local * CAP_PAD, 2 * D), bf16),
        ((local, 8, t), f32),
    ]
    if last:
        kinds = [f32, bf16, bf16, bf16]
        outs = [((PAY, D), k) for k in kinds] + [((t, D), k) for k in kinds]
    else:
        outs = list(passed)
    n_main = len(outs)
    out_specs = [whole(s) for s, _ in outs]
    kept = [D, FFE, 2 * FFE, D]
    outs = outs + [((local, m, w), bf16) for w in kept]
    out_specs = out_specs + [pl.BlockSpec((1, m, w), lambda e, *_: (e, 0, 0)) for w in kept]
    scratch = [
        pltpu.VMEM((local, 8, t), f32),
        pltpu.VMEM((local, 8, t), f32),
        pltpu.VMEM((PAY, D), bf16),
        pltpu.VMEM((PAY, D), bf16),
        pltpu.VMEM((t, D), bf16),
        pltpu.VMEM((t, D), bf16),
        pltpu.VMEM((2, D, PAIR), bf16),
        pltpu.SemaphoreType.DMA((2, n_dp)),
    ]
    if last:
        scratch += [pltpu.VMEM(s, d) for s, d in passed]
    res = pl.pallas_call(
        functools.partial(expert_kernel, layout, local, len(before), last),
        grid_spec=pltpu.PrefetchScalarGridSpec(
            num_scalar_prefetch=1,
            grid=(local,),
            in_specs=in_specs,
            out_specs=out_specs,
            scratch_shapes=scratch,
        ),
        out_shape=[jax.ShapeDtypeStruct(s, d) for s, d in outs],
        compiler_params=params(),
        cost_estimate=cost(1, 1),
        name="experts",
    )(pos, *ins)
    return res[:n_main], res[n_main:]


def expert_grad_kernel(n_dp, n_kept, pos, *refs):
    kept = [refs[4 * i : 4 * i + 4] for i in range(n_kept)]
    outs = refs[4 * n_kept :]
    shard = D // n_dp
    for p in range(n_dp):
        at = pl.ds(pl.multiple_of(pos[p] * shard, shard), shard)
        gate_up, down = None, None
        for sent, hid, gboth, geo in kept:
            part = dot(sent[0, :, at], gboth[0], 0, 0)
            gate_up = part if gate_up is None else gate_up + part
            part = dot(geo[0, :, at], hid[0], 0, 0)
            down = part if down is None else down + part
        out = outs[p % len(outs)]
        out[p // len(outs), 0, :, : 2 * FFE] = gate_up.astype(out.dtype)
        out[p // len(outs), 0, :, 2 * FFE :] = down.astype(out.dtype)


def expert_grads(pos, kept, chips, cores):
    local, m, _ = kept[0][0].shape
    n_dp = chips * cores
    shard = D // n_dp
    flat = [a for one in kept for a in one]
    shape = (chips, local, shard, PAIR)
    return pl.pallas_call(
        functools.partial(expert_grad_kernel, n_dp, len(kept)),
        grid_spec=pltpu.PrefetchScalarGridSpec(
            num_scalar_prefetch=1,
            grid=(local,),
            in_specs=[pl.BlockSpec((1, *a.shape[1:]), lambda e, *_: (e, 0, 0)) for a in flat],
            out_specs=[pl.BlockSpec((chips, 1, shard, PAIR), lambda e, *_: (0, e, 0, 0))] * cores,
        ),
        out_shape=[jax.ShapeDtypeStruct(shape, bf16)] * cores,
        compiler_params=params(),
        cost_estimate=cost(1, 1),
        name="expert_grads",
    )(pos, *flat)


def backward_kernel(n_dense, n_grads, offsets, *refs):
    grads = refs[:n_grads]
    tokens, hidden, cot, gates, q, k2, v2, bias, cos2, sin2, gain_a, gain_m = refs[n_grads : n_grads + 12]
    dense = refs[n_grads + 12 : n_grads + 12 + n_dense]
    rest = refs[n_grads + 12 + n_dense :]
    grad_tokens, xn1_out, gqkv_out, gbr_out, xn2_out, gl_out, gains_out = rest[:7]
    gmix, w, sem = rest[7:]
    t = TREE_TOKENS
    gather_weights(dense, offsets, w, sem, False)
    total = grads[0][...].astype(f32)
    for other in grads[1:]:
        total = total + other[...].astype(f32)
    gg = unpack_rows(total[t : t + 8] + total[t + 8 : t + 16])
    g = gates[...]
    gl = g * (gg - jnp.sum(g * gg, axis=0, keepdims=True))
    gl = jnp.concatenate([gl, jnp.zeros((128 - EXPERTS, t), f32)], axis=0).T.astype(bf16)
    gl_out[...] = gl
    gather_weights(dense, offsets, w, sem, True)
    gx2 = total[:t] + dot(gl, w[:, QKV:WO], 1, 1)
    h = hidden[...]
    r2 = lax.rsqrt(jnp.mean(h * h, axis=1, keepdims=True) + epsilon)
    xn2_out[...] = (h * r2 * gain_m[...]).astype(bf16)
    u2 = gx2 * gain_m[...]
    ghs = cot[...].astype(f32) + r2 * u2 - h * (r2 * r2 * r2) * jnp.mean(u2 * h, axis=1, keepdims=True)
    gain2 = jnp.sum(gx2 * h * r2, axis=0, keepdims=True)
    gbr_out[...] = (resid_mult * ghs).astype(bf16)
    gmix[...] = dot(gbr_out[...], w[:, WO:]).astype(bf16)
    low = lanes((t, 128)) < HEAD_SIZE
    c, s = cos2[...], sin2[...]

    def unrotate(w):
        return w * c + swap_halves(w * s)

    def one(n, carry):
        keys, values = [], []
        for half in range(2):
            at = pl.ds(pl.multiple_of(n * 256 + 128 * half, 128), 128)
            qq = split_heads(q[:, at])
            dd = split_heads(gmix[:, at])
            kk = k2[:, at]
            pf = softmax_rows(dot(qq, kk, 1, 1), bias[...])
            gp = dot(dd, v2[:, at], 1, 1)
            gsc = (pf * (gp - jnp.sum(pf * gp, axis=1, keepdims=True))).astype(bf16)
            gq = dot(gsc, kk)
            gq = attn_mult * jnp.where(low, gq[:t], gq[t:])
            gqkv_out[:, at] = unrotate(gq).astype(bf16)
            gk = attn_mult * dot(gsc, qq, 0, 0)
            keys.append(gk + pltpu.roll(gk, HEAD_SIZE, 1))
            gv = dot(pf.astype(bf16), dd, 0, 0)
            values.append(gv + pltpu.roll(gv, HEAD_SIZE, 1))
        at = pl.ds(pl.multiple_of(QD + n * 128, 128), 128)
        gqkv_out[:, at] = unrotate(jnp.where(low, keys[0], keys[1])).astype(bf16)
        at = pl.ds(pl.multiple_of(QD + KD + n * 128, 128), 128)
        gqkv_out[:, at] = jnp.where(low, values[0], values[1]).astype(bf16)
        return carry

    lax.fori_loop(0, KEY_VALUE_HEADS // 2, one, 0)
    gx1 = dot(gqkv_out[...], w[:, :QKV], 1, 1)
    x = tokens[...].astype(f32)
    r1 = lax.rsqrt(jnp.mean(x * x, axis=1, keepdims=True) + epsilon)
    xn1_out[...] = (x * r1 * gain_a[...]).astype(bf16)
    u1 = gx1 * gain_a[...]
    grad_tokens[...] = ghs + r1 * u1 - x * (r1 * r1 * r1) * jnp.mean(u1 * x, axis=1, keepdims=True)
    gain1 = jnp.sum(gx1 * x * r1, axis=0, keepdims=True)
    gains_out[...] = jnp.concatenate([gain1, gain2, jnp.zeros((6, D), f32)], axis=0)


def backward_part(offsets, grads, tokens, hidden, cot, gates, q, k2, v2, bias, tables, gain_a, gain_m, dense):
    t = TREE_TOKENS
    ins = [*grads, tokens, hidden, cot, gates, q, k2, v2, bias, *tables, gain_a, gain_m]
    outs = [
        ((t, D), f32),
        ((t, D), bf16),
        ((t, QKV), bf16),
        ((t, D), bf16),
        ((t, D), bf16),
        ((t, 128), bf16),
        ((8, D), f32),
    ]
    return pl.pallas_call(
        functools.partial(backward_kernel, len(dense), len(grads)),
        grid_spec=pltpu.PrefetchScalarGridSpec(
            num_scalar_prefetch=1,
            grid=(1,),
            in_specs=[whole(a.shape) for a in ins] + any_space(len(dense)),
            out_specs=[whole(s) for s, _ in outs],
            scratch_shapes=[
                pltpu.VMEM((t, D), bf16),
                pltpu.VMEM((D, WIDE), bf16),
                pltpu.SemaphoreType.DMA((len(dense),)),
            ],
        ),
        out_shape=[jax.ShapeDtypeStruct(s, d) for s, d in outs],
        compiler_params=params(),
        cost_estimate=cost(1, 1),
        name="attention_backward",
    )(offsets, *ins, *dense)


def in_kernel(rows):
    return rows % 16 == 0


def weight_kernel(n_dp, n_exp, pos, *refs):
    per = 7
    sets = [refs[per * i : per * i + per] for i in range(MB)]
    outs = refs[per * MB :]
    cores = len(outs)
    shard, small = D // n_dp, D // n_dp // n_exp
    for p in range(n_dp):
        at = pl.ds(pl.multiple_of(pos[p] * shard, shard), shard)

        def product(left, right):
            total = None
            for one in sets:
                part = dot(one[left][:, at], one[right][...], 0, 0)
                total = part if total is None else total + part
            return total

        gains = sets[0][6][:, at]
        for one in sets[1:]:
            gains = gains + one[6][:, at]
        gains = jnp.concatenate(
            [jnp.zeros((EXPERTS, shard), f32), gains, jnp.zeros((120 - EXPERTS, shard), f32)], axis=0
        )
        blocks = [product(0, 1), product(4, 5) + gains.T, product(2, 3)]
        pieces = n_exp if in_kernel(small) else 1
        size = shard // pieces
        for i in range(pieces):
            rows = slice(size * i, size * i + size)
            to = pl.ds(pl.multiple_of(pos[n_dp + i] * size, size), size) if pieces > 1 else slice(None)
            offset = 0
            for value in blocks:
                width = value.shape[1]
                outs[p % cores][p // cores, to, offset : offset + width] = value[rows].astype(bf16)
                offset += width


def weight_part(pos, sets, chips, cores, n_exp):
    flat = [a for one in sets for a in one]
    n_dp = chips * cores
    shape = (chips, D // n_dp, WIDE)
    return pl.pallas_call(
        functools.partial(weight_kernel, n_dp, n_exp),
        grid_spec=pltpu.PrefetchScalarGridSpec(
            num_scalar_prefetch=1,
            grid=(1,),
            in_specs=[whole(a.shape) for a in flat],
            out_specs=[whole(shape)] * cores,
        ),
        out_shape=[jax.ShapeDtypeStruct(shape, bf16)] * cores,
        compiler_params=params(),
        cost_estimate=cost(1, 1),
        name="dense_grads",
    )(pos, *flat)


class Grid:
    def __init__(self, n_dp, n_exp):
        self.n_dp, self.n_exp = n_dp, n_exp
        self.cores = 2 if n_dp % 2 == 0 else 1
        self.chips = n_dp // self.cores
        self.major = 4
        self.minor = n_exp // self.major

    def move(self, x, axis, to):
        major, minor = (self.chips, self.cores) if axis == "dp" else (self.major, self.minor)
        pairs = []
        for i in range(major * minor):
            target = to(*divmod(i, minor))
            if target is not None:
                pairs.append((i, target[0] * minor + target[1]))
        return lax.ppermute(x, axis, pairs)

    def chip(self, x, s):
        return self.move(x, "dp", lambda a, b: ((a + s) % self.chips, b))

    def core(self, x, s):
        return self.move(x, "dp", lambda a, b: (a, (b + s) % self.cores))

    def line(self, x, s):
        return self.move(x, "expert", lambda a, b: (a, (b + s) % self.minor))

    def up(self, x, s):
        return self.move(x, "expert", lambda a, b: ((a + s) % 4, b))

    def next_up(self, x):
        return self.move(x, "expert", lambda a, b: (a + 1, b) if a < 3 else None)

    def next_down(self, x):
        return self.move(x, "expert", lambda a, b: (a - 1, b) if a > 0 else None)

    def outward(self, x):
        return self.move(x, "expert", lambda a, b: {1: (0, b), 2: (3, b)}.get(a))

    def back(self, parts):
        return [self.up(x, -k) for k, x in enumerate(parts, 1)]

    def dp_places(self):
        i = lax.axis_index("dp")
        a, b = i // self.cores, i % self.cores
        return [
            (a - s) % self.chips * self.cores + (b - c) % self.cores
            for s in range(self.chips)
            for c in range(self.cores)
        ]

    def exp_steps(self):
        i = lax.axis_index("expert")
        a, b = i // self.minor, i % self.minor
        return [
            (a - k // self.minor) % self.major * self.minor + (b - k % self.minor) % self.minor
            for k in range(self.n_exp)
        ]

    def cores_moved(self, groups):
        return [self.core(g, -c) for c, g in enumerate(groups) if c]

    def cores_added(self, groups, moved, s):
        total = groups[0][s].astype(f32)
        for part in moved:
            total = total + part[s].astype(f32)
        return total

    def major_home(self, blocks):
        total = blocks[0]
        for s in range(1, self.major):
            total = total + self.up(blocks[s].astype(bf16), -s).astype(f32)
        return total


def on_device(
    grid,
    tokens,
    parents,
    routes,
    gain_attn,
    w_query,
    key_matrix,
    value_matrix,
    w_out,
    gain_moe,
    router,
    expert_gate_up,
    expert_down,
    cotangent,
):
    n_dp, n_exp = grid.n_dp, grid.n_exp
    shard = D // n_dp
    places = grid.dp_places()
    me = lax.axis_index("expert")
    major, minor = me // grid.minor, me % grid.minor
    steps = grid.exp_steps()
    owners = [major * grid.minor + (minor - r) % grid.minor for r in range(grid.minor)]

    def pos(i, r):
        before = owners[:r] if i == 0 else (owners[1:r] if r else owners[1:])
        return jnp.stack([*places, owners[r], major, *before, jnp.int32(0)]).astype(jnp.int32)

    pos_dense = jnp.stack([*places, *steps]).astype(jnp.int32)
    chips, lines, cores = range(1, grid.chips), range(1, grid.minor), range(grid.cores)
    local = expert_gate_up.shape[0]
    cut = local - local // 2
    v = {}

    def gate(*names):
        flat, tree = jax.tree.flatten([v[name] for name in names])
        v.update(zip(names, jax.tree.unflatten(tree, lax.optimization_barrier(flat))))

    segment, position = tree_layout()
    tables = rope_tables(position)
    gain_a, gain_m = gain_attn.reshape(1, D), gain_moe.reshape(1, D)
    biases = [mask_bias(parents[i, 0], segment) for i in range(MB)]
    for i in range(MB):
        v["tok%d" % i], v["cot%d" % i] = tokens[i, 0], cotangent[i, 0]

    def pairs(a, b):
        if a == b:
            return []
        return [jnp.concatenate([expert_gate_up[a:b], expert_down[a:b].transpose(0, 2, 1)], axis=2)]

    def over_cores(arrays):
        return [[grid.core(x, c) for x in arrays] for c in cores[1:]]

    def joined(*parts):
        return [sum(held, []) for held in zip(*parts)]

    packed = jnp.concatenate(
        [w_query, key_matrix, value_matrix, router, jnp.zeros((shard, 128 - EXPERTS), bf16), w_out.T], axis=1
    )
    half = local // 2
    quarter = half // 2
    v["far"] = [grid.chip(packed, s) for s in chips]
    v["packed"] = packed
    v["wy"] = [[grid.line(w, r) for w in pairs(0, half)] for r in lines]
    v["c0a"], v["c0b"], v["c0c"] = grid.next_up(v["cot0"]), grid.up(v["cot0"], 2), grid.next_down(v["cot0"])
    v["pair"] = pairs(0, local)
    v["xa"], v["xb"], v["xc"] = pairs(0, quarter), pairs(half, local), pairs(quarter, half)
    gate("far", "packed", "wy", "c0a", "c0b", "c0c", "pair", "xa", "xb", "xc")

    v["far_core"] = [[grid.core(f, c) for c in cores[1:]] for f in v["far"]]
    v["packed_core"] = [grid.core(v["packed"], c) for c in cores[1:]]
    gate("far_core", "packed_core", "tok0", "pair", "xa", "xb", "xc", "cot1", "c0b", "wy")

    dense = [packed, *v["packed_core"]]
    for f, fs in zip(v["far"], v["far_core"]):
        dense += [f, *fs]
    offsets = (jnp.stack(places) * shard).astype(jnp.int32)

    def forward(i):
        return forward_part(
            offsets, v["tok%d" % i], biases[i], tables, gain_a, gain_m, routes[i, 0].T, dense
        )

    v["f0"] = forward(0)
    v["wxa"] = [[grid.chip(w, s) for w in v["xa"]] for s in chips]
    v["pair_core"] = over_cores(v["pair"])
    v["c0d"], v["c1b"] = grid.outward(v["c0b"]), grid.up(v["cot1"], 2)
    gate("f0", "wxa", "pair_core", "c0d", "c1b", "tok1", "xb", "xc", "wy")

    row = v["f0"][0]
    v["n0a"], v["n0b"], v["n0c"] = grid.next_up(row), grid.up(row, 2), grid.next_down(row)
    v["wxb"] = [[grid.chip(w, s) for w in v["xb"]] for s in chips]
    v["wyb"] = [[grid.line(w, r) for w in v["xb"]] for r in lines]
    v["f1"] = forward(1)
    gate("n0a", "n0b", "n0c", "wxb", "wyb", "f1", "cot1", "xc", "wy")

    v["wxc"] = [[grid.chip(w, s) for w in v["xc"]] for s in chips]
    v["wxa_core"] = [over_cores(ws) for ws in v["wxa"]]
    v["wxb_core"] = [over_cores(ws) for ws in v["wxb"]]
    v["n0d"] = grid.outward(v["n0b"])
    v["wy_core"] = [over_cores(ws) for ws in v["wy"]]
    gate("wxc", "wxa_core", "wxb_core", "wy_core", "n0d", "f1", "cot1", "wy", "wxb", "wyb")

    v["wxc_core"] = [over_cores(ws) for ws in v["wxc"]]
    v["wyb_core"] = [over_cores(ws) for ws in v["wyb"]]
    gate("wxc_core", "wyb_core", "f1", "cot1", "wy", "wxb")

    own = [tuple(v["pair"]), *[tuple(w) for w in v["pair_core"]]]
    for k in range(len(chips)):
        own.append((*v["wxa"][k], *v["wxc"][k], *v["wxb"][k]))
        own += [tuple(ws) for ws in joined(v["wxa_core"][k], v["wxc_core"][k], v["wxb_core"][k])]

    def experts(i, r, weights, before):
        name = "%d" % i
        rows = [v["f" + name][0], *[v["n" + name + k] for k in "abcd"]]
        cots = [v["cot" + name], *[v["c" + name + k] for k in "abcd"]]
        return expert_part(pos(i, r), rows, cots, weights, before, len(before) == grid.minor - 1)

    v["e00"], v["k00"] = experts(0, 0, own, [])
    row = v["f1"][0]
    v["n1a"], v["n1b"], v["n1c"] = grid.next_up(row), grid.up(row, 2), grid.next_down(row)
    v["low"] = [[[grid.chip(w, s) for w in ws] for s in chips] for ws in v["wy"]]
    v["high"] = [[[grid.line(w, r) for w in ws] for ws in v["wxb"]] for r in lines]
    gate("e00", "low", "high", "n1a", "n1b", "n1c", "f1", "cot1", "c1b", "wy", "wyb")

    v["low_core"] = [[over_cores(w) for w in ws] for ws in v["low"]]
    v["high_core"] = [[over_cores(w) for w in ws] for ws in v["high"]]
    gate("low_core", "high_core", "f1", "n1b", "e00", "cot1", "c1b")

    sets = [own]
    for i in range(len(lines)):
        parts = [(*v["wy"][i], *v["wyb"][i])]
        parts += [tuple(ws) for ws in joined(v["wy_core"][i], v["wyb_core"][i])]
        for k in range(len(chips)):
            parts.append((*v["low"][i][k], *v["high"][i][k]))
            parts += [tuple(ws) for ws in joined(v["low_core"][i][k], v["high_core"][i][k])]
        sets.append(parts)
    v["n1d"] = grid.outward(v["n1b"])
    v["c1d"] = grid.outward(v["c1b"])
    v["c1a"], v["c1c"] = grid.next_up(v["cot1"]), grid.next_down(v["cot1"])
    passed = [v["e00"]]
    for r in lines:
        out, v["k%d0" % r] = experts(0, r, sets[r], passed)
        passed.append(out)
    v["out0"] = passed[-1]
    gate("out0", "c1a", "c1c", "c1d", "n1d", "f1")

    v["g0"] = [v["out0"][0], *grid.back(v["out0"][1:4])]
    passed = []
    for r in lines:
        out, v["k%d1" % r] = experts(1, r, sets[r], passed)
        passed.append(out)
    v["e1"] = passed
    v["dw_other"] = [
        expert_grads(pos_dense, [v["k%d0" % r], v["k%d1" % r]], grid.chips, grid.cores) for r in lines
    ]
    gate("dw_other", "e1", "g0", "out0")

    v["other_core"] = [grid.cores_moved(groups) for groups in v["dw_other"]]
    gate("other_core", "e1", "out0", "dw_other")

    corner = [[grid.cores_added(g, m, s).astype(bf16) for s in chips] for g, m in zip(v["dw_other"], v["other_core"])]
    v["t_low"] = [[grid.chip(t[:cut], -s) for s, t in zip(chips, ts)] for ts in corner]
    v["t_high"] = [[grid.line(t[cut:], -r) for t in ts] if cut < local else [] for r, ts in zip(lines, corner)]
    v["m0"] = [v["out0"][4], grid.up(v["out0"][6], -2), grid.up(v["out0"][5], -1)]
    v["out1"], v["k01"] = experts(1, 0, own, v["e1"])
    gate("out1", "k01", "t_low", "t_high", "m0", "dw_other", "other_core", "out0")

    def backward(i):
        _, hidden, q, k2, v2, mixed, gates = v["f%d" % i]
        grad_tokens, xn1, gqkv, gbr, xn2, gl, gains = backward_part(
            offsets, v["g%d" % i], tokens[i, 0], hidden, cotangent[i, 0], gates, q, k2, v2,
            biases[i], tables, gain_a, gain_m, dense,
        )
        return grad_tokens, (xn1, gqkv, gbr, mixed, xn2, gl, gains)

    v["to_lines"] = []
    for i, r in enumerate(lines):
        total = grid.cores_added(v["dw_other"][i], v["other_core"][i], 0)
        for low in v["t_low"][i]:
            total = jnp.concatenate([total[:cut] + low.astype(f32), total[cut:]], axis=0)
        total = total.astype(bf16)
        v["to_lines"].append([total[:cut], total[cut:]] if cut < local else [total])
    gate("to_lines", "out1", "k01", "g0")
    v["g1"] = [v["out1"][0], *grid.back(v["out1"][1:4])]
    v["dw_own"] = expert_grads(pos_dense, [v["k00"], v["k01"]], grid.chips, grid.cores)
    v["home_y"] = [[grid.line(ts[0], -r)] for r, ts in zip(lines, v["to_lines"])]
    v["b0"] = backward(0)
    gate("b0", "g1", "dw_own", "t_high", "out1", "home_y", "to_lines")
    v["own_core"] = grid.cores_moved(v["dw_own"])
    gate("own_core", "dw_own", "t_high")

    ends = [cut, cut + (local - cut + 1) // 2, local]
    v["to_chips"] = []
    for k, s in enumerate(chips):
        total = grid.cores_added(v["dw_own"], v["own_core"], s)
        for i in range(len(lines)):
            if cut < local:
                total = jnp.concatenate([total[:cut], total[cut:] + v["t_high"][i][k].astype(f32)], axis=0)
        total = total.astype(bf16)
        v["to_chips"].append([total[a:b] for a, b in zip([0, *ends], ends) if a < b])
    v["home_x"] = [[grid.chip(ts[0], -s)] for s, ts in zip(chips, v["to_chips"])]
    for r, ts, held in zip(lines, v["to_lines"], v["home_y"]):
        held += [grid.line(t, -r) for t in ts[1:]]
    v["m1"] = [v["out1"][4], grid.up(v["out1"][6], -2)]
    v["b1"] = backward(1)
    v["dense"] = weight_part(pos_dense, [v["b0"][1], v["b1"][1]], grid.chips, grid.cores, n_exp)
    if not in_kernel(shard // n_exp):
        order = jnp.argsort(jnp.stack(steps))
        v["dense"] = [
            p.reshape(grid.chips, n_exp, shard // n_exp, WIDE)[:, order].reshape(p.shape) for p in v["dense"]
        ]
    gate("dense", "home_x", "to_chips", "m1", "out1", "home_y", "out0")

    v["dense_core"] = grid.cores_moved(v["dense"])
    for s, ts, held in zip(chips, v["to_chips"], v["home_x"]):
        held += [grid.chip(t, -s) for t in ts[1:2]]
    v["m1"].append(grid.up(v["out1"][5], -1))
    gate("dense_core", "dense", "home_x", "to_chips", "m1", "out1", "out0")

    split = WIDE // 2 // 128 * 128
    small = shard // n_exp
    sums = [
        grid.cores_added(v["dense"], v["dense_core"], s).reshape(grid.major, grid.minor, small, WIDE)
        for s in range(grid.chips)
    ]
    v["left"], v["right"] = [x[..., :split].astype(bf16) for x in sums], [x[..., split:].astype(bf16) for x in sums]
    v["left_far"] = [grid.chip(v["left"][s], -s) for s in chips]
    right = jnp.stack(v["right"])
    v["right_far"] = [grid.line(right[:, :, r], -r) for r in lines]
    v["m1"].append(grid.up(v["out1"][7], -3))
    gate("left", "right", "left_far", "right_far", "m1", "to_chips", "out0")

    left = v["left"][0].astype(f32)
    for part in v["left_far"]:
        left = left + part.astype(f32)
    right = jnp.stack(v["right"])[:, :, 0].astype(f32)
    for part in v["right_far"]:
        right = right + part.astype(f32)
    v["left"], v["right"] = left[:, 0], right[0]
    v["left_far"] = [grid.line(left[:, r].astype(bf16), -r) for r in lines]
    v["right_far"] = [grid.chip(right[s].astype(bf16), -s) for s in chips]
    v["m0"].append(grid.up(v["out0"][7], -3))
    gate("left", "right", "left_far", "right_far", "to_chips", "m0")

    left, right = v["left"], v["right"]
    for part in v["left_far"]:
        left = left + part.astype(f32)
    for part in v["right_far"]:
        right = right + part.astype(f32)
    mine = grid.major_home(jnp.concatenate([left, right], axis=-1))
    for s, ts, held in zip(chips, v["to_chips"], v["home_x"]):
        held += [grid.chip(t, -s) for t in ts[2:]]
    outputs = []
    for i in range(MB):
        total = v["m%d" % i][0]
        for part in v["m%d" % i][1:]:
            total = total + part.astype(f32)
        outputs.append((v["f%d" % i][1] + resid_mult * total).astype(bf16))
    grad_rows = [v["b0"][0], v["b1"][0]]

    total = grid.cores_added(v["dw_own"], v["own_core"], 0)
    for parts in (*v["home_y"], *v["home_x"]):
        total = total + jnp.concatenate(parts, axis=0).astype(f32)
    grad_gate_up, grad_down = total[:, :, : 2 * FFE], total[:, :, 2 * FFE :].transpose(0, 2, 1)

    return (
        jnp.stack(outputs)[:, None],
        jnp.stack(grad_rows)[:, None],
        mine[:, QKV + EXPERTS],
        mine[:, :QD],
        mine[:, QD : QD + KD],
        mine[:, QD + KD : QKV],
        mine[:, WO:].T,
        mine[:, QKV + EXPERTS + 1],
        mine[:, QKV : QKV + EXPERTS],
        grad_gate_up,
        grad_down,
    )


def solution(mesh):
    grid = Grid(mesh.shape["dp"], mesh.shape["expert"])
    in_specs = (
        P(None, ("dp", "expert"), None, None),
        P(None, ("dp", "expert"), None),
        P(None, ("dp", "expert"), None, None),
        P(),
        P("dp", None),
        P("dp", None),
        P("dp", None),
        P(None, "dp"),
        P(),
        P("dp", None),
        P("expert", "dp", None),
        P("expert", None, "dp"),
        P(None, ("dp", "expert"), None, None),
    )
    out_specs = (
        P(None, ("dp", "expert"), None, None),
        P(None, ("dp", "expert"), None, None),
        P(("dp", "expert")),
        P(("dp", "expert"), None),
        P(("dp", "expert"), None),
        P(("dp", "expert"), None),
        P(None, ("dp", "expert")),
        P(("dp", "expert")),
        P(("dp", "expert"), None),
        P("expert", "dp", None),
        P("expert", None, "dp"),
    )
    return jax.shard_map(
        functools.partial(on_device, grid), mesh=mesh, in_specs=in_specs, out_specs=out_specs, check_vma=False
    )
```

```python
import functools

import jax
import jax.numpy as jnp
from jax import lax
from jax.experimental import pallas as pl
from jax.experimental.pallas import tpu as pltpu
from jax.sharding import PartitionSpec as P

D = 1024
QUERY_HEADS = 16
KEY_VALUE_HEADS = 8
HEAD_SIZE = 64
FFE = 512
EXPERTS = 32
TOP = 8
SEG_LEN = 16
BRANCHES = 4
MB = 2
TRUNK = 64
NSEG = 13
TREE_TOKENS = 256
QD = 1024
KD = 512
CAP = 72
CAP_PAD = 80
QKV = QD + 2 * KD
WIDE = QKV + 128 + D
WO = QKV + 128
PAIR = 3 * FFE
EXT = 16
PAY = TREE_TOKENS + EXT

epsilon = 1e-06
attn_mult = 0.015625
resid_mult = 0.22
theta_base = 10000.0
neg_fill = -1e30

f32 = jnp.float32
bf16 = jnp.bfloat16
VMEM_LIMIT = 60 * 1024 * 1024


def dot(a, b, ca=1, cb=0):
    return lax.dot_general(a, b, (((ca,), (cb,)), ((), ())), preferred_element_type=f32)


def lanes(shape):
    return lax.broadcasted_iota(jnp.int32, shape, len(shape) - 1)


def params(**extra):
    return pltpu.CompilerParams(vmem_limit_bytes=VMEM_LIMIT, **extra)


def whole(shape):
    return pl.BlockSpec(shape, lambda *_: (0,) * len(shape))


def cost(flops, size, exps=0):
    return pl.CostEstimate(flops=int(flops), bytes_accessed=int(size), transcendentals=int(exps))


def tree_layout():
    row_index = jnp.arange(TREE_TOKENS, dtype=jnp.int32)
    branch_rest = row_index - TRUNK
    leaf_rest = branch_rest - BRANCHES * SEG_LEN
    in_trunk = row_index < TRUNK
    in_branch = branch_rest < BRANCHES * SEG_LEN
    segment = jnp.where(
        in_trunk,
        0,
        jnp.where(in_branch, 1 + branch_rest // SEG_LEN, 1 + BRANCHES + leaf_rest // SEG_LEN),
    )
    position = jnp.where(
        in_trunk,
        row_index,
        jnp.where(in_branch, TRUNK + branch_rest % SEG_LEN, TRUNK + SEG_LEN + leaf_rest % SEG_LEN),
    )
    return (segment, position)


def rope_tables(position):
    half_width = HEAD_SIZE // 2
    inverse_freq = theta_base ** (-2.0 * jnp.arange(half_width, dtype=f32) / HEAD_SIZE)
    angles = position.astype(f32)[:, None] * inverse_freq[None, :]
    c, s = jnp.cos(angles), jnp.sin(angles)
    return jnp.concatenate([c, c, c, c], axis=1), jnp.concatenate([-s, s, -s, s], axis=1)


def mask_bias(parent_row, segment):
    seg_ids = jnp.arange(NSEG, dtype=jnp.int32)
    parent_hot = (parent_row[:, None] == seg_ids[None, :]).astype(f32)
    ancestor = jnp.eye(NSEG, dtype=f32) + parent_hot + jnp.dot(parent_hot, parent_hot)
    seg_hot = (segment[:, None] == seg_ids[None, :]).astype(f32)
    reach = jnp.dot(jnp.dot(seg_hot, ancestor), seg_hot.T)
    rows = jnp.arange(TREE_TOKENS, dtype=jnp.int32)
    allowed = (reach > 0.5) & (rows[None, :] <= rows[:, None])
    return jnp.where(allowed, 0.0, neg_fill).astype(f32)


def swap_halves(u):
    first = (lanes(u.shape) % HEAD_SIZE) < HEAD_SIZE // 2
    return jnp.where(first, pltpu.roll(u, 96, 1), pltpu.roll(u, 32, 1))


def twice(u, upper):
    low = lanes(u.shape) < HEAD_SIZE
    turned = pltpu.roll(u, HEAD_SIZE, 1)
    return jnp.where(low, turned, u) if upper else jnp.where(low, u, turned)


def split_heads(u):
    low = lanes(u.shape) < HEAD_SIZE
    zero = jnp.zeros_like(u)
    return jnp.concatenate([jnp.where(low, u, zero), jnp.where(low, zero, u)], axis=0)


def softmax_rows(scores, bias):
    s = scores.reshape(2, TREE_TOKENS, TREE_TOKENS) * attn_mult + bias[None]
    e = jnp.exp(s - jnp.max(s, axis=-1, keepdims=True))
    p = e * (1.0 / jnp.sum(e, axis=-1, keepdims=True))
    return p.reshape(2 * TREE_TOKENS, TREE_TOKENS)


def gather_weights(refs, offsets, to, sem, wait):
    for i, ref in enumerate(refs):
        rows = ref.shape[0]
        copy = pltpu.make_async_copy(
            ref, to.at[pl.ds(pl.multiple_of(offsets[i], rows), rows)], sem.at[i]
        )
        if wait:
            copy.wait()
        else:
            copy.start()


def forward_kernel(n_dense, offsets, *refs):
    tokens, bias, cos2, sin2, gain_a, gain_m, routes = refs[:7]
    dense = refs[7 : 7 + n_dense]
    xnp, hidden_out, q_out, k2_out, v2_out, mixed_out, gates_out = refs[7 + n_dense : 14 + n_dense]
    w, sem = refs[14 + n_dense :]
    gather_weights(dense, offsets, w, sem, False)
    x = tokens[...].astype(f32)
    r1 = lax.rsqrt(jnp.mean(x * x, axis=1, keepdims=True) + epsilon)
    xn1 = (x * r1 * gain_a[...]).astype(bf16)
    gather_weights(dense, offsets, w, sem, True)
    qkv = dot(xn1, w[:, :QKV])
    c, s = cos2[...], sin2[...]
    for m in range(KEY_VALUE_HEADS):
        u = qkv[:, 128 * m : 128 * m + 128]
        q_out[:, 128 * m : 128 * m + 128] = (u * c + swap_halves(u) * s).astype(bf16)
    for n in range(KEY_VALUE_HEADS // 2):
        u = qkv[:, QD + 128 * n : QD + 128 * n + 128]
        u = u * c + swap_halves(u) * s
        o = qkv[:, QD + KD + 128 * n : QD + KD + 128 * n + 128]
        for half in range(2):
            at = 128 * (2 * n + half)
            k2_out[:, at : at + 128] = twice(u, half).astype(bf16)
            v2_out[:, at : at + 128] = twice(o, half).astype(bf16)

    def one(m, carry):
        at = pl.ds(pl.multiple_of(m * 128, 128), 128)
        qq = split_heads(q_out[:, at])
        p = softmax_rows(dot(qq, k2_out[:, at], 1, 1), bias[...]).astype(bf16)
        o = dot(p, v2_out[:, at])
        low = lanes((TREE_TOKENS, 128)) < HEAD_SIZE
        mixed_out[:, at] = jnp.where(low, o[:TREE_TOKENS], o[TREE_TOKENS:]).astype(bf16)
        return carry

    lax.fori_loop(0, KEY_VALUE_HEADS, one, 0, unroll=2)
    h = x + resid_mult * dot(mixed_out[...], w[:, WO:], 1, 1)
    hidden_out[...] = h
    r2 = lax.rsqrt(jnp.mean(h * h, axis=1, keepdims=True) + epsilon)
    xn2 = (h * r2 * gain_m[...]).astype(bf16)
    xnp[:TREE_TOKENS] = xn2
    lt = dot(xn2, w[:, QKV:WO]).T[:EXPERTS]
    ids = lax.broadcasted_iota(jnp.int32, (EXPERTS, TREE_TOKENS), 0)
    named = ids == routes[0:1, :]
    for k in range(1, TOP):
        named = named | (ids == routes[k : k + 1, :])
    lt = jnp.where(named, lt, neg_fill)
    e = jnp.where(named, jnp.exp(lt - jnp.max(lt, axis=0, keepdims=True)), 0.0)
    g = e / jnp.sum(e, axis=0, keepdims=True)
    gates_out[...] = g
    packed = pack_rows(g)
    hi = packed.astype(bf16)
    low_part = (packed - hi.astype(f32)).astype(bf16)
    xnp[TREE_TOKENS:] = jnp.concatenate([hi.astype(f32), low_part.astype(f32)], axis=0).astype(bf16)


def pack_rows(g):
    return jnp.concatenate([g[8 * i : 8 * i + 8] for i in range(4)], axis=1)


def unpack_rows(g):
    return jnp.concatenate([g[:, 256 * i : 256 * i + 256] for i in range(4)], axis=0)


def any_space(n):
    return [pl.BlockSpec(memory_space=pl.ANY)] * n


def forward_part(offsets, tokens, bias, tables, gain_a, gain_m, routes, dense):
    t = TREE_TOKENS
    ins = [tokens, bias, *tables, gain_a, gain_m, routes]
    outs = [((PAY, D), bf16), ((t, D), f32)] + [((t, QD), bf16)] * 4 + [((EXPERTS, t), f32)]
    return pl.pallas_call(
        functools.partial(forward_kernel, len(dense)),
        grid_spec=pltpu.PrefetchScalarGridSpec(
            num_scalar_prefetch=1,
            grid=(1,),
            in_specs=[whole(a.shape) for a in ins] + any_space(len(dense)),
            out_specs=[whole(s) for s, _ in outs],
            scratch_shapes=[pltpu.VMEM((D, WIDE), bf16), pltpu.SemaphoreType.DMA((len(dense),))],
        ),
        out_shape=[jax.ShapeDtypeStruct(s, d) for s, d in outs],
        compiler_params=params(),
        cost_estimate=cost(1, 1),
        name="attention_forward",
    )(offsets, *ins, *dense)


def expert_kernel(layout, local, n_before, last, pos, *refs):
    refs = list(refs)

    def take(n):
        out = refs[:n]
        del refs[:n]
        return out

    n_dp = len(layout)
    rows_in, cots_in = take(5), take(5)
    weights = [take(len(sizes)) for sizes in layout]
    before_in = [take(3) for _ in range(n_before)]
    outs = take(8) if last else take(3)
    sent_out, hid_out, gboth_out, geo_out = take(4)
    rank_s, gate_s, x1_s, x3_s, c1_s, c3_s, w_s, w_sem = take(8)
    sel_s, comb_s, gg_s = take(3) if last else outs
    e = pl.program_id(0)
    shard = D // n_dp
    base = pos[n_dp] * local
    at_start, at_end = pos[n_dp + 1] == 0, pos[n_dp + 1] == 3
    t = TREE_TOKENS
    ids = lax.broadcasted_iota(jnp.int32, (EXPERTS, t), 0)
    xs = [rows_in[0], x1_s, rows_in[2], x3_s]
    cots = [cots_in[0], c1_s, cots_in[2], c3_s]

    def load(expert, slot):
        for p, (parts, sizes) in enumerate(zip(weights, layout)):
            to = w_s.at[slot, pl.ds(pl.multiple_of(pos[p] * shard, shard), shard)]
            offset = 0
            for part, size in zip(parts, sizes):
                if len(sizes) == 1:
                    pltpu.make_async_copy(part.at[expert], to, w_sem.at[slot, p]).start()
                else:

                    @pl.when((expert >= offset) & (expert < offset + size))
                    def _():
                        pltpu.make_async_copy(part.at[expert - offset], to, w_sem.at[slot, p]).start()

                offset += size

    def arrive(slot):
        for p in range(n_dp):
            to = w_s.at[slot, pl.ds(pl.multiple_of(pos[p] * shard, shard), shard)]
            pltpu.make_async_copy(weights[p][0].at[0], to, w_sem.at[slot, p]).wait()

    slot_now = e % 2

    @pl.when(e == 0)
    def _():
        load(0, 0)

    @pl.when(e + 1 < local)
    def _():
        load(e + 1, 1 - slot_now)

    @pl.when(e == 0)
    def _():
        for given, lower, upper in ((rows_in, x1_s, x3_s), (cots_in, c1_s, c3_s)):
            lower[...] = jnp.where(at_start, given[4][...], given[1][...])
            upper[...] = jnp.where(at_end, given[4][...], given[3][...])
        gates = []
        for b in range(4):
            ext = xs[b][t:].astype(f32)
            full = unpack_rows(ext[:8] + ext[8:16])
            gates.append(
                [
                    jnp.sum(jnp.where(ids == base + el, full, 0.0), axis=0, keepdims=True)
                    for el in range(local)
                ]
            )
        before = lax.broadcasted_iota(jnp.int32, (t, t), 0) < lax.broadcasted_iota(jnp.int32, (t, t), 1)
        before = before.astype(f32).astype(bf16)
        for el in range(local):
            gate = jnp.concatenate([gates[b][el] for b in range(4)] + [jnp.zeros((4, t), f32)], axis=0)
            used = gate > 0.0
            rank = dot(used.astype(f32).astype(bf16), before)
            gate_s[el] = gate
            rank_s[el] = jnp.where(used, rank, -1.0)
        sel_s[...] = jnp.zeros_like(sel_s)
        comb_s[...] = jnp.zeros_like(comb_s)

    gate, rank = gate_s[e], rank_s[e]
    slot = lax.broadcasted_iota(jnp.int32, (CAP, t), 0).astype(f32)
    sels, sent, cot, gate_slot = [], [], [], []
    for b in range(4):
        hit = slot == rank[b : b + 1]
        sel = jnp.where(hit, 1.0, 0.0)
        sels.append(sel)
        low = sel.astype(bf16)
        sent.append(dot(low, xs[b][:t]))
        cot.append(dot(low, cots[b][:t]))
        gate_slot.append(jnp.sum(jnp.where(hit, gate[b : b + 1], 0.0), axis=1, keepdims=True))
    sent_out[0] = jnp.concatenate(sent, axis=0).astype(bf16)
    gm = jnp.concatenate(cot, axis=0) * resid_mult
    gate_slot = jnp.concatenate(gate_slot, axis=0)
    geo_out[0] = (gm * gate_slot).astype(bf16)
    arrive(slot_now)
    both = dot(sent_out[0], w_s[slot_now, :, : 2 * FFE])
    gh, up = both[:, :FFE], both[:, FFE:]
    sigma = 1.0 / (1.0 + jnp.exp(-gh))
    hid_out[0] = (gh * sigma * up).astype(bf16)
    eo = dot(hid_out[0], w_s[slot_now, :, 2 * FFE :], 1, 1).astype(bf16).astype(f32)
    gs = dot(geo_out[0], w_s[slot_now, :, 2 * FFE :]) * sigma
    gboth_out[0] = jnp.concatenate(
        [(gs * up * (1.0 + gh * (1.0 - sigma))).astype(bf16), (gs * gh).astype(bf16)], axis=1
    )
    grad_sent = dot(gboth_out[0], w_s[slot_now, :, : 2 * FFE], 1, 1)
    gg = jnp.sum(gm * eo, axis=1, keepdims=True)
    weighted = gate_slot * eo
    ggs = []
    for b in range(4):
        part = slice(CAP * b, CAP * b + CAP)
        where = pl.ds(pl.multiple_of(e * CAP_PAD, 16), CAP)
        sel_s[b, where] = sels[b].astype(bf16)
        comb_s[b, where, :D] = grad_sent[part].astype(bf16)
        comb_s[b, where, D:] = weighted[part].astype(bf16)
        ggs.append(jnp.sum(sels[b] * gg[part], axis=0, keepdims=True))
    gg_s[e] = jnp.concatenate(ggs + [jnp.zeros((4, t), f32)], axis=0)

    if not last:
        return

    @pl.when(e == local - 1)
    def _():
        for b in range(4):
            total = dot(sel_s[b], comb_s[b], 0, 0)
            full = jnp.zeros((EXPERTS, t), f32)
            for el in range(local):
                full = full + jnp.where(ids == base + el, gg_s[el, b : b + 1], 0.0)
            for i, (sel_b, comb_b, gg_b) in enumerate(before_in):
                total = total + dot(sel_b[b], comb_b[b], 0, 0)
                owner = pos[n_dp + 2 + i] * local
                for el in range(local):
                    full = full + jnp.where(ids == owner + el, gg_b[el, b : b + 1], 0.0)
            outs[b][:t] = total[:, :D].astype(outs[b].dtype)
            outs[4 + b][...] = total[:, D:].astype(outs[4 + b].dtype)
            packed = pack_rows(full)
            hi = packed.astype(bf16)
            rest = (packed - hi.astype(f32)).astype(bf16)
            ext = jnp.concatenate([hi.astype(f32), rest.astype(f32)], axis=0)
            outs[b][t:] = ext.astype(outs[b].dtype)


def expert_part(pos, rows, cots, weights, before, last):
    n_dp = len(weights)
    local = sum(part.shape[0] for part in weights[0])
    t = TREE_TOKENS
    m = CAP * 4
    layout = tuple(tuple(part.shape[0] for part in parts) for parts in weights)
    flat = [part for parts in weights for part in parts]
    earlier = [a for one in before for a in one]
    ins = [*rows, *cots, *flat, *earlier]
    in_specs = [whole(a.shape) for a in (*rows, *cots)]
    in_specs += [pl.BlockSpec(memory_space=pl.ANY)] * len(flat)
    in_specs += [whole(a.shape) for a in earlier]
    passed = [
        ((4, local * CAP_PAD, t), bf16),
        ((4, local * CAP_PAD, 2 * D), bf16),
        ((local, 8, t), f32),
    ]
    if last:
        kinds = [f32, bf16, bf16, bf16]
        outs = [((PAY, D), k) for k in kinds] + [((t, D), k) for k in kinds]
    else:
        outs = list(passed)
    n_main = len(outs)
    out_specs = [whole(s) for s, _ in outs]
    kept = [D, FFE, 2 * FFE, D]
    outs = outs + [((local, m, w), bf16) for w in kept]
    out_specs = out_specs + [pl.BlockSpec((1, m, w), lambda e, *_: (e, 0, 0)) for w in kept]
    scratch = [
        pltpu.VMEM((local, 8, t), f32),
        pltpu.VMEM((local, 8, t), f32),
        pltpu.VMEM((PAY, D), bf16),
        pltpu.VMEM((PAY, D), bf16),
        pltpu.VMEM(cots[0].shape, bf16),
        pltpu.VMEM(cots[0].shape, bf16),
        pltpu.VMEM((2, D, PAIR), bf16),
        pltpu.SemaphoreType.DMA((2, n_dp)),
    ]
    if last:
        scratch += [pltpu.VMEM(s, d) for s, d in passed]
    res = pl.pallas_call(
        functools.partial(expert_kernel, layout, local, len(before), last),
        grid_spec=pltpu.PrefetchScalarGridSpec(
            num_scalar_prefetch=1,
            grid=(local,),
            in_specs=in_specs,
            out_specs=out_specs,
            scratch_shapes=scratch,
        ),
        out_shape=[jax.ShapeDtypeStruct(s, d) for s, d in outs],
        compiler_params=params(),
        cost_estimate=cost(1, 1),
        name="experts",
    )(pos, *ins)
    return res[:n_main], res[n_main:]


def expert_grad_kernel(n_dp, n_kept, pos, *refs):
    kept = [refs[4 * i : 4 * i + 4] for i in range(n_kept)]
    outs = refs[4 * n_kept :]
    shard = D // n_dp
    for p in range(n_dp):
        at = pl.ds(pl.multiple_of(pos[p] * shard, shard), shard)
        gate_up, down = None, None
        for sent, hid, gboth, geo in kept:
            part = dot(sent[0, :, at], gboth[0], 0, 0)
            gate_up = part if gate_up is None else gate_up + part
            part = dot(geo[0, :, at], hid[0], 0, 0)
            down = part if down is None else down + part
        out = outs[p % len(outs)]
        out[p // len(outs), 0, :, : 2 * FFE] = gate_up.astype(out.dtype)
        out[p // len(outs), 0, :, 2 * FFE :] = down.astype(out.dtype)


def expert_grads(pos, kept, chips, cores):
    local, m, _ = kept[0][0].shape
    n_dp = chips * cores
    shard = D // n_dp
    flat = [a for one in kept for a in one]
    shape = (chips, local, shard, PAIR)
    return pl.pallas_call(
        functools.partial(expert_grad_kernel, n_dp, len(kept)),
        grid_spec=pltpu.PrefetchScalarGridSpec(
            num_scalar_prefetch=1,
            grid=(local,),
            in_specs=[pl.BlockSpec((1, *a.shape[1:]), lambda e, *_: (e, 0, 0)) for a in flat],
            out_specs=[pl.BlockSpec((chips, 1, shard, PAIR), lambda e, *_: (0, e, 0, 0))] * cores,
        ),
        out_shape=[jax.ShapeDtypeStruct(shape, bf16)] * cores,
        compiler_params=params(),
        cost_estimate=cost(1, 1),
        name="expert_grads",
    )(pos, *flat)


def backward_kernel(n_dense, n_grads, offsets, *refs):
    grads = refs[:n_grads]
    tokens, hidden, cot, gates, q, k2, v2, bias, cos2, sin2, gain_a, gain_m = refs[n_grads : n_grads + 12]
    dense = refs[n_grads + 12 : n_grads + 12 + n_dense]
    rest = refs[n_grads + 12 + n_dense :]
    grad_tokens, xn1_out, gqkv_out, gbr_out, xn2_out, gl_out, gains_out = rest[:7]
    gmix, w, sem = rest[7:]
    t = TREE_TOKENS
    gather_weights(dense, offsets, w, sem, False)
    total = grads[0][...].astype(f32)
    for other in grads[1:]:
        total = total + other[...].astype(f32)
    gg = unpack_rows(total[t : t + 8] + total[t + 8 : t + 16])
    g = gates[...]
    gl = g * (gg - jnp.sum(g * gg, axis=0, keepdims=True))
    gl = jnp.concatenate([gl, jnp.zeros((128 - EXPERTS, t), f32)], axis=0).T.astype(bf16)
    gl_out[...] = gl
    gather_weights(dense, offsets, w, sem, True)
    gx2 = total[:t] + dot(gl, w[:, QKV:WO], 1, 1)
    h = hidden[...]
    r2 = lax.rsqrt(jnp.mean(h * h, axis=1, keepdims=True) + epsilon)
    xn2_out[...] = (h * r2 * gain_m[...]).astype(bf16)
    u2 = gx2 * gain_m[...]
    ghs = cot[...].astype(f32) + r2 * u2 - h * (r2 * r2 * r2) * jnp.mean(u2 * h, axis=1, keepdims=True)
    gain2 = jnp.sum(gx2 * h * r2, axis=0, keepdims=True)
    gbr_out[...] = (resid_mult * ghs).astype(bf16)
    gmix[...] = dot(gbr_out[...], w[:, WO:]).astype(bf16)
    low = lanes((t, 128)) < HEAD_SIZE
    c, s = cos2[...], sin2[...]

    def unrotate(w):
        return w * c + swap_halves(w * s)

    def one(n, carry):
        keys, values = [], []
        for half in range(2):
            at = pl.ds(pl.multiple_of(n * 256 + 128 * half, 128), 128)
            qq = split_heads(q[:, at])
            dd = split_heads(gmix[:, at])
            kk = k2[:, at]
            pf = softmax_rows(dot(qq, kk, 1, 1), bias[...])
            gp = dot(dd, v2[:, at], 1, 1)
            gsc = (pf * (gp - jnp.sum(pf * gp, axis=1, keepdims=True))).astype(bf16)
            gq = dot(gsc, kk)
            gq = attn_mult * jnp.where(low, gq[:t], gq[t:])
            gqkv_out[:, at] = unrotate(gq).astype(bf16)
            gk = attn_mult * dot(gsc, qq, 0, 0)
            keys.append(gk + pltpu.roll(gk, HEAD_SIZE, 1))
            gv = dot(pf.astype(bf16), dd, 0, 0)
            values.append(gv + pltpu.roll(gv, HEAD_SIZE, 1))
        at = pl.ds(pl.multiple_of(QD + n * 128, 128), 128)
        gqkv_out[:, at] = unrotate(jnp.where(low, keys[0], keys[1])).astype(bf16)
        at = pl.ds(pl.multiple_of(QD + KD + n * 128, 128), 128)
        gqkv_out[:, at] = jnp.where(low, values[0], values[1]).astype(bf16)
        return carry

    lax.fori_loop(0, KEY_VALUE_HEADS // 2, one, 0)
    gx1 = dot(gqkv_out[...], w[:, :QKV], 1, 1)
    x = tokens[...].astype(f32)
    r1 = lax.rsqrt(jnp.mean(x * x, axis=1, keepdims=True) + epsilon)
    xn1_out[...] = (x * r1 * gain_a[...]).astype(bf16)
    u1 = gx1 * gain_a[...]
    grad_tokens[...] = ghs + r1 * u1 - x * (r1 * r1 * r1) * jnp.mean(u1 * x, axis=1, keepdims=True)
    gain1 = jnp.sum(gx1 * x * r1, axis=0, keepdims=True)
    gains_out[...] = jnp.concatenate([gain1, gain2, jnp.zeros((6, D), f32)], axis=0)


def backward_part(offsets, grads, tokens, hidden, cot, gates, q, k2, v2, bias, tables, gain_a, gain_m, dense):
    t = TREE_TOKENS
    ins = [*grads, tokens, hidden, cot, gates, q, k2, v2, bias, *tables, gain_a, gain_m]
    outs = [
        ((t, D), f32),
        ((t, D), bf16),
        ((t, QKV), bf16),
        ((t, D), bf16),
        ((t, D), bf16),
        ((t, 128), bf16),
        ((8, D), f32),
    ]
    return pl.pallas_call(
        functools.partial(backward_kernel, len(dense), len(grads)),
        grid_spec=pltpu.PrefetchScalarGridSpec(
            num_scalar_prefetch=1,
            grid=(1,),
            in_specs=[whole(a.shape) for a in ins] + any_space(len(dense)),
            out_specs=[whole(s) for s, _ in outs],
            scratch_shapes=[
                pltpu.VMEM((t, D), bf16),
                pltpu.VMEM((D, WIDE), bf16),
                pltpu.SemaphoreType.DMA((len(dense),)),
            ],
        ),
        out_shape=[jax.ShapeDtypeStruct(s, d) for s, d in outs],
        compiler_params=params(),
        cost_estimate=cost(1, 1),
        name="attention_backward",
    )(offsets, *ins, *dense)


def in_kernel(rows):
    return rows % 16 == 0


def weight_kernel(n_dp, n_exp, pos, *refs):
    per = 7
    sets = [refs[per * i : per * i + per] for i in range(MB)]
    outs = refs[per * MB :]
    cores = len(outs)
    shard, small = D // n_dp, D // n_dp // n_exp
    for p in range(n_dp):
        at = pl.ds(pl.multiple_of(pos[p] * shard, shard), shard)

        def product(left, right):
            total = None
            for one in sets:
                part = dot(one[left][:, at], one[right][...], 0, 0)
                total = part if total is None else total + part
            return total

        gains = sets[0][6][:, at]
        for one in sets[1:]:
            gains = gains + one[6][:, at]
        gains = jnp.concatenate(
            [jnp.zeros((EXPERTS, shard), f32), gains, jnp.zeros((120 - EXPERTS, shard), f32)], axis=0
        )
        blocks = [product(0, 1), product(4, 5) + gains.T, product(2, 3)]
        pieces = n_exp if in_kernel(small) else 1
        size = shard // pieces
        for i in range(pieces):
            rows = slice(size * i, size * i + size)
            to = pl.ds(pl.multiple_of(pos[n_dp + i] * size, size), size) if pieces > 1 else slice(None)
            offset = 0
            for value in blocks:
                width = value.shape[1]
                outs[p % cores][p // cores, to, offset : offset + width] = value[rows].astype(bf16)
                offset += width


def weight_part(pos, sets, chips, cores, n_exp):
    flat = [a for one in sets for a in one]
    n_dp = chips * cores
    shape = (chips, D // n_dp, WIDE)
    return pl.pallas_call(
        functools.partial(weight_kernel, n_dp, n_exp),
        grid_spec=pltpu.PrefetchScalarGridSpec(
            num_scalar_prefetch=1,
            grid=(1,),
            in_specs=[whole(a.shape) for a in flat],
            out_specs=[whole(shape)] * cores,
        ),
        out_shape=[jax.ShapeDtypeStruct(shape, bf16)] * cores,
        compiler_params=params(),
        cost_estimate=cost(1, 1),
        name="dense_grads",
    )(pos, *flat)


class Grid:
    def __init__(self, n_dp, n_exp):
        self.n_dp, self.n_exp = n_dp, n_exp
        self.cores = 2 if n_dp % 2 == 0 else 1
        self.chips = n_dp // self.cores
        self.major = 4
        self.minor = n_exp // self.major

    def move(self, x, axis, to):
        major, minor = (self.chips, self.cores) if axis == "dp" else (self.major, self.minor)
        pairs = []
        for i in range(major * minor):
            target = to(*divmod(i, minor))
            if target is not None:
                pairs.append((i, target[0] * minor + target[1]))
        return lax.ppermute(x, axis, pairs)

    def chip(self, x, s):
        return self.move(x, "dp", lambda a, b: ((a + s) % self.chips, b))

    def core(self, x, s):
        return self.move(x, "dp", lambda a, b: (a, (b + s) % self.cores))

    def line(self, x, s):
        return self.move(x, "expert", lambda a, b: (a, (b + s) % self.minor))

    def up(self, x, s):
        return self.move(x, "expert", lambda a, b: ((a + s) % 4, b))

    def next_up(self, x):
        return self.move(x, "expert", lambda a, b: (a + 1, b) if a < 3 else None)

    def next_down(self, x):
        return self.move(x, "expert", lambda a, b: (a - 1, b) if a > 0 else None)

    def outward(self, x):
        return self.move(x, "expert", lambda a, b: {1: (0, b), 2: (3, b)}.get(a))

    def back(self, parts):
        return [self.up(x, -k) for k, x in enumerate(parts, 1)]

    def dp_places(self):
        i = lax.axis_index("dp")
        a, b = i // self.cores, i % self.cores
        return [
            (a - s) % self.chips * self.cores + (b - c) % self.cores
            for s in range(self.chips)
            for c in range(self.cores)
        ]

    def exp_steps(self):
        i = lax.axis_index("expert")
        a, b = i // self.minor, i % self.minor
        return [
            (a - k // self.minor) % self.major * self.minor + (b - k % self.minor) % self.minor
            for k in range(self.n_exp)
        ]

    def cores_moved(self, groups):
        return [self.core(g, -c) for c, g in enumerate(groups) if c]

    def cores_added(self, groups, moved, s, a=None, b=None):
        total = groups[0][s, a:b].astype(f32)
        for part in moved:
            total = total + part[s, a:b].astype(f32)
        return total

    def major_home(self, blocks):
        total = blocks[0]
        for s in range(1, self.major):
            total = total + self.up(blocks[s].astype(bf16), -s).astype(f32)
        return total


def on_device(
    grid,
    tokens,
    parents,
    routes,
    gain_attn,
    w_query,
    key_matrix,
    value_matrix,
    w_out,
    gain_moe,
    router,
    expert_gate_up,
    expert_down,
    cotangent,
):
    n_dp, n_exp = grid.n_dp, grid.n_exp
    shard = D // n_dp
    places = grid.dp_places()
    me = lax.axis_index("expert")
    major, minor = me // grid.minor, me % grid.minor
    steps = grid.exp_steps()
    owners = [major * grid.minor + (minor - r) % grid.minor for r in range(grid.minor)]

    def pos(i, r):
        before = owners[:r] if i == 0 else (owners[1:r] if r else owners[1:])
        return jnp.stack([*places, owners[r], major, *before, jnp.int32(0)]).astype(jnp.int32)

    pos_dense = jnp.stack([*places, *steps]).astype(jnp.int32)
    chips, lines, cores = range(1, grid.chips), range(1, grid.minor), range(grid.cores)
    local = expert_gate_up.shape[0]
    cut = local - local // 2
    v = {}

    def gate(*names):
        flat, tree = jax.tree.flatten([v[name] for name in names])
        v.update(zip(names, jax.tree.unflatten(tree, lax.optimization_barrier(flat))))

    segment, position = tree_layout()
    tables = rope_tables(position)
    gain_a, gain_m = gain_attn.reshape(1, D), gain_moe.reshape(1, D)
    biases = [mask_bias(parents[i, 0], segment) for i in range(MB)]
    for i in range(MB):
        v["tok%d" % i], v["cot%d" % i] = tokens[i, 0], cotangent[i, 0]

    def pairs(a, b):
        if a == b:
            return []
        return [jnp.concatenate([expert_gate_up[a:b], expert_down[a:b].transpose(0, 2, 1)], axis=2)]

    def over_cores(arrays):
        return [[grid.core(x, c) for x in arrays] for c in cores[1:]]

    def joined(*parts):
        return [sum(held, []) for held in zip(*parts)]

    packed = jnp.concatenate(
        [w_query, key_matrix, value_matrix, router, jnp.zeros((shard, 128 - EXPERTS), bf16), w_out.T], axis=1
    )
    half = local // 2
    quarter = half // 2
    v["far"] = [grid.chip(packed, s) for s in chips]
    v["packed"] = packed
    v["wy"] = [[grid.line(w, r) for w in pairs(0, half)] for r in lines]
    v["c0a"], v["c0b"], v["c0c"] = grid.next_up(v["cot0"]), grid.up(v["cot0"], 2), grid.next_down(v["cot0"])
    v["pair"] = pairs(0, local)
    v["xa"], v["xb"], v["xc"] = pairs(0, quarter), pairs(half, local), pairs(quarter, half)
    gate("far", "packed", "wy", "c0a", "c0b", "c0c", "pair", "xa", "xb", "xc")

    v["far_core"] = [[grid.core(f, c) for c in cores[1:]] for f in v["far"]]
    v["packed_core"] = [grid.core(v["packed"], c) for c in cores[1:]]
    gate("far_core", "packed_core", "tok0", "pair", "xa", "xb", "xc", "cot1", "c0b", "wy")

    dense = [packed, *v["packed_core"]]
    for f, fs in zip(v["far"], v["far_core"]):
        dense += [f, *fs]
    offsets = (jnp.stack(places) * shard).astype(jnp.int32)

    def forward(i):
        return forward_part(
            offsets, v["tok%d" % i], biases[i], tables, gain_a, gain_m, routes[i, 0].T, dense
        )

    v["f0"] = forward(0)
    v["wxa"] = [[grid.chip(w, s) for w in v["xa"]] for s in chips]
    v["pair_core"] = over_cores(v["pair"])
    v["c0d"], v["c1b"] = grid.outward(v["c0b"]), grid.up(v["cot1"], 2)
    gate("f0", "wxa", "pair_core", "c0d", "c1b", "tok1", "xb", "xc", "wy")

    row = v["f0"][0]
    v["n0a"], v["n0b"], v["n0c"] = grid.next_up(row), grid.up(row, 2), grid.next_down(row)
    v["wxb"] = [[grid.chip(w, s) for w in v["xb"]] for s in chips]
    v["wyb"] = [[grid.line(w, r) for w in v["xb"]] for r in lines]
    v["f1"] = forward(1)
    gate("n0a", "n0b", "n0c", "wxb", "wyb", "f1", "cot1", "xc", "wy")

    v["wxc"] = [[grid.chip(w, s) for w in v["xc"]] for s in chips]
    v["wxa_core"] = [over_cores(ws) for ws in v["wxa"]]
    v["wxb_core"] = [over_cores(ws) for ws in v["wxb"]]
    v["n0d"] = grid.outward(v["n0b"])
    v["wy_core"] = [over_cores(ws) for ws in v["wy"]]
    gate("wxc", "wxa_core", "wxb_core", "wy_core", "n0d", "f1", "cot1", "wy", "wxb", "wyb")

    v["wxc_core"] = [over_cores(ws) for ws in v["wxc"]]
    v["wyb_core"] = [over_cores(ws) for ws in v["wyb"]]
    gate("wxc_core", "wyb_core", "f1", "cot1", "wy", "wxb")

    own = [tuple(v["pair"]), *[tuple(w) for w in v["pair_core"]]]
    for k in range(len(chips)):
        own.append((*v["wxa"][k], *v["wxc"][k], *v["wxb"][k]))
        own += [tuple(ws) for ws in joined(v["wxa_core"][k], v["wxc_core"][k], v["wxb_core"][k])]

    def experts(i, r, weights, before):
        name = "%d" % i
        rows = [v["f" + name][0], *[v["n" + name + k] for k in "abcd"]]
        cots = [v["cot" + name], *[v["c" + name + k] for k in "abcd"]]
        return expert_part(pos(i, r), rows, cots, weights, before, len(before) == grid.minor - 1)

    v["e00"], v["k00"] = experts(0, 0, own, [])
    row = v["f1"][0]
    v["n1a"], v["n1b"], v["n1c"] = grid.next_up(row), grid.up(row, 2), grid.next_down(row)
    v["low"] = [[[grid.chip(w, s) for w in ws] for s in chips] for ws in v["wy"]]
    v["high"] = [[[grid.line(w, r) for w in ws] for ws in v["wxb"]] for r in lines]
    gate("e00", "low", "high", "n1a", "n1b", "n1c", "f1", "cot1", "c1b", "wy", "wyb")

    v["low_core"] = [[over_cores(w) for w in ws] for ws in v["low"]]
    v["high_core"] = [[over_cores(w) for w in ws] for ws in v["high"]]
    gate("low_core", "high_core", "f1", "n1b", "e00", "cot1", "c1b")

    sets = [own]
    for i in range(len(lines)):
        parts = [(*v["wy"][i], *v["wyb"][i])]
        parts += [tuple(ws) for ws in joined(v["wy_core"][i], v["wyb_core"][i])]
        for k in range(len(chips)):
            parts.append((*v["low"][i][k], *v["high"][i][k]))
            parts += [tuple(ws) for ws in joined(v["low_core"][i][k], v["high_core"][i][k])]
        sets.append(parts)
    v["n1d"] = grid.outward(v["n1b"])
    v["c1d"] = grid.outward(v["c1b"])
    v["c1a"], v["c1c"] = grid.next_up(v["cot1"]), grid.next_down(v["cot1"])
    passed = [v["e00"]]
    for r in lines:
        out, v["k%d0" % r] = experts(0, r, sets[r], passed)
        passed.append(out)
    v["out0"] = passed[-1]
    gate("out0", "c1a", "c1c", "c1d", "n1d", "f1")

    def home(out, first, *steps):
        return [grid.up(out[first + k], -k) for k in steps]

    v["g0"] = [v["out0"][0], *home(v["out0"], 0, 1, 2)]
    passed = []
    for r in lines:
        out, v["k%d1" % r] = experts(1, r, sets[r], passed)
        passed.append(out)
    v["e1"] = passed
    v["dw_other"] = [
        expert_grads(pos_dense, [v["k%d0" % r], v["k%d1" % r]], grid.chips, grid.cores) for r in lines
    ]
    gate("dw_other", "e1", "g0", "out0")

    v["other_core"] = [grid.cores_moved(groups) for groups in v["dw_other"]]
    v["g0"] += home(v["out0"], 0, 3)
    v["m0"] = [v["out0"][4], *home(v["out0"], 4, 1)]
    v["out1"], v["k01"] = experts(1, 0, own, v["e1"])
    gate("out1", "k01", "other_core", "g0", "m0", "dw_other", "out0")

    def backward(i):
        _, hidden, q, k2, v2, mixed, gates = v["f%d" % i]
        grad_tokens, xn1, gqkv, gbr, xn2, gl, gains = backward_part(
            offsets, v["g%d" % i], tokens[i, 0], hidden, cotangent[i, 0], gates, q, k2, v2,
            biases[i], tables, gain_a, gain_m, dense,
        )
        return grad_tokens, (xn1, gqkv, gbr, mixed, xn2, gl, gains)

    def corner(a, b):
        return [
            [grid.cores_added(g, m, s, a, b).astype(bf16) for s in chips]
            for g, m in zip(v["dw_other"], v["other_core"])
        ]

    middle, top = (cut + 1) // 2, cut + (local - cut + 1) // 2
    lows = [(a, b) for a, b in ((0, middle), (middle, cut)) if a < b]
    highs = [(a, b) for a, b in ((cut, top), (top, local)) if a < b]
    v["corner_low"], v["corner_high"] = [corner(*ab) for ab in lows], [corner(*ab) for ab in highs]
    gate("corner_low", "corner_high", "out1", "k01", "g0", "out0")
    v["t_low"], v["t_high"] = [], []

    def send_corner(k):
        for ts in v["corner_low"][k : k + 1]:
            v["t_low"].append([[grid.chip(t, -s) for s, t in zip(chips, row)] for row in ts])
        for ts in v["corner_high"][k : k + 1]:
            v["t_high"].append([[grid.line(t, -r) for t in row] for r, row in zip(lines, ts)])

    send_corner(0)
    v["g1"] = [v["out1"][0], *home(v["out1"], 0, 1)]
    v["dw_own"] = expert_grads(pos_dense, [v["k00"], v["k01"]], grid.chips, grid.cores)
    gate("dw_own", "t_low", "t_high", "g1", "out1", "g0", "corner_low", "corner_high")

    send_corner(1)
    v["own_core"] = grid.cores_moved(v["dw_own"])
    v["g1"] += home(v["out1"], 0, 2)
    v["b0"] = backward(0)
    gate("b0", "own_core", "dw_own", "t_low", "t_high", "g1", "dw_other", "other_core", "out0", "out1")

    bounds = [(a, b) for a, b in ((0, cut), (cut, top), (top, local)) if a < b]
    v["to_lines"], v["to_chips"] = [], []
    for i in range(len(lines)):
        v["to_lines"].append([])
        for a, b in bounds:
            total = grid.cores_added(v["dw_other"][i], v["other_core"][i], 0, a, b)
            for k in range(len(chips)) if b <= cut else []:
                total = total + jnp.concatenate([t[i][k] for t in v["t_low"]], axis=0).astype(f32)
            v["to_lines"][i].append(total.astype(bf16))
    for k, s in enumerate(chips):
        v["to_chips"].append([])
        for a, b in bounds:
            total = grid.cores_added(v["dw_own"], v["own_core"], s, a, b)
            for i in range(len(lines)) if a >= cut else []:
                total = total + v["t_high"][highs.index((a, b))][i][k].astype(f32)
            v["to_chips"][k].append(total.astype(bf16))
    v["g1"] += home(v["out1"], 0, 3)
    gate("to_lines", "to_chips", "g1", "out0", "out1")
    v["home_x"], v["home_y"] = [[] for _ in chips], [[] for _ in lines]

    def send_home(a, b):
        for s, ts, held in zip(chips, v["to_chips"], v["home_x"]):
            held += [grid.chip(t, -s) for t in ts[a:b]]
        for r, ts, held in zip(lines, v["to_lines"], v["home_y"]):
            held += [grid.line(t, -r) for t in ts[a:b]]

    send_home(0, 1)
    v["m0"] += home(v["out0"], 4, 2)
    v["m1"] = [v["out1"][4], *home(v["out1"], 4, 1)]
    v["b1"] = backward(1)
    v["dense"] = weight_part(pos_dense, [v["b0"][1], v["b1"][1]], grid.chips, grid.cores, n_exp)
    if not in_kernel(shard // n_exp):
        order = jnp.argsort(jnp.stack(steps))
        v["dense"] = [
            p.reshape(grid.chips, n_exp, shard // n_exp, WIDE)[:, order].reshape(p.shape) for p in v["dense"]
        ]
    gate("dense", "home_x", "home_y", "to_chips", "to_lines", "m0", "m1", "out0", "out1")

    v["dense_core"] = grid.cores_moved(v["dense"])
    send_home(1, 2)
    v["m1"] += home(v["out1"], 4, 3)
    gate("dense_core", "dense", "home_x", "home_y", "to_chips", "to_lines", "m1", "out0", "out1")

    split = WIDE // 2 // 128 * 128
    small = shard // n_exp
    sums = [
        grid.cores_added(v["dense"], v["dense_core"], s).reshape(grid.major, grid.minor, small, WIDE)
        for s in range(grid.chips)
    ]
    v["left"], v["right"] = [x[..., :split].astype(bf16) for x in sums], [x[..., split:].astype(bf16) for x in sums]
    v["left_far"] = [grid.chip(v["left"][s], -s) for s in chips]
    right = jnp.stack(v["right"])
    v["right_far"] = [grid.line(right[:, :, r], -r) for r in lines]
    v["m1"] += home(v["out1"], 4, 2)
    gate("left", "right", "left_far", "right_far", "m1", "to_chips", "to_lines", "out0")

    left = v["left"][0].astype(f32)
    for part in v["left_far"]:
        left = left + part.astype(f32)
    right = jnp.stack(v["right"])[:, :, 0].astype(f32)
    for part in v["right_far"]:
        right = right + part.astype(f32)
    v["left"], v["right"] = left[:, 0], right[0]
    v["left_far"] = [grid.line(left[:, r].astype(bf16), -r) for r in lines]
    v["right_far"] = [grid.chip(right[s].astype(bf16), -s) for s in chips]
    v["m0"] += home(v["out0"], 4, 3)
    gate("left", "right", "left_far", "right_far", "to_chips", "to_lines", "m0")

    left, right = v["left"], v["right"]
    for part in v["left_far"]:
        left = left + part.astype(f32)
    for part in v["right_far"]:
        right = right + part.astype(f32)
    mine = grid.major_home(jnp.concatenate([left, right], axis=-1))
    send_home(2, 3)
    outputs = []
    for i in range(MB):
        total = v["m%d" % i][0]
        for part in v["m%d" % i][1:]:
            total = total + part.astype(f32)
        outputs.append((v["f%d" % i][1] + resid_mult * total).astype(bf16))
    grad_rows = [v["b0"][0], v["b1"][0]]

    total = grid.cores_added(v["dw_own"], v["own_core"], 0)
    for parts in (*v["home_y"], *v["home_x"]):
        total = total + jnp.concatenate(parts, axis=0).astype(f32)
    grad_gate_up, grad_down = total[:, :, : 2 * FFE], total[:, :, 2 * FFE :].transpose(0, 2, 1)

    return (
        jnp.stack(outputs)[:, None],
        jnp.stack(grad_rows)[:, None],
        mine[:, QKV + EXPERTS],
        mine[:, :QD],
        mine[:, QD : QD + KD],
        mine[:, QD + KD : QKV],
        mine[:, WO:].T,
        mine[:, QKV + EXPERTS + 1],
        mine[:, QKV : QKV + EXPERTS],
        grad_gate_up,
        grad_down,
    )


def solution(mesh):
    grid = Grid(mesh.shape["dp"], mesh.shape["expert"])
    in_specs = (
        P(None, ("dp", "expert"), None, None),
        P(None, ("dp", "expert"), None),
        P(None, ("dp", "expert"), None, None),
        P(),
        P("dp", None),
        P("dp", None),
        P("dp", None),
        P(None, "dp"),
        P(),
        P("dp", None),
        P("expert", "dp", None),
        P("expert", None, "dp"),
        P(None, ("dp", "expert"), None, None),
    )
    out_specs = (
        P(None, ("dp", "expert"), None, None),
        P(None, ("dp", "expert"), None, None),
        P(("dp", "expert")),
        P(("dp", "expert"), None),
        P(("dp", "expert"), None),
        P(("dp", "expert"), None),
        P(None, ("dp", "expert")),
        P(("dp", "expert")),
        P(("dp", "expert"), None),
        P("expert", "dp", None),
        P("expert", None, "dp"),
    )
    return jax.shard_map(
        functools.partial(on_device, grid), mesh=mesh, in_specs=in_specs, out_specs=out_specs, check_vma=False
    )
```

```python
import functools

import jax
import jax.numpy as jnp
from jax import lax
from jax.experimental import pallas as pl
from jax.experimental.pallas import tpu as pltpu
from jax.sharding import PartitionSpec as P

D = 1024
QUERY_HEADS = 16
KEY_VALUE_HEADS = 8
HEAD_SIZE = 64
FFE = 512
EXPERTS = 32
TOP = 8
SEG_LEN = 16
BRANCHES = 4
MB = 2
TRUNK = 64
NSEG = 13
TREE_TOKENS = 256
QD = 1024
KD = 512
CAP = 72
CAP_PAD = 80
QKV = QD + 2 * KD
WIDE = QKV + 128 + D
WO = QKV + 128
PAIR = 3 * FFE
EXT = 16
PAY = TREE_TOKENS + EXT

epsilon = 1e-06
attn_mult = 0.015625
resid_mult = 0.22
theta_base = 10000.0
neg_fill = -1e30

f32 = jnp.float32
bf16 = jnp.bfloat16
VMEM_LIMIT = 60 * 1024 * 1024


def dot(a, b, ca=1, cb=0):
    return lax.dot_general(a, b, (((ca,), (cb,)), ((), ())), preferred_element_type=f32)


def lanes(shape):
    return lax.broadcasted_iota(jnp.int32, shape, len(shape) - 1)


def params(**extra):
    return pltpu.CompilerParams(vmem_limit_bytes=VMEM_LIMIT, **extra)


def whole(shape):
    return pl.BlockSpec(shape, lambda *_: (0,) * len(shape))


def cost(flops, size, exps=0):
    return pl.CostEstimate(flops=int(flops), bytes_accessed=int(size), transcendentals=int(exps))


def tree_layout():
    row_index = jnp.arange(TREE_TOKENS, dtype=jnp.int32)
    branch_rest = row_index - TRUNK
    leaf_rest = branch_rest - BRANCHES * SEG_LEN
    in_trunk = row_index < TRUNK
    in_branch = branch_rest < BRANCHES * SEG_LEN
    segment = jnp.where(
        in_trunk,
        0,
        jnp.where(in_branch, 1 + branch_rest // SEG_LEN, 1 + BRANCHES + leaf_rest // SEG_LEN),
    )
    position = jnp.where(
        in_trunk,
        row_index,
        jnp.where(in_branch, TRUNK + branch_rest % SEG_LEN, TRUNK + SEG_LEN + leaf_rest % SEG_LEN),
    )
    return (segment, position)


def rope_tables(position):
    half_width = HEAD_SIZE // 2
    inverse_freq = theta_base ** (-2.0 * jnp.arange(half_width, dtype=f32) / HEAD_SIZE)
    angles = position.astype(f32)[:, None] * inverse_freq[None, :]
    c, s = jnp.cos(angles), jnp.sin(angles)
    return jnp.concatenate([c, c, c, c], axis=1), jnp.concatenate([-s, s, -s, s], axis=1)


def mask_bias(parent_row, segment):
    seg_ids = jnp.arange(NSEG, dtype=jnp.int32)
    parent_hot = (parent_row[:, None] == seg_ids[None, :]).astype(f32)
    ancestor = jnp.eye(NSEG, dtype=f32) + parent_hot + jnp.dot(parent_hot, parent_hot)
    seg_hot = (segment[:, None] == seg_ids[None, :]).astype(f32)
    reach = jnp.dot(jnp.dot(seg_hot, ancestor), seg_hot.T)
    rows = jnp.arange(TREE_TOKENS, dtype=jnp.int32)
    allowed = (reach > 0.5) & (rows[None, :] <= rows[:, None])
    return jnp.where(allowed, 0.0, neg_fill).astype(f32)


def swap_halves(u):
    first = (lanes(u.shape) % HEAD_SIZE) < HEAD_SIZE // 2
    return jnp.where(first, pltpu.roll(u, 96, 1), pltpu.roll(u, 32, 1))


def twice(u, upper):
    low = lanes(u.shape) < HEAD_SIZE
    turned = pltpu.roll(u, HEAD_SIZE, 1)
    return jnp.where(low, turned, u) if upper else jnp.where(low, u, turned)


def split_heads(u):
    low = lanes(u.shape) < HEAD_SIZE
    zero = jnp.zeros_like(u)
    return jnp.concatenate([jnp.where(low, u, zero), jnp.where(low, zero, u)], axis=0)


def softmax_rows(scores, bias):
    s = scores.reshape(2, TREE_TOKENS, TREE_TOKENS) * attn_mult + bias[None]
    e = jnp.exp(s - jnp.max(s, axis=-1, keepdims=True))
    p = e * (1.0 / jnp.sum(e, axis=-1, keepdims=True))
    return p.reshape(2 * TREE_TOKENS, TREE_TOKENS)


def gather_weights(refs, offsets, to, sem, wait):
    for i, ref in enumerate(refs):
        rows = ref.shape[0]
        copy = pltpu.make_async_copy(
            ref, to.at[pl.ds(pl.multiple_of(offsets[i], rows), rows)], sem.at[i]
        )
        if wait:
            copy.wait()
        else:
            copy.start()


def forward_kernel(n_dense, offsets, *refs):
    tokens, bias, cos2, sin2, gain_a, gain_m, routes = refs[:7]
    dense = refs[7 : 7 + n_dense]
    xnp, hidden_out, q_out, k2_out, v2_out, mixed_out, gates_out = refs[7 + n_dense : 14 + n_dense]
    w, sem = refs[14 + n_dense :]
    gather_weights(dense, offsets, w, sem, False)
    x = tokens[...].astype(f32)
    r1 = lax.rsqrt(jnp.mean(x * x, axis=1, keepdims=True) + epsilon)
    xn1 = (x * r1 * gain_a[...]).astype(bf16)
    gather_weights(dense, offsets, w, sem, True)
    qkv = dot(xn1, w[:, :QKV])
    c, s = cos2[...], sin2[...]
    for m in range(KEY_VALUE_HEADS):
        u = qkv[:, 128 * m : 128 * m + 128]
        q_out[:, 128 * m : 128 * m + 128] = (u * c + swap_halves(u) * s).astype(bf16)
    for n in range(KEY_VALUE_HEADS // 2):
        u = qkv[:, QD + 128 * n : QD + 128 * n + 128]
        u = u * c + swap_halves(u) * s
        o = qkv[:, QD + KD + 128 * n : QD + KD + 128 * n + 128]
        for half in range(2):
            at = 128 * (2 * n + half)
            k2_out[:, at : at + 128] = twice(u, half).astype(bf16)
            v2_out[:, at : at + 128] = twice(o, half).astype(bf16)

    def one(m, carry):
        at = pl.ds(pl.multiple_of(m * 128, 128), 128)
        qq = split_heads(q_out[:, at])
        p = softmax_rows(dot(qq, k2_out[:, at], 1, 1), bias[...]).astype(bf16)
        o = dot(p, v2_out[:, at])
        low = lanes((TREE_TOKENS, 128)) < HEAD_SIZE
        mixed_out[:, at] = jnp.where(low, o[:TREE_TOKENS], o[TREE_TOKENS:]).astype(bf16)
        return carry

    lax.fori_loop(0, KEY_VALUE_HEADS, one, 0, unroll=2)
    h = x + resid_mult * dot(mixed_out[...], w[:, WO:], 1, 1)
    hidden_out[...] = h
    r2 = lax.rsqrt(jnp.mean(h * h, axis=1, keepdims=True) + epsilon)
    xn2 = (h * r2 * gain_m[...]).astype(bf16)
    xnp[:TREE_TOKENS] = xn2
    lt = dot(xn2, w[:, QKV:WO]).T[:EXPERTS]
    ids = lax.broadcasted_iota(jnp.int32, (EXPERTS, TREE_TOKENS), 0)
    named = ids == routes[0:1, :]
    for k in range(1, TOP):
        named = named | (ids == routes[k : k + 1, :])
    lt = jnp.where(named, lt, neg_fill)
    e = jnp.where(named, jnp.exp(lt - jnp.max(lt, axis=0, keepdims=True)), 0.0)
    g = e / jnp.sum(e, axis=0, keepdims=True)
    gates_out[...] = g
    packed = pack_rows(g)
    hi = packed.astype(bf16)
    low_part = (packed - hi.astype(f32)).astype(bf16)
    xnp[TREE_TOKENS:] = jnp.concatenate([hi.astype(f32), low_part.astype(f32)], axis=0).astype(bf16)


def pack_rows(g):
    return jnp.concatenate([g[8 * i : 8 * i + 8] for i in range(4)], axis=1)


def unpack_rows(g):
    return jnp.concatenate([g[:, 256 * i : 256 * i + 256] for i in range(4)], axis=0)


def any_space(n):
    return [pl.BlockSpec(memory_space=pl.ANY)] * n


def forward_part(offsets, tokens, bias, tables, gain_a, gain_m, routes, dense):
    t = TREE_TOKENS
    ins = [tokens, bias, *tables, gain_a, gain_m, routes]
    outs = [((PAY, D), bf16), ((t, D), f32)] + [((t, QD), bf16)] * 4 + [((EXPERTS, t), f32)]
    return pl.pallas_call(
        functools.partial(forward_kernel, len(dense)),
        grid_spec=pltpu.PrefetchScalarGridSpec(
            num_scalar_prefetch=1,
            grid=(1,),
            in_specs=[whole(a.shape) for a in ins] + any_space(len(dense)),
            out_specs=[whole(s) for s, _ in outs],
            scratch_shapes=[pltpu.VMEM((D, WIDE), bf16), pltpu.SemaphoreType.DMA((len(dense),))],
        ),
        out_shape=[jax.ShapeDtypeStruct(s, d) for s, d in outs],
        compiler_params=params(),
        cost_estimate=cost(1, 1),
        name="attention_forward",
    )(offsets, *ins, *dense)


def expert_kernel(layout, local, n_before, last, pos, *refs):
    refs = list(refs)

    def take(n):
        out = refs[:n]
        del refs[:n]
        return out

    n_dp = len(layout)
    rows_in, cots_in = take(5), take(5)
    weights = [take(len(sizes)) for sizes in layout]
    before_in = [take(3) for _ in range(n_before)]
    outs = take(8) if last else take(3)
    sent_out, hid_out, gboth_out, geo_out = take(4)
    rank_s, gate_s, x1_s, x3_s, c1_s, c3_s, w_s, w_sem = take(8)
    sel_s, comb_s, gg_s = take(3) if last else outs
    e = pl.program_id(0)
    shard = D // n_dp
    base = pos[n_dp] * local
    at_start, at_end = pos[n_dp + 1] == 0, pos[n_dp + 1] == 3
    t = TREE_TOKENS
    ids = lax.broadcasted_iota(jnp.int32, (EXPERTS, t), 0)
    xs = [rows_in[0], x1_s, rows_in[2], x3_s]
    cots = [cots_in[0], c1_s, cots_in[2], c3_s]

    def load(expert, slot):
        for p, (parts, sizes) in enumerate(zip(weights, layout)):
            to = w_s.at[slot, pl.ds(pl.multiple_of(pos[p] * shard, shard), shard)]
            offset = 0
            for part, size in zip(parts, sizes):
                if len(sizes) == 1:
                    pltpu.make_async_copy(part.at[expert], to, w_sem.at[slot, p]).start()
                else:

                    @pl.when((expert >= offset) & (expert < offset + size))
                    def _():
                        pltpu.make_async_copy(part.at[expert - offset], to, w_sem.at[slot, p]).start()

                offset += size

    def arrive(slot):
        for p in range(n_dp):
            to = w_s.at[slot, pl.ds(pl.multiple_of(pos[p] * shard, shard), shard)]
            pltpu.make_async_copy(weights[p][0].at[0], to, w_sem.at[slot, p]).wait()

    slot_now = e % 2

    @pl.when(e == 0)
    def _():
        load(0, 0)

    @pl.when(e + 1 < local)
    def _():
        load(e + 1, 1 - slot_now)

    @pl.when(e == 0)
    def _():
        for given, lower, upper in ((rows_in, x1_s, x3_s), (cots_in, c1_s, c3_s)):
            lower[...] = jnp.where(at_start, given[4][...], given[1][...])
            upper[...] = jnp.where(at_end, given[4][...], given[3][...])
        gates = []
        for b in range(4):
            ext = xs[b][t:].astype(f32)
            full = unpack_rows(ext[:8] + ext[8:16])
            gates.append(
                [
                    jnp.sum(jnp.where(ids == base + el, full, 0.0), axis=0, keepdims=True)
                    for el in range(local)
                ]
            )
        before = lax.broadcasted_iota(jnp.int32, (t, t), 0) < lax.broadcasted_iota(jnp.int32, (t, t), 1)
        before = before.astype(f32).astype(bf16)
        for el in range(local):
            gate = jnp.concatenate([gates[b][el] for b in range(4)] + [jnp.zeros((4, t), f32)], axis=0)
            used = gate > 0.0
            rank = dot(used.astype(f32).astype(bf16), before)
            gate_s[el] = gate
            rank_s[el] = jnp.where(used, rank, -1.0)
        sel_s[...] = jnp.zeros_like(sel_s)
        comb_s[...] = jnp.zeros_like(comb_s)

    gate, rank = gate_s[e], rank_s[e]
    slot = lax.broadcasted_iota(jnp.int32, (CAP, t), 0).astype(f32)
    sels, sent, cot, gate_slot = [], [], [], []
    for b in range(4):
        hit = slot == rank[b : b + 1]
        sel = jnp.where(hit, 1.0, 0.0)
        sels.append(sel)
        low = sel.astype(bf16)
        sent.append(dot(low, xs[b][:t]))
        cot.append(dot(low, cots[b][:t]))
        gate_slot.append(jnp.sum(jnp.where(hit, gate[b : b + 1], 0.0), axis=1, keepdims=True))
    sent_out[0] = jnp.concatenate(sent, axis=0).astype(bf16)
    gm = jnp.concatenate(cot, axis=0) * resid_mult
    gate_slot = jnp.concatenate(gate_slot, axis=0)
    geo_out[0] = (gm * gate_slot).astype(bf16)
    arrive(slot_now)
    both = dot(sent_out[0], w_s[slot_now, :, : 2 * FFE])
    gh, up = both[:, :FFE], both[:, FFE:]
    sigma = 1.0 / (1.0 + jnp.exp(-gh))
    hid_out[0] = (gh * sigma * up).astype(bf16)
    eo = dot(hid_out[0], w_s[slot_now, :, 2 * FFE :], 1, 1).astype(bf16).astype(f32)
    gs = dot(geo_out[0], w_s[slot_now, :, 2 * FFE :]) * sigma
    gboth_out[0] = jnp.concatenate(
        [(gs * up * (1.0 + gh * (1.0 - sigma))).astype(bf16), (gs * gh).astype(bf16)], axis=1
    )
    grad_sent = dot(gboth_out[0], w_s[slot_now, :, : 2 * FFE], 1, 1)
    gg = jnp.sum(gm * eo, axis=1, keepdims=True)
    weighted = gate_slot * eo
    ggs = []
    for b in range(4):
        part = slice(CAP * b, CAP * b + CAP)
        where = pl.ds(pl.multiple_of(e * CAP_PAD, 16), CAP)
        sel_s[b, where] = sels[b].astype(bf16)
        comb_s[b, where, :D] = grad_sent[part].astype(bf16)
        comb_s[b, where, D:] = weighted[part].astype(bf16)
        ggs.append(jnp.sum(sels[b] * gg[part], axis=0, keepdims=True))
    gg_s[e] = jnp.concatenate(ggs + [jnp.zeros((4, t), f32)], axis=0)

    if not last:
        return

    @pl.when(e == local - 1)
    def _():
        for b in range(4):
            total = dot(sel_s[b], comb_s[b], 0, 0)
            full = jnp.zeros((EXPERTS, t), f32)
            for el in range(local):
                full = full + jnp.where(ids == base + el, gg_s[el, b : b + 1], 0.0)
            for i, (sel_b, comb_b, gg_b) in enumerate(before_in):
                total = total + dot(sel_b[b], comb_b[b], 0, 0)
                owner = pos[n_dp + 2 + i] * local
                for el in range(local):
                    full = full + jnp.where(ids == owner + el, gg_b[el, b : b + 1], 0.0)
            outs[b][:t] = total[:, :D].astype(outs[b].dtype)
            outs[4 + b][...] = total[:, D:].astype(outs[4 + b].dtype)
            packed = pack_rows(full)
            hi = packed.astype(bf16)
            rest = (packed - hi.astype(f32)).astype(bf16)
            ext = jnp.concatenate([hi.astype(f32), rest.astype(f32)], axis=0)
            outs[b][t:] = ext.astype(outs[b].dtype)


def expert_part(pos, rows, cots, weights, before, last):
    n_dp = len(weights)
    local = sum(part.shape[0] for part in weights[0])
    t = TREE_TOKENS
    m = CAP * 4
    layout = tuple(tuple(part.shape[0] for part in parts) for parts in weights)
    flat = [part for parts in weights for part in parts]
    earlier = [a for one in before for a in one]
    ins = [*rows, *cots, *flat, *earlier]
    in_specs = [whole(a.shape) for a in (*rows, *cots)]
    in_specs += [pl.BlockSpec(memory_space=pl.ANY)] * len(flat)
    in_specs += [whole(a.shape) for a in earlier]
    passed = [
        ((4, local * CAP_PAD, t), bf16),
        ((4, local * CAP_PAD, 2 * D), bf16),
        ((local, 8, t), f32),
    ]
    if last:
        kinds = [f32, bf16, bf16, bf16]
        outs = [((PAY, D), k) for k in kinds] + [((t, D), k) for k in kinds]
    else:
        outs = list(passed)
    n_main = len(outs)
    out_specs = [whole(s) for s, _ in outs]
    kept = [D, FFE, 2 * FFE, D]
    outs = outs + [((local, m, w), bf16) for w in kept]
    out_specs = out_specs + [pl.BlockSpec((1, m, w), lambda e, *_: (e, 0, 0)) for w in kept]
    scratch = [
        pltpu.VMEM((local, 8, t), f32),
        pltpu.VMEM((local, 8, t), f32),
        pltpu.VMEM((PAY, D), bf16),
        pltpu.VMEM((PAY, D), bf16),
        pltpu.VMEM(cots[0].shape, bf16),
        pltpu.VMEM(cots[0].shape, bf16),
        pltpu.VMEM((2, D, PAIR), bf16),
        pltpu.SemaphoreType.DMA((2, n_dp)),
    ]
    if last:
        scratch += [pltpu.VMEM(s, d) for s, d in passed]
    res = pl.pallas_call(
        functools.partial(expert_kernel, layout, local, len(before), last),
        grid_spec=pltpu.PrefetchScalarGridSpec(
            num_scalar_prefetch=1,
            grid=(local,),
            in_specs=in_specs,
            out_specs=out_specs,
            scratch_shapes=scratch,
        ),
        out_shape=[jax.ShapeDtypeStruct(s, d) for s, d in outs],
        compiler_params=params(),
        cost_estimate=cost(1, 1),
        name="experts",
    )(pos, *ins)
    return res[:n_main], res[n_main:]


def expert_grad_kernel(n_dp, n_kept, pos, *refs):
    kept = [refs[4 * i : 4 * i + 4] for i in range(n_kept)]
    outs = refs[4 * n_kept :]
    shard = D // n_dp
    for p in range(n_dp):
        at = pl.ds(pl.multiple_of(pos[p] * shard, shard), shard)
        gate_up, down = None, None
        for sent, hid, gboth, geo in kept:
            part = dot(sent[0, :, at], gboth[0], 0, 0)
            gate_up = part if gate_up is None else gate_up + part
            part = dot(geo[0, :, at], hid[0], 0, 0)
            down = part if down is None else down + part
        out = outs[p % len(outs)]
        out[p // len(outs), 0, :, : 2 * FFE] = gate_up.astype(out.dtype)
        out[p // len(outs), 0, :, 2 * FFE :] = down.astype(out.dtype)


def expert_grads(pos, kept, chips, cores):
    local, m, _ = kept[0][0].shape
    n_dp = chips * cores
    shard = D // n_dp
    flat = [a for one in kept for a in one]
    shape = (chips, local, shard, PAIR)
    return pl.pallas_call(
        functools.partial(expert_grad_kernel, n_dp, len(kept)),
        grid_spec=pltpu.PrefetchScalarGridSpec(
            num_scalar_prefetch=1,
            grid=(local,),
            in_specs=[pl.BlockSpec((1, *a.shape[1:]), lambda e, *_: (e, 0, 0)) for a in flat],
            out_specs=[pl.BlockSpec((chips, 1, shard, PAIR), lambda e, *_: (0, e, 0, 0))] * cores,
        ),
        out_shape=[jax.ShapeDtypeStruct(shape, bf16)] * cores,
        compiler_params=params(),
        cost_estimate=cost(1, 1),
        name="expert_grads",
    )(pos, *flat)


def home_kernel(sides, bounds, *refs):
    refs = list(refs)
    e = pl.program_id(0)
    work = []
    for groups in sides:
        work.append([[(refs.pop(0), at) for _, _, at in group] for group in groups])
    for (groups, held) in zip(sides, work):
        outs = [refs.pop(0) for _ in bounds]
        whole_groups, part_groups = [], []
        for group, here in zip(groups, held):
            first, stop = group[0][2], group[-1][2] + group[-1][0].shape[-3]
            (whole_groups if (first, stop) == (0, bounds[-1][1]) else part_groups).append((first, stop, here))
        shape = outs[0].shape

        def value(here):
            total = None
            for ref, at in here:
                one = ref[...].reshape(shape).astype(f32)
                total = one if total is None else jnp.where(e >= at, one, total)
            return total

        base = None
        for _, _, here in whole_groups:
            base = value(here) if base is None else base + value(here)
        for (a, b), out in zip(bounds, outs):

            @pl.when((e >= a) & (e < b))
            def _(a=a, b=b, out=out):
                total = base
                for first, stop, here in part_groups:
                    if first <= a and b <= stop:
                        total = total + value(here)
                out[...] = total.astype(out.dtype)


def home_sums(sides, bounds):
    ins, specs = [], []
    for groups in sides:
        for group in groups:
            for array, chip, first in group:

                def at(e, chip=chip, first=first, size=array.shape[-3]):
                    place = jnp.clip(e - first, 0, size - 1)
                    return (place, 0, 0) if chip is None else (chip, place, 0, 0)

                ins.append(array)
                specs.append(pl.BlockSpec((1,) * (array.ndim - 2) + array.shape[-2:], at))
    tail = ins[0].shape[-2:]
    shapes = [(b - a, *tail) for _ in sides for a, b in bounds]

    def out_at(e, a=0, n=1):
        return (jnp.clip(e - a, 0, n - 1), 0, 0)

    out_specs = [
        pl.BlockSpec((1, *tail), functools.partial(out_at, a=a, n=b - a)) for _ in sides for a, b in bounds
    ]
    res = pl.pallas_call(
        functools.partial(home_kernel, sides_layout(sides), bounds),
        grid=(bounds[-1][1],),
        in_specs=specs,
        out_specs=out_specs,
        out_shape=[jax.ShapeDtypeStruct(shape, bf16) for shape in shapes],
        compiler_params=params(),
        cost_estimate=cost(1, 1),
        name="home_sums",
    )(*ins)
    n = len(bounds)
    return [res[n * i : n * i + n] for i in range(len(sides))]


def sides_layout(sides):
    return [
        [[(jax.ShapeDtypeStruct(a.shape, a.dtype), c, at) for a, c, at in group] for group in groups] for groups in sides
    ]


def backward_kernel(n_dense, n_grads, offsets, *refs):
    grads = refs[:n_grads]
    tokens, hidden, cot, gates, q, k2, v2, bias, cos2, sin2, gain_a, gain_m = refs[n_grads : n_grads + 12]
    dense = refs[n_grads + 12 : n_grads + 12 + n_dense]
    rest = refs[n_grads + 12 + n_dense :]
    grad_tokens, xn1_out, gqkv_out, gbr_out, xn2_out, gl_out, gains_out = rest[:7]
    gmix, w, sem = rest[7:]
    t = TREE_TOKENS
    gather_weights(dense, offsets, w, sem, False)
    total = grads[0][...].astype(f32)
    for other in grads[1:]:
        total = total + other[...].astype(f32)
    gg = unpack_rows(total[t : t + 8] + total[t + 8 : t + 16])
    g = gates[...]
    gl = g * (gg - jnp.sum(g * gg, axis=0, keepdims=True))
    gl = jnp.concatenate([gl, jnp.zeros((128 - EXPERTS, t), f32)], axis=0).T.astype(bf16)
    gl_out[...] = gl
    gather_weights(dense, offsets, w, sem, True)
    gx2 = total[:t] + dot(gl, w[:, QKV:WO], 1, 1)
    h = hidden[...]
    r2 = lax.rsqrt(jnp.mean(h * h, axis=1, keepdims=True) + epsilon)
    xn2_out[...] = (h * r2 * gain_m[...]).astype(bf16)
    u2 = gx2 * gain_m[...]
    ghs = cot[...].astype(f32) + r2 * u2 - h * (r2 * r2 * r2) * jnp.mean(u2 * h, axis=1, keepdims=True)
    gain2 = jnp.sum(gx2 * h * r2, axis=0, keepdims=True)
    gbr_out[...] = (resid_mult * ghs).astype(bf16)
    gmix[...] = dot(gbr_out[...], w[:, WO:]).astype(bf16)
    low = lanes((t, 128)) < HEAD_SIZE
    c, s = cos2[...], sin2[...]

    def unrotate(w):
        return w * c + swap_halves(w * s)

    def one(n, carry):
        keys, values = [], []
        for half in range(2):
            at = pl.ds(pl.multiple_of(n * 256 + 128 * half, 128), 128)
            qq = split_heads(q[:, at])
            dd = split_heads(gmix[:, at])
            kk = k2[:, at]
            pf = softmax_rows(dot(qq, kk, 1, 1), bias[...])
            gp = dot(dd, v2[:, at], 1, 1)
            gsc = (pf * (gp - jnp.sum(pf * gp, axis=1, keepdims=True))).astype(bf16)
            gq = dot(gsc, kk)
            gq = attn_mult * jnp.where(low, gq[:t], gq[t:])
            gqkv_out[:, at] = unrotate(gq).astype(bf16)
            gk = attn_mult * dot(gsc, qq, 0, 0)
            keys.append(gk + pltpu.roll(gk, HEAD_SIZE, 1))
            gv = dot(pf.astype(bf16), dd, 0, 0)
            values.append(gv + pltpu.roll(gv, HEAD_SIZE, 1))
        at = pl.ds(pl.multiple_of(QD + n * 128, 128), 128)
        gqkv_out[:, at] = unrotate(jnp.where(low, keys[0], keys[1])).astype(bf16)
        at = pl.ds(pl.multiple_of(QD + KD + n * 128, 128), 128)
        gqkv_out[:, at] = jnp.where(low, values[0], values[1]).astype(bf16)
        return carry

    lax.fori_loop(0, KEY_VALUE_HEADS // 2, one, 0)
    gx1 = dot(gqkv_out[...], w[:, :QKV], 1, 1)
    x = tokens[...].astype(f32)
    r1 = lax.rsqrt(jnp.mean(x * x, axis=1, keepdims=True) + epsilon)
    xn1_out[...] = (x * r1 * gain_a[...]).astype(bf16)
    u1 = gx1 * gain_a[...]
    grad_tokens[...] = ghs + r1 * u1 - x * (r1 * r1 * r1) * jnp.mean(u1 * x, axis=1, keepdims=True)
    gain1 = jnp.sum(gx1 * x * r1, axis=0, keepdims=True)
    gains_out[...] = jnp.concatenate([gain1, gain2, jnp.zeros((6, D), f32)], axis=0)


def backward_part(offsets, grads, tokens, hidden, cot, gates, q, k2, v2, bias, tables, gain_a, gain_m, dense):
    t = TREE_TOKENS
    ins = [*grads, tokens, hidden, cot, gates, q, k2, v2, bias, *tables, gain_a, gain_m]
    outs = [
        ((t, D), f32),
        ((t, D), bf16),
        ((t, QKV), bf16),
        ((t, D), bf16),
        ((t, D), bf16),
        ((t, 128), bf16),
        ((8, D), f32),
    ]
    return pl.pallas_call(
        functools.partial(backward_kernel, len(dense), len(grads)),
        grid_spec=pltpu.PrefetchScalarGridSpec(
            num_scalar_prefetch=1,
            grid=(1,),
            in_specs=[whole(a.shape) for a in ins] + any_space(len(dense)),
            out_specs=[whole(s) for s, _ in outs],
            scratch_shapes=[
                pltpu.VMEM((t, D), bf16),
                pltpu.VMEM((D, WIDE), bf16),
                pltpu.SemaphoreType.DMA((len(dense),)),
            ],
        ),
        out_shape=[jax.ShapeDtypeStruct(s, d) for s, d in outs],
        compiler_params=params(),
        cost_estimate=cost(1, 1),
        name="attention_backward",
    )(offsets, *ins, *dense)


def in_kernel(rows):
    return rows % 16 == 0


def weight_kernel(n_dp, n_exp, pos, *refs):
    per = 7
    sets = [refs[per * i : per * i + per] for i in range(MB)]
    outs = refs[per * MB :]
    cores = len(outs)
    shard, small = D // n_dp, D // n_dp // n_exp
    for p in range(n_dp):
        at = pl.ds(pl.multiple_of(pos[p] * shard, shard), shard)

        def product(left, right):
            total = None
            for one in sets:
                part = dot(one[left][:, at], one[right][...], 0, 0)
                total = part if total is None else total + part
            return total

        gains = sets[0][6][:, at]
        for one in sets[1:]:
            gains = gains + one[6][:, at]
        gains = jnp.concatenate(
            [jnp.zeros((EXPERTS, shard), f32), gains, jnp.zeros((120 - EXPERTS, shard), f32)], axis=0
        )
        blocks = [product(0, 1), product(4, 5) + gains.T, product(2, 3)]
        pieces = n_exp if in_kernel(small) else 1
        size = shard // pieces
        for i in range(pieces):
            rows = slice(size * i, size * i + size)
            to = pl.ds(pl.multiple_of(pos[n_dp + i] * size, size), size) if pieces > 1 else slice(None)
            offset = 0
            for value in blocks:
                width = value.shape[1]
                outs[p % cores][p // cores, to, offset : offset + width] = value[rows].astype(bf16)
                offset += width


def weight_part(pos, sets, chips, cores, n_exp):
    flat = [a for one in sets for a in one]
    n_dp = chips * cores
    shape = (chips, D // n_dp, WIDE)
    return pl.pallas_call(
        functools.partial(weight_kernel, n_dp, n_exp),
        grid_spec=pltpu.PrefetchScalarGridSpec(
            num_scalar_prefetch=1,
            grid=(1,),
            in_specs=[whole(a.shape) for a in flat],
            out_specs=[whole(shape)] * cores,
        ),
        out_shape=[jax.ShapeDtypeStruct(shape, bf16)] * cores,
        compiler_params=params(),
        cost_estimate=cost(1, 1),
        name="dense_grads",
    )(pos, *flat)


class Grid:
    def __init__(self, n_dp, n_exp):
        self.n_dp, self.n_exp = n_dp, n_exp
        self.cores = 2 if n_dp % 2 == 0 else 1
        self.chips = n_dp // self.cores
        self.major = 4
        self.minor = n_exp // self.major

    def move(self, x, axis, to):
        major, minor = (self.chips, self.cores) if axis == "dp" else (self.major, self.minor)
        pairs = []
        for i in range(major * minor):
            target = to(*divmod(i, minor))
            if target is not None:
                pairs.append((i, target[0] * minor + target[1]))
        return lax.ppermute(x, axis, pairs)

    def chip(self, x, s):
        return self.move(x, "dp", lambda a, b: ((a + s) % self.chips, b))

    def core(self, x, s):
        return self.move(x, "dp", lambda a, b: (a, (b + s) % self.cores))

    def line(self, x, s):
        return self.move(x, "expert", lambda a, b: (a, (b + s) % self.minor))

    def up(self, x, s):
        return self.move(x, "expert", lambda a, b: ((a + s) % 4, b))

    def next_up(self, x):
        return self.move(x, "expert", lambda a, b: (a + 1, b) if a < 3 else None)

    def next_down(self, x):
        return self.move(x, "expert", lambda a, b: (a - 1, b) if a > 0 else None)

    def outward(self, x):
        return self.move(x, "expert", lambda a, b: {1: (0, b), 2: (3, b)}.get(a))

    def back(self, parts):
        return [self.up(x, -k) for k, x in enumerate(parts, 1)]

    def dp_places(self):
        i = lax.axis_index("dp")
        a, b = i // self.cores, i % self.cores
        return [
            (a - s) % self.chips * self.cores + (b - c) % self.cores
            for s in range(self.chips)
            for c in range(self.cores)
        ]

    def exp_steps(self):
        i = lax.axis_index("expert")
        a, b = i // self.minor, i % self.minor
        return [
            (a - k // self.minor) % self.major * self.minor + (b - k % self.minor) % self.minor
            for k in range(self.n_exp)
        ]

    def cores_moved(self, groups):
        return [self.core(g, -c) for c, g in enumerate(groups) if c]

    def cores_added(self, groups, moved, s, a=None, b=None):
        total = groups[0][s, a:b].astype(f32)
        for part in moved:
            total = total + part[s, a:b].astype(f32)
        return total

    def major_home(self, blocks):
        total = blocks[0]
        for s in range(1, self.major):
            total = total + self.up(blocks[s].astype(bf16), -s).astype(f32)
        return total


def on_device(
    grid,
    tokens,
    parents,
    routes,
    gain_attn,
    w_query,
    key_matrix,
    value_matrix,
    w_out,
    gain_moe,
    router,
    expert_gate_up,
    expert_down,
    cotangent,
):
    n_dp, n_exp = grid.n_dp, grid.n_exp
    shard = D // n_dp
    places = grid.dp_places()
    me = lax.axis_index("expert")
    major, minor = me // grid.minor, me % grid.minor
    steps = grid.exp_steps()
    owners = [major * grid.minor + (minor - r) % grid.minor for r in range(grid.minor)]

    def pos(i, r):
        before = owners[:r] if i == 0 else (owners[1:r] if r else owners[1:])
        return jnp.stack([*places, owners[r], major, *before, jnp.int32(0)]).astype(jnp.int32)

    pos_dense = jnp.stack([*places, *steps]).astype(jnp.int32)
    chips, lines, cores = range(1, grid.chips), range(1, grid.minor), range(grid.cores)
    local = expert_gate_up.shape[0]
    cut = local - local // 2
    v = {}

    def gate(*names):
        flat, tree = jax.tree.flatten([v[name] for name in names])
        v.update(zip(names, jax.tree.unflatten(tree, lax.optimization_barrier(flat))))

    segment, position = tree_layout()
    tables = rope_tables(position)
    gain_a, gain_m = gain_attn.reshape(1, D), gain_moe.reshape(1, D)
    biases = [mask_bias(parents[i, 0], segment) for i in range(MB)]
    for i in range(MB):
        v["tok%d" % i], v["cot%d" % i] = tokens[i, 0], cotangent[i, 0]

    def pairs(a, b):
        if a == b:
            return []
        return [jnp.concatenate([expert_gate_up[a:b], expert_down[a:b].transpose(0, 2, 1)], axis=2)]

    def over_cores(arrays):
        return [[grid.core(x, c) for x in arrays] for c in cores[1:]]

    def joined(*parts):
        return [sum(held, []) for held in zip(*parts)]

    packed = jnp.concatenate(
        [w_query, key_matrix, value_matrix, router, jnp.zeros((shard, 128 - EXPERTS), bf16), w_out.T], axis=1
    )
    half = local // 2
    quarter = half // 2
    v["far"] = [grid.chip(packed, s) for s in chips]
    v["packed"] = packed
    v["wy"] = [[grid.line(w, r) for w in pairs(0, half)] for r in lines]
    v["c0a"], v["c0b"], v["c0c"] = grid.next_up(v["cot0"]), grid.up(v["cot0"], 2), grid.next_down(v["cot0"])
    v["pair"] = pairs(0, local)
    v["xa"], v["xb"], v["xc"] = pairs(0, quarter), pairs(half, local), pairs(quarter, half)
    gate("far", "packed", "wy", "c0a", "c0b", "c0c", "pair", "xa", "xb", "xc")

    v["far_core"] = [[grid.core(f, c) for c in cores[1:]] for f in v["far"]]
    v["packed_core"] = [grid.core(v["packed"], c) for c in cores[1:]]
    gate("far_core", "packed_core", "tok0", "pair", "xa", "xb", "xc", "cot1", "c0b", "wy")

    dense = [packed, *v["packed_core"]]
    for f, fs in zip(v["far"], v["far_core"]):
        dense += [f, *fs]
    offsets = (jnp.stack(places) * shard).astype(jnp.int32)

    def forward(i):
        return forward_part(
            offsets, v["tok%d" % i], biases[i], tables, gain_a, gain_m, routes[i, 0].T, dense
        )

    v["f0"] = forward(0)
    v["wxa"] = [[grid.chip(w, s) for w in v["xa"]] for s in chips]
    v["pair_core"] = over_cores(v["pair"])
    v["c0d"], v["c1b"] = grid.outward(v["c0b"]), grid.up(v["cot1"], 2)
    gate("f0", "wxa", "pair_core", "c0d", "c1b", "tok1", "xb", "xc", "wy")

    row = v["f0"][0]
    v["n0a"], v["n0b"], v["n0c"] = grid.next_up(row), grid.up(row, 2), grid.next_down(row)
    v["wxb"] = [[grid.chip(w, s) for w in v["xb"]] for s in chips]
    v["wyb"] = [[grid.line(w, r) for w in v["xb"]] for r in lines]
    v["f1"] = forward(1)
    gate("n0a", "n0b", "n0c", "wxb", "wyb", "f1", "cot1", "xc", "wy")

    v["wxc"] = [[grid.chip(w, s) for w in v["xc"]] for s in chips]
    v["wxa_core"] = [over_cores(ws) for ws in v["wxa"]]
    v["wxb_core"] = [over_cores(ws) for ws in v["wxb"]]
    v["n0d"] = grid.outward(v["n0b"])
    v["wy_core"] = [over_cores(ws) for ws in v["wy"]]
    gate("wxc", "wxa_core", "wxb_core", "wy_core", "n0d", "f1", "cot1", "wy", "wxb", "wyb")

    v["wxc_core"] = [over_cores(ws) for ws in v["wxc"]]
    v["wyb_core"] = [over_cores(ws) for ws in v["wyb"]]
    gate("wxc_core", "wyb_core", "f1", "cot1", "wy", "wxb")

    own = [tuple(v["pair"]), *[tuple(w) for w in v["pair_core"]]]
    for k in range(len(chips)):
        own.append((*v["wxa"][k], *v["wxc"][k], *v["wxb"][k]))
        own += [tuple(ws) for ws in joined(v["wxa_core"][k], v["wxc_core"][k], v["wxb_core"][k])]

    def experts(i, r, weights, before):
        name = "%d" % i
        rows = [v["f" + name][0], *[v["n" + name + k] for k in "abcd"]]
        cots = [v["cot" + name], *[v["c" + name + k] for k in "abcd"]]
        return expert_part(pos(i, r), rows, cots, weights, before, len(before) == grid.minor - 1)

    v["e00"], v["k00"] = experts(0, 0, own, [])
    row = v["f1"][0]
    v["n1a"], v["n1b"], v["n1c"] = grid.next_up(row), grid.up(row, 2), grid.next_down(row)
    v["low"] = [[[grid.chip(w, s) for w in ws] for s in chips] for ws in v["wy"]]
    v["high"] = [[[grid.line(w, r) for w in ws] for ws in v["wxb"]] for r in lines]
    gate("e00", "low", "high", "n1a", "n1b", "n1c", "f1", "cot1", "c1b", "wy", "wyb")

    v["low_core"] = [[over_cores(w) for w in ws] for ws in v["low"]]
    v["high_core"] = [[over_cores(w) for w in ws] for ws in v["high"]]
    gate("low_core", "high_core", "f1", "n1b", "e00", "cot1", "c1b")

    sets = [own]
    for i in range(len(lines)):
        parts = [(*v["wy"][i], *v["wyb"][i])]
        parts += [tuple(ws) for ws in joined(v["wy_core"][i], v["wyb_core"][i])]
        for k in range(len(chips)):
            parts.append((*v["low"][i][k], *v["high"][i][k]))
            parts += [tuple(ws) for ws in joined(v["low_core"][i][k], v["high_core"][i][k])]
        sets.append(parts)
    v["n1d"] = grid.outward(v["n1b"])
    v["c1d"] = grid.outward(v["c1b"])
    v["c1a"], v["c1c"] = grid.next_up(v["cot1"]), grid.next_down(v["cot1"])
    passed = [v["e00"]]
    for r in lines:
        out, v["k%d0" % r] = experts(0, r, sets[r], passed)
        passed.append(out)
    v["out0"] = passed[-1]
    gate("out0", "c1a", "c1c", "c1d", "n1d", "f1")

    def home(out, first, *steps):
        return [grid.up(out[first + k], -k) for k in steps]

    v["g0"] = [v["out0"][0], *home(v["out0"], 0, 1, 2)]
    passed = []
    for r in lines:
        out, v["k%d1" % r] = experts(1, r, sets[r], passed)
        passed.append(out)
    v["e1"] = passed
    v["dw_other"] = [
        expert_grads(pos_dense, [v["k%d0" % r], v["k%d1" % r]], grid.chips, grid.cores) for r in lines
    ]
    gate("dw_other", "e1", "g0", "out0")

    v["other_core"] = [grid.cores_moved(groups) for groups in v["dw_other"]]
    v["g0"] += home(v["out0"], 0, 3)
    v["m0"] = [v["out0"][4], *home(v["out0"], 4, 1)]
    v["out1"], v["k01"] = experts(1, 0, own, v["e1"])
    gate("out1", "k01", "other_core", "g0", "m0", "dw_other", "out0")

    def backward(i):
        _, hidden, q, k2, v2, mixed, gates = v["f%d" % i]
        grad_tokens, xn1, gqkv, gbr, xn2, gl, gains = backward_part(
            offsets, v["g%d" % i], tokens[i, 0], hidden, cotangent[i, 0], gates, q, k2, v2,
            biases[i], tables, gain_a, gain_m, dense,
        )
        return grad_tokens, (xn1, gqkv, gbr, mixed, xn2, gl, gains)

    def corner(a, b):
        return [
            [grid.cores_added(g, m, s, a, b).astype(bf16) for s in chips]
            for g, m in zip(v["dw_other"], v["other_core"])
        ]

    middle, top = (cut + 1) // 2, cut + (local - cut + 1) // 2
    lows = [(a, b) for a, b in ((0, middle), (middle, cut)) if a < b]
    highs = [(a, b) for a, b in ((cut, top), (top, local)) if a < b]
    v["corner_low"], v["corner_high"] = [corner(*ab) for ab in lows], [corner(*ab) for ab in highs]
    gate("corner_low", "corner_high", "out1", "k01", "g0", "out0")
    v["t_low"], v["t_high"] = [], []

    def send_corner(k):
        for ts in v["corner_low"][k : k + 1]:
            v["t_low"].append([[grid.chip(t, -s) for s, t in zip(chips, row)] for row in ts])
        for ts in v["corner_high"][k : k + 1]:
            v["t_high"].append([[grid.line(t, -r) for t in row] for r, row in zip(lines, ts)])

    send_corner(0)
    v["g1"] = [v["out1"][0], *home(v["out1"], 0, 1)]
    v["dw_own"] = expert_grads(pos_dense, [v["k00"], v["k01"]], grid.chips, grid.cores)
    gate("dw_own", "t_low", "t_high", "g1", "out1", "g0", "corner_low", "corner_high")

    send_corner(1)
    v["own_core"] = grid.cores_moved(v["dw_own"])
    v["g1"] += home(v["out1"], 0, 2)
    v["b0"] = backward(0)
    gate("b0", "own_core", "dw_own", "t_low", "t_high", "g1", "dw_other", "other_core", "out0", "out1")

    bounds = [(a, b) for a, b in ((0, cut), (cut, top), (top, local)) if a < b]
    sides = []
    for i in range(len(lines)):
        groups = [[(v["dw_other"][i][0], 0, 0)]] + [[(m, 0, 0)] for m in v["other_core"][i]]
        groups += [[(t[i][k], None, a) for t, (a, _) in zip(v["t_low"], lows)] for k in range(len(chips))]
        sides.append(groups)
    for k, s in enumerate(chips):
        groups = [[(v["dw_own"][0], s, 0)]] + [[(m, s, 0)] for m in v["own_core"]]
        if highs:
            groups += [[(t[i][k], None, a) for t, (a, _) in zip(v["t_high"], highs)] for i in range(len(lines))]
        sides.append(groups)
    sums = home_sums(sides, bounds)
    v["to_lines"], v["to_chips"] = sums[: len(lines)], sums[len(lines) :]
    v["g1"] += home(v["out1"], 0, 3)
    gate("to_lines", "to_chips", "g1", "out0", "out1")
    v["home_x"], v["home_y"] = [[] for _ in chips], [[] for _ in lines]

    def send_home(a, b):
        for s, ts, held in zip(chips, v["to_chips"], v["home_x"]):
            held += [grid.chip(t, -s) for t in ts[a:b]]
        for r, ts, held in zip(lines, v["to_lines"], v["home_y"]):
            held += [grid.line(t, -r) for t in ts[a:b]]

    send_home(0, 1)
    v["m0"] += home(v["out0"], 4, 2)
    v["m1"] = [v["out1"][4], *home(v["out1"], 4, 1)]
    v["b1"] = backward(1)
    v["dense"] = weight_part(pos_dense, [v["b0"][1], v["b1"][1]], grid.chips, grid.cores, n_exp)
    if not in_kernel(shard // n_exp):
        order = jnp.argsort(jnp.stack(steps))
        v["dense"] = [
            p.reshape(grid.chips, n_exp, shard // n_exp, WIDE)[:, order].reshape(p.shape) for p in v["dense"]
        ]
    gate("dense", "home_x", "home_y", "to_chips", "to_lines", "m0", "m1", "out0", "out1")

    v["dense_core"] = grid.cores_moved(v["dense"])
    send_home(1, 2)
    v["m1"] += home(v["out1"], 4, 3)
    gate("dense_core", "dense", "home_x", "home_y", "to_chips", "to_lines", "m1", "out0", "out1")

    split = WIDE // 2 // 128 * 128
    small = shard // n_exp
    sums = [
        grid.cores_added(v["dense"], v["dense_core"], s).reshape(grid.major, grid.minor, small, WIDE)
        for s in range(grid.chips)
    ]
    v["left"], v["right"] = [x[..., :split].astype(bf16) for x in sums], [x[..., split:].astype(bf16) for x in sums]
    v["left_far"] = [grid.chip(v["left"][s], -s) for s in chips]
    right = jnp.stack(v["right"])
    v["right_far"] = [grid.line(right[:, :, r], -r) for r in lines]
    v["m1"] += home(v["out1"], 4, 2)
    gate("left", "right", "left_far", "right_far", "m1", "to_chips", "to_lines", "out0")

    left = v["left"][0].astype(f32)
    for part in v["left_far"]:
        left = left + part.astype(f32)
    right = jnp.stack(v["right"])[:, :, 0].astype(f32)
    for part in v["right_far"]:
        right = right + part.astype(f32)
    v["left"], v["right"] = left[:, 0], right[0]
    v["left_far"] = [grid.line(left[:, r].astype(bf16), -r) for r in lines]
    v["right_far"] = [grid.chip(right[s].astype(bf16), -s) for s in chips]
    v["m0"] += home(v["out0"], 4, 3)
    gate("left", "right", "left_far", "right_far", "to_chips", "to_lines", "m0")

    left, right = v["left"], v["right"]
    for part in v["left_far"]:
        left = left + part.astype(f32)
    for part in v["right_far"]:
        right = right + part.astype(f32)
    mine = grid.major_home(jnp.concatenate([left, right], axis=-1))
    send_home(2, 3)
    outputs = []
    for i in range(MB):
        total = v["m%d" % i][0]
        for part in v["m%d" % i][1:]:
            total = total + part.astype(f32)
        outputs.append((v["f%d" % i][1] + resid_mult * total).astype(bf16))
    grad_rows = [v["b0"][0], v["b1"][0]]

    total = grid.cores_added(v["dw_own"], v["own_core"], 0)
    for parts in (*v["home_y"], *v["home_x"]):
        total = total + jnp.concatenate(parts, axis=0).astype(f32)
    grad_gate_up, grad_down = total[:, :, : 2 * FFE], total[:, :, 2 * FFE :].transpose(0, 2, 1)

    return (
        jnp.stack(outputs)[:, None],
        jnp.stack(grad_rows)[:, None],
        mine[:, QKV + EXPERTS],
        mine[:, :QD],
        mine[:, QD : QD + KD],
        mine[:, QD + KD : QKV],
        mine[:, WO:].T,
        mine[:, QKV + EXPERTS + 1],
        mine[:, QKV : QKV + EXPERTS],
        grad_gate_up,
        grad_down,
    )


def solution(mesh):
    grid = Grid(mesh.shape["dp"], mesh.shape["expert"])
    in_specs = (
        P(None, ("dp", "expert"), None, None),
        P(None, ("dp", "expert"), None),
        P(None, ("dp", "expert"), None, None),
        P(),
        P("dp", None),
        P("dp", None),
        P("dp", None),
        P(None, "dp"),
        P(),
        P("dp", None),
        P("expert", "dp", None),
        P("expert", None, "dp"),
        P(None, ("dp", "expert"), None, None),
    )
    out_specs = (
        P(None, ("dp", "expert"), None, None),
        P(None, ("dp", "expert"), None, None),
        P(("dp", "expert")),
        P(("dp", "expert"), None),
        P(("dp", "expert"), None),
        P(("dp", "expert"), None),
        P(None, ("dp", "expert")),
        P(("dp", "expert")),
        P(("dp", "expert"), None),
        P("expert", "dp", None),
        P("expert", None, "dp"),
    )
    return jax.shard_map(
        functools.partial(on_device, grid), mesh=mesh, in_specs=in_specs, out_specs=out_specs, check_vma=False
    )
```

```python
import functools

import jax
import jax.numpy as jnp
from jax import lax
from jax.experimental import pallas as pl
from jax.experimental.pallas import tpu as pltpu
from jax.sharding import PartitionSpec as P

D = 1024
QUERY_HEADS = 16
KEY_VALUE_HEADS = 8
HEAD_SIZE = 64
FFE = 512
EXPERTS = 32
TOP = 8
SEG_LEN = 16
BRANCHES = 4
MB = 2
TRUNK = 64
NSEG = 13
TREE_TOKENS = 256
QD = 1024
KD = 512
CAP = 72
CAP_PAD = 80
QKV = QD + 2 * KD
WIDE = QKV + 128 + D
WO = QKV + 128
PAIR = 3 * FFE
EXT = 16
PAY = TREE_TOKENS + EXT

epsilon = 1e-06
attn_mult = 0.015625
resid_mult = 0.22
theta_base = 10000.0
neg_fill = -1e30

f32 = jnp.float32
bf16 = jnp.bfloat16
VMEM_LIMIT = 60 * 1024 * 1024


def dot(a, b, ca=1, cb=0):
    return lax.dot_general(a, b, (((ca,), (cb,)), ((), ())), preferred_element_type=f32)


def lanes(shape):
    return lax.broadcasted_iota(jnp.int32, shape, len(shape) - 1)


def params(**extra):
    return pltpu.CompilerParams(vmem_limit_bytes=VMEM_LIMIT, **extra)


def whole(shape):
    return pl.BlockSpec(shape, lambda *_: (0,) * len(shape))


def cost(flops, size, exps=0):
    return pl.CostEstimate(flops=int(flops), bytes_accessed=int(size), transcendentals=int(exps))


def tree_layout():
    row_index = jnp.arange(TREE_TOKENS, dtype=jnp.int32)
    branch_rest = row_index - TRUNK
    leaf_rest = branch_rest - BRANCHES * SEG_LEN
    in_trunk = row_index < TRUNK
    in_branch = branch_rest < BRANCHES * SEG_LEN
    segment = jnp.where(
        in_trunk,
        0,
        jnp.where(in_branch, 1 + branch_rest // SEG_LEN, 1 + BRANCHES + leaf_rest // SEG_LEN),
    )
    position = jnp.where(
        in_trunk,
        row_index,
        jnp.where(in_branch, TRUNK + branch_rest % SEG_LEN, TRUNK + SEG_LEN + leaf_rest % SEG_LEN),
    )
    return (segment, position)


def rope_tables(position):
    half_width = HEAD_SIZE // 2
    inverse_freq = theta_base ** (-2.0 * jnp.arange(half_width, dtype=f32) / HEAD_SIZE)
    angles = position.astype(f32)[:, None] * inverse_freq[None, :]
    c, s = jnp.cos(angles), jnp.sin(angles)
    return jnp.concatenate([c, c, c, c], axis=1), jnp.concatenate([-s, s, -s, s], axis=1)


def mask_bias(parent_row, segment):
    seg_ids = jnp.arange(NSEG, dtype=jnp.int32)
    parent_hot = (parent_row[:, None] == seg_ids[None, :]).astype(f32)
    ancestor = jnp.eye(NSEG, dtype=f32) + parent_hot + jnp.dot(parent_hot, parent_hot)
    seg_hot = (segment[:, None] == seg_ids[None, :]).astype(f32)
    reach = jnp.dot(jnp.dot(seg_hot, ancestor), seg_hot.T)
    rows = jnp.arange(TREE_TOKENS, dtype=jnp.int32)
    allowed = (reach > 0.5) & (rows[None, :] <= rows[:, None])
    return jnp.where(allowed, 0.0, neg_fill).astype(f32)


def swap_halves(u):
    first = (lanes(u.shape) % HEAD_SIZE) < HEAD_SIZE // 2
    return jnp.where(first, pltpu.roll(u, 96, 1), pltpu.roll(u, 32, 1))


def twice(u, upper):
    low = lanes(u.shape) < HEAD_SIZE
    turned = pltpu.roll(u, HEAD_SIZE, 1)
    return jnp.where(low, turned, u) if upper else jnp.where(low, u, turned)


def split_heads(u):
    low = lanes(u.shape) < HEAD_SIZE
    zero = jnp.zeros_like(u)
    return jnp.concatenate([jnp.where(low, u, zero), jnp.where(low, zero, u)], axis=0)


def softmax_rows(scores, bias):
    s = scores.reshape(2, TREE_TOKENS, TREE_TOKENS) * attn_mult + bias[None]
    e = jnp.exp(s - jnp.max(s, axis=-1, keepdims=True))
    p = e * (1.0 / jnp.sum(e, axis=-1, keepdims=True))
    return p.reshape(2 * TREE_TOKENS, TREE_TOKENS)


def gather_weights(refs, offsets, to, sem, wait):
    for i, ref in enumerate(refs):
        rows = ref.shape[0]
        copy = pltpu.make_async_copy(
            ref, to.at[pl.ds(pl.multiple_of(offsets[i], rows), rows)], sem.at[i]
        )
        if wait:
            copy.wait()
        else:
            copy.start()


def forward_kernel(n_dense, offsets, *refs):
    tokens, bias, cos2, sin2, gain_a, gain_m, routes = refs[:7]
    dense = refs[7 : 7 + n_dense]
    xnp, hidden_out, q_out, k2_out, v2_out, mixed_out, gates_out = refs[7 + n_dense : 14 + n_dense]
    w, sem = refs[14 + n_dense :]
    gather_weights(dense, offsets, w, sem, False)
    x = tokens[...].astype(f32)
    r1 = lax.rsqrt(jnp.mean(x * x, axis=1, keepdims=True) + epsilon)
    xn1 = (x * r1 * gain_a[...]).astype(bf16)
    gather_weights(dense, offsets, w, sem, True)
    qkv = dot(xn1, w[:, :QKV])
    c, s = cos2[...], sin2[...]
    for m in range(KEY_VALUE_HEADS):
        u = qkv[:, 128 * m : 128 * m + 128]
        q_out[:, 128 * m : 128 * m + 128] = (u * c + swap_halves(u) * s).astype(bf16)
    for n in range(KEY_VALUE_HEADS // 2):
        u = qkv[:, QD + 128 * n : QD + 128 * n + 128]
        u = u * c + swap_halves(u) * s
        o = qkv[:, QD + KD + 128 * n : QD + KD + 128 * n + 128]
        for half in range(2):
            at = 128 * (2 * n + half)
            k2_out[:, at : at + 128] = twice(u, half).astype(bf16)
            v2_out[:, at : at + 128] = twice(o, half).astype(bf16)

    def one(m, carry):
        at = pl.ds(pl.multiple_of(m * 128, 128), 128)
        qq = split_heads(q_out[:, at])
        p = softmax_rows(dot(qq, k2_out[:, at], 1, 1), bias[...]).astype(bf16)
        o = dot(p, v2_out[:, at])
        low = lanes((TREE_TOKENS, 128)) < HEAD_SIZE
        mixed_out[:, at] = jnp.where(low, o[:TREE_TOKENS], o[TREE_TOKENS:]).astype(bf16)
        return carry

    lax.fori_loop(0, KEY_VALUE_HEADS, one, 0, unroll=2)
    h = x + resid_mult * dot(mixed_out[...], w[:, WO:], 1, 1)
    hidden_out[...] = h
    r2 = lax.rsqrt(jnp.mean(h * h, axis=1, keepdims=True) + epsilon)
    xn2 = (h * r2 * gain_m[...]).astype(bf16)
    xnp[:TREE_TOKENS] = xn2
    lt = dot(xn2, w[:, QKV:WO]).T[:EXPERTS]
    ids = lax.broadcasted_iota(jnp.int32, (EXPERTS, TREE_TOKENS), 0)
    named = ids == routes[0:1, :]
    for k in range(1, TOP):
        named = named | (ids == routes[k : k + 1, :])
    lt = jnp.where(named, lt, neg_fill)
    e = jnp.where(named, jnp.exp(lt - jnp.max(lt, axis=0, keepdims=True)), 0.0)
    g = e / jnp.sum(e, axis=0, keepdims=True)
    gates_out[...] = g
    packed = pack_rows(g)
    hi = packed.astype(bf16)
    low_part = (packed - hi.astype(f32)).astype(bf16)
    xnp[TREE_TOKENS:] = jnp.concatenate([hi.astype(f32), low_part.astype(f32)], axis=0).astype(bf16)


def pack_rows(g):
    return jnp.concatenate([g[8 * i : 8 * i + 8] for i in range(4)], axis=1)


def unpack_rows(g):
    return jnp.concatenate([g[:, 256 * i : 256 * i + 256] for i in range(4)], axis=0)


def any_space(n):
    return [pl.BlockSpec(memory_space=pl.ANY)] * n


def forward_part(offsets, tokens, bias, tables, gain_a, gain_m, routes, dense):
    t = TREE_TOKENS
    ins = [tokens, bias, *tables, gain_a, gain_m, routes]
    outs = [((PAY, D), bf16), ((t, D), f32)] + [((t, QD), bf16)] * 4 + [((EXPERTS, t), f32)]
    return pl.pallas_call(
        functools.partial(forward_kernel, len(dense)),
        grid_spec=pltpu.PrefetchScalarGridSpec(
            num_scalar_prefetch=1,
            grid=(1,),
            in_specs=[whole(a.shape) for a in ins] + any_space(len(dense)),
            out_specs=[whole(s) for s, _ in outs],
            scratch_shapes=[pltpu.VMEM((D, WIDE), bf16), pltpu.SemaphoreType.DMA((len(dense),))],
        ),
        out_shape=[jax.ShapeDtypeStruct(s, d) for s, d in outs],
        compiler_params=params(),
        cost_estimate=cost(1, 1),
        name="attention_forward",
    )(offsets, *ins, *dense)


def expert_kernel(layout, local, n_before, last, pos, *refs):
    refs = list(refs)

    def take(n):
        out = refs[:n]
        del refs[:n]
        return out

    n_dp = len(layout)
    rows_in, cots_in = take(5), take(5)
    weights = [take(len(sizes)) for sizes in layout]
    before_in = [take(3) for _ in range(n_before)]
    outs = take(8) if last else take(3)
    sent_out, hid_out, gboth_out, geo_out = take(4)
    rank_s, gate_s, x1_s, x3_s, c1_s, c3_s, w_s, w_sem = take(8)
    sel_s, comb_s, gg_s = take(3) if last else outs
    before_s = [take(3) for _ in range(n_before)]
    before_sem = take(1)[0] if n_before else None
    e = pl.program_id(0)
    shard = D // n_dp
    base = pos[n_dp] * local
    at_start, at_end = pos[n_dp + 1] == 0, pos[n_dp + 1] == 3
    t = TREE_TOKENS
    ids = lax.broadcasted_iota(jnp.int32, (EXPERTS, t), 0)
    xs = [rows_in[0], x1_s, rows_in[2], x3_s]
    cots = [cots_in[0], c1_s, cots_in[2], c3_s]

    def load(expert, slot):
        for p, (parts, sizes) in enumerate(zip(weights, layout)):
            to = w_s.at[slot, pl.ds(pl.multiple_of(pos[p] * shard, shard), shard)]
            offset = 0
            for part, size in zip(parts, sizes):
                if len(sizes) == 1:
                    pltpu.make_async_copy(part.at[expert], to, w_sem.at[slot, p]).start()
                else:

                    @pl.when((expert >= offset) & (expert < offset + size))
                    def _():
                        pltpu.make_async_copy(part.at[expert - offset], to, w_sem.at[slot, p]).start()

                offset += size

    def arrive(slot):
        for p in range(n_dp):
            to = w_s.at[slot, pl.ds(pl.multiple_of(pos[p] * shard, shard), shard)]
            pltpu.make_async_copy(weights[p][0].at[0], to, w_sem.at[slot, p]).wait()

    slot_now = e % 2

    @pl.when(e == 0)
    def _():
        load(0, 0)

    @pl.when(e + 1 < local)
    def _():
        load(e + 1, 1 - slot_now)

    @pl.when(e == 0)
    def _():
        for given, lower, upper in ((rows_in, x1_s, x3_s), (cots_in, c1_s, c3_s)):
            lower[...] = jnp.where(at_start, given[4][...], given[1][...])
            upper[...] = jnp.where(at_end, given[4][...], given[3][...])
        gates = []
        for b in range(4):
            ext = xs[b][t:].astype(f32)
            full = unpack_rows(ext[:8] + ext[8:16])
            gates.append(
                [
                    jnp.sum(jnp.where(ids == base + el, full, 0.0), axis=0, keepdims=True)
                    for el in range(local)
                ]
            )
        before = lax.broadcasted_iota(jnp.int32, (t, t), 0) < lax.broadcasted_iota(jnp.int32, (t, t), 1)
        before = before.astype(f32).astype(bf16)
        for el in range(local):
            gate = jnp.concatenate([gates[b][el] for b in range(4)] + [jnp.zeros((4, t), f32)], axis=0)
            used = gate > 0.0
            rank = dot(used.astype(f32).astype(bf16), before)
            gate_s[el] = gate
            rank_s[el] = jnp.where(used, rank, -1.0)
        for i, (given, held) in enumerate(zip(before_in, before_s)):
            for j in range(3):
                pltpu.make_async_copy(given[j], held[j], before_sem.at[i, j]).start()

    gate, rank = gate_s[e], rank_s[e]
    slot = lax.broadcasted_iota(jnp.int32, (CAP_PAD, t), 0).astype(f32)
    sels, sent, cot, gate_slot = [], [], [], []
    for b in range(4):
        sel = jnp.where(slot == rank[b : b + 1], 1.0, 0.0)
        sel_s[b, pl.ds(pl.multiple_of(e * CAP_PAD, 16), CAP_PAD)] = sel.astype(bf16)
        sel = sel[:CAP]
        hit = sel > 0.0
        sels.append(sel)
        low = sel.astype(bf16)
        sent.append(dot(low, xs[b][:t]))
        cot.append(dot(low, cots[b][:t]))
        gate_slot.append(jnp.sum(jnp.where(hit, gate[b : b + 1], 0.0), axis=1, keepdims=True))
    sent_out[0] = jnp.concatenate(sent, axis=0).astype(bf16)
    gm = jnp.concatenate(cot, axis=0) * resid_mult
    gate_slot = jnp.concatenate(gate_slot, axis=0)
    geo_out[0] = (gm * gate_slot).astype(bf16)
    arrive(slot_now)
    both = dot(sent_out[0], w_s[slot_now, :, : 2 * FFE])
    gh, up = both[:, :FFE], both[:, FFE:]
    sigma = 1.0 / (1.0 + jnp.exp(-gh))
    hid_out[0] = (gh * sigma * up).astype(bf16)
    eo = dot(hid_out[0], w_s[slot_now, :, 2 * FFE :], 1, 1).astype(bf16).astype(f32)
    gs = dot(geo_out[0], w_s[slot_now, :, 2 * FFE :]) * sigma
    gboth_out[0] = jnp.concatenate(
        [(gs * up * (1.0 + gh * (1.0 - sigma))).astype(bf16), (gs * gh).astype(bf16)], axis=1
    )
    grad_sent = dot(gboth_out[0], w_s[slot_now, :, : 2 * FFE], 1, 1)
    gg = jnp.sum(gm * eo, axis=1, keepdims=True)
    weighted = gate_slot * eo
    ggs = []
    for b in range(4):
        part = slice(CAP * b, CAP * b + CAP)
        where = pl.ds(pl.multiple_of(e * CAP_PAD, 16), CAP_PAD)
        rest = jnp.zeros((CAP_PAD - CAP, D), f32)
        comb_s[b, where, :D] = jnp.concatenate([grad_sent[part], rest], axis=0).astype(bf16)
        comb_s[b, where, D:] = jnp.concatenate([weighted[part], rest], axis=0).astype(bf16)
        ggs.append(jnp.sum(sels[b] * gg[part], axis=0, keepdims=True))
    gg_s[e] = jnp.concatenate(ggs + [jnp.zeros((4, t), f32)], axis=0)

    if not last:
        return

    @pl.when(e == local - 1)
    def _():
        for i, (given, held) in enumerate(zip(before_in, before_s)):
            for j in range(3):
                pltpu.make_async_copy(given[j], held[j], before_sem.at[i, j]).wait()
        for b in range(4):
            total = dot(sel_s[b], comb_s[b], 0, 0)
            full = jnp.zeros((EXPERTS, t), f32)
            for el in range(local):
                full = full + jnp.where(ids == base + el, gg_s[el, b : b + 1], 0.0)
            for i, (sel_b, comb_b, gg_b) in enumerate(before_s):
                total = total + dot(sel_b[b], comb_b[b], 0, 0)
                owner = pos[n_dp + 2 + i] * local
                for el in range(local):
                    full = full + jnp.where(ids == owner + el, gg_b[el, b : b + 1], 0.0)
            outs[b][:t] = total[:, :D].astype(outs[b].dtype)
            outs[4 + b][...] = total[:, D:].astype(outs[4 + b].dtype)
            packed = pack_rows(full)
            hi = packed.astype(bf16)
            rest = (packed - hi.astype(f32)).astype(bf16)
            ext = jnp.concatenate([hi.astype(f32), rest.astype(f32)], axis=0)
            outs[b][t:] = ext.astype(outs[b].dtype)


def expert_part(pos, rows, cots, weights, before, last):
    n_dp = len(weights)
    local = sum(part.shape[0] for part in weights[0])
    t = TREE_TOKENS
    m = CAP * 4
    layout = tuple(tuple(part.shape[0] for part in parts) for parts in weights)
    flat = [part for parts in weights for part in parts]
    earlier = [a for one in before for a in one]
    ins = [*rows, *cots, *flat, *earlier]
    in_specs = [whole(a.shape) for a in (*rows, *cots)]
    in_specs += [pl.BlockSpec(memory_space=pl.ANY)] * len(flat)
    in_specs += any_space(len(earlier))
    passed = [
        ((4, local * CAP_PAD, t), bf16),
        ((4, local * CAP_PAD, 2 * D), bf16),
        ((local, 8, t), f32),
    ]
    if last:
        kinds = [f32, bf16, bf16, bf16]
        outs = [((PAY, D), k) for k in kinds] + [((t, D), k) for k in kinds]
    else:
        outs = list(passed)
    n_main = len(outs)
    out_specs = [whole(s) for s, _ in outs]
    kept = [D, FFE, 2 * FFE, D]
    outs = outs + [((local, m, w), bf16) for w in kept]
    out_specs = out_specs + [pl.BlockSpec((1, m, w), lambda e, *_: (e, 0, 0)) for w in kept]
    scratch = [
        pltpu.VMEM((local, 8, t), f32),
        pltpu.VMEM((local, 8, t), f32),
        pltpu.VMEM((PAY, D), bf16),
        pltpu.VMEM((PAY, D), bf16),
        pltpu.VMEM(cots[0].shape, bf16),
        pltpu.VMEM(cots[0].shape, bf16),
        pltpu.VMEM((2, D, PAIR), bf16),
        pltpu.SemaphoreType.DMA((2, n_dp)),
    ]
    if last:
        scratch += [pltpu.VMEM(s, d) for s, d in passed]
    scratch += [pltpu.VMEM(a.shape, a.dtype) for a in earlier]
    if before:
        scratch.append(pltpu.SemaphoreType.DMA((len(before), 3)))
    res = pl.pallas_call(
        functools.partial(expert_kernel, layout, local, len(before), last),
        grid_spec=pltpu.PrefetchScalarGridSpec(
            num_scalar_prefetch=1,
            grid=(local,),
            in_specs=in_specs,
            out_specs=out_specs,
            scratch_shapes=scratch,
        ),
        out_shape=[jax.ShapeDtypeStruct(s, d) for s, d in outs],
        compiler_params=params(),
        cost_estimate=cost(1, 1),
        name="experts",
    )(pos, *ins)
    return res[:n_main], res[n_main:]


def expert_grad_kernel(n_dp, n_kept, pos, *refs):
    kept = [refs[4 * i : 4 * i + 4] for i in range(n_kept)]
    outs = refs[4 * n_kept :]
    shard = D // n_dp
    for p in range(n_dp):
        at = pl.ds(pl.multiple_of(pos[p] * shard, shard), shard)
        gate_up, down = None, None
        for sent, hid, gboth, geo in kept:
            part = dot(sent[0, :, at], gboth[0], 0, 0)
            gate_up = part if gate_up is None else gate_up + part
            part = dot(geo[0, :, at], hid[0], 0, 0)
            down = part if down is None else down + part
        out = outs[p % len(outs)]
        out[p // len(outs), 0, :, : 2 * FFE] = gate_up.astype(out.dtype)
        out[p // len(outs), 0, :, 2 * FFE :] = down.astype(out.dtype)


def expert_grads(pos, kept, chips, cores):
    local, m, _ = kept[0][0].shape
    n_dp = chips * cores
    shard = D // n_dp
    flat = [a for one in kept for a in one]
    shape = (chips, local, shard, PAIR)
    return pl.pallas_call(
        functools.partial(expert_grad_kernel, n_dp, len(kept)),
        grid_spec=pltpu.PrefetchScalarGridSpec(
            num_scalar_prefetch=1,
            grid=(local,),
            in_specs=[pl.BlockSpec((1, *a.shape[1:]), lambda e, *_: (e, 0, 0)) for a in flat],
            out_specs=[pl.BlockSpec((chips, 1, shard, PAIR), lambda e, *_: (0, e, 0, 0))] * cores,
        ),
        out_shape=[jax.ShapeDtypeStruct(shape, bf16)] * cores,
        compiler_params=params(),
        cost_estimate=cost(1, 1),
        name="expert_grads",
    )(pos, *flat)


def home_kernel(sides, bounds, *refs):
    refs = list(refs)
    e = pl.program_id(0)
    work = []
    for groups in sides:
        work.append([[(refs.pop(0), at) for _, _, at in group] for group in groups])
    for (groups, held) in zip(sides, work):
        outs = [refs.pop(0) for _ in bounds]
        whole_groups, part_groups = [], []
        for group, here in zip(groups, held):
            first, stop = group[0][2], group[-1][2] + group[-1][0].shape[-3]
            (whole_groups if (first, stop) == (0, bounds[-1][1]) else part_groups).append((first, stop, here))
        shape = outs[0].shape

        def value(here):
            total = None
            for ref, at in here:
                one = ref[...].reshape(shape).astype(f32)
                total = one if total is None else jnp.where(e >= at, one, total)
            return total

        base = None
        for _, _, here in whole_groups:
            base = value(here) if base is None else base + value(here)
        for (a, b), out in zip(bounds, outs):

            @pl.when((e >= a) & (e < b))
            def _(a=a, b=b, out=out):
                total = base
                for first, stop, here in part_groups:
                    if first <= a and b <= stop:
                        total = total + value(here)
                out[...] = total.astype(out.dtype)


def home_sums(sides, bounds):
    ins, specs = [], []
    for groups in sides:
        for group in groups:
            for array, chip, first in group:

                def at(e, chip=chip, first=first, size=array.shape[-3]):
                    place = jnp.clip(e - first, 0, size - 1)
                    return (place, 0, 0) if chip is None else (chip, place, 0, 0)

                ins.append(array)
                specs.append(pl.BlockSpec((1,) * (array.ndim - 2) + array.shape[-2:], at))
    tail = ins[0].shape[-2:]
    shapes = [(b - a, *tail) for _ in sides for a, b in bounds]

    def out_at(e, a=0, n=1):
        return (jnp.clip(e - a, 0, n - 1), 0, 0)

    out_specs = [
        pl.BlockSpec((1, *tail), functools.partial(out_at, a=a, n=b - a)) for _ in sides for a, b in bounds
    ]
    res = pl.pallas_call(
        functools.partial(home_kernel, sides_layout(sides), bounds),
        grid=(bounds[-1][1],),
        in_specs=specs,
        out_specs=out_specs,
        out_shape=[jax.ShapeDtypeStruct(shape, bf16) for shape in shapes],
        compiler_params=params(),
        cost_estimate=cost(1, 1),
        name="home_sums",
    )(*ins)
    n = len(bounds)
    return [res[n * i : n * i + n] for i in range(len(sides))]


def total_kernel(start, firsts, n_alias, *refs):
    refs = list(refs[n_alias:])
    gate_up, down = refs[-2:]
    expert = pl.program_id(0) + start
    total = None
    for places in firsts:
        value = None
        for place in places:
            one = refs.pop(0)[...].reshape(gate_up.shape[1], PAIR).astype(f32)
            value = one if value is None else jnp.where(expert >= place, one, value)
        total = value if total is None else total + value
    gate_up[0] = total[:, : 2 * FFE]
    down[0] = total[:, 2 * FFE :].T


def expert_totals(groups, start, stop, local, held):
    ins, specs = list(held), any_space(len(held))
    for group in groups:
        for array, chip, first in group:

            def at(i, k, chip=chip, first=first, size=array.shape[-3]):
                place = jnp.clip(i + start - first, 0, size - 1)
                return (place, k, 0) if chip is None else (chip, place, k, 0)

            ins.append(array)
            specs.append(pl.BlockSpec((1,) * (array.ndim - 2) + (128, array.shape[-1]), at))
    shard = ins[-1].shape[-2]
    shapes = [(local, shard, 2 * FFE), (local, FFE, shard)]
    return pl.pallas_call(
        functools.partial(total_kernel, start, [[first for *_, first in group] for group in groups], len(held)),
        grid=(stop - start, shard // 128),
        in_specs=specs,
        out_specs=[
            pl.BlockSpec((1, 128, 2 * FFE), lambda i, k: (i + start, k, 0)),
            pl.BlockSpec((1, FFE, 128), lambda i, k: (i + start, 0, k)),
        ],
        out_shape=[jax.ShapeDtypeStruct(shape, f32) for shape in shapes],
        input_output_aliases={i: i for i in range(len(held))},
        compiler_params=params(),
        cost_estimate=cost(1, 1),
        name="expert_totals",
    )(*ins)


def sides_layout(sides):
    return [
        [[(jax.ShapeDtypeStruct(a.shape, a.dtype), c, at) for a, c, at in group] for group in groups] for groups in sides
    ]


def backward_kernel(n_dense, n_grads, offsets, *refs):
    grads = refs[:n_grads]
    tokens, hidden, cot, gates, q, k2, v2, bias, cos2, sin2, gain_a, gain_m = refs[n_grads : n_grads + 12]
    dense = refs[n_grads + 12 : n_grads + 12 + n_dense]
    rest = refs[n_grads + 12 + n_dense :]
    grad_tokens, xn1_out, gqkv_out, gbr_out, xn2_out, gl_out, gains_out = rest[:7]
    gmix, w, sem = rest[7:]
    t = TREE_TOKENS
    gather_weights(dense, offsets, w, sem, False)
    total = grads[0][...].astype(f32)
    for other in grads[1:]:
        total = total + other[...].astype(f32)
    gg = unpack_rows(total[t : t + 8] + total[t + 8 : t + 16])
    g = gates[...]
    gl = g * (gg - jnp.sum(g * gg, axis=0, keepdims=True))
    gl = jnp.concatenate([gl, jnp.zeros((128 - EXPERTS, t), f32)], axis=0).T.astype(bf16)
    gl_out[...] = gl
    gather_weights(dense, offsets, w, sem, True)
    gx2 = total[:t] + dot(gl, w[:, QKV:WO], 1, 1)
    h = hidden[...]
    r2 = lax.rsqrt(jnp.mean(h * h, axis=1, keepdims=True) + epsilon)
    xn2_out[...] = (h * r2 * gain_m[...]).astype(bf16)
    u2 = gx2 * gain_m[...]
    ghs = cot[...].astype(f32) + r2 * u2 - h * (r2 * r2 * r2) * jnp.mean(u2 * h, axis=1, keepdims=True)
    gain2 = jnp.sum(gx2 * h * r2, axis=0, keepdims=True)
    gbr_out[...] = (resid_mult * ghs).astype(bf16)
    gmix[...] = dot(gbr_out[...], w[:, WO:]).astype(bf16)
    low = lanes((t, 128)) < HEAD_SIZE
    c, s = cos2[...], sin2[...]

    def unrotate(w):
        return w * c + swap_halves(w * s)

    def one(n, carry):
        keys, values = [], []
        for half in range(2):
            at = pl.ds(pl.multiple_of(n * 256 + 128 * half, 128), 128)
            qq = split_heads(q[:, at])
            dd = split_heads(gmix[:, at])
            kk = k2[:, at]
            pf = softmax_rows(dot(qq, kk, 1, 1), bias[...])
            gp = dot(dd, v2[:, at], 1, 1)
            gsc = (pf * (gp - jnp.sum(pf * gp, axis=1, keepdims=True))).astype(bf16)
            gq = dot(gsc, kk)
            gq = attn_mult * jnp.where(low, gq[:t], gq[t:])
            gqkv_out[:, at] = unrotate(gq).astype(bf16)
            gk = attn_mult * dot(gsc, qq, 0, 0)
            keys.append(gk + pltpu.roll(gk, HEAD_SIZE, 1))
            gv = dot(pf.astype(bf16), dd, 0, 0)
            values.append(gv + pltpu.roll(gv, HEAD_SIZE, 1))
        at = pl.ds(pl.multiple_of(QD + n * 128, 128), 128)
        gqkv_out[:, at] = unrotate(jnp.where(low, keys[0], keys[1])).astype(bf16)
        at = pl.ds(pl.multiple_of(QD + KD + n * 128, 128), 128)
        gqkv_out[:, at] = jnp.where(low, values[0], values[1]).astype(bf16)
        return carry

    lax.fori_loop(0, KEY_VALUE_HEADS // 2, one, 0)
    gx1 = dot(gqkv_out[...], w[:, :QKV], 1, 1)
    x = tokens[...].astype(f32)
    r1 = lax.rsqrt(jnp.mean(x * x, axis=1, keepdims=True) + epsilon)
    xn1_out[...] = (x * r1 * gain_a[...]).astype(bf16)
    u1 = gx1 * gain_a[...]
    grad_tokens[...] = ghs + r1 * u1 - x * (r1 * r1 * r1) * jnp.mean(u1 * x, axis=1, keepdims=True)
    gain1 = jnp.sum(gx1 * x * r1, axis=0, keepdims=True)
    gains_out[...] = jnp.concatenate([gain1, gain2, jnp.zeros((6, D), f32)], axis=0)


def backward_part(offsets, grads, tokens, hidden, cot, gates, q, k2, v2, bias, tables, gain_a, gain_m, dense):
    t = TREE_TOKENS
    ins = [*grads, tokens, hidden, cot, gates, q, k2, v2, bias, *tables, gain_a, gain_m]
    outs = [
        ((t, D), f32),
        ((t, D), bf16),
        ((t, QKV), bf16),
        ((t, D), bf16),
        ((t, D), bf16),
        ((t, 128), bf16),
        ((8, D), f32),
    ]
    return pl.pallas_call(
        functools.partial(backward_kernel, len(dense), len(grads)),
        grid_spec=pltpu.PrefetchScalarGridSpec(
            num_scalar_prefetch=1,
            grid=(1,),
            in_specs=[whole(a.shape) for a in ins] + any_space(len(dense)),
            out_specs=[whole(s) for s, _ in outs],
            scratch_shapes=[
                pltpu.VMEM((t, D), bf16),
                pltpu.VMEM((D, WIDE), bf16),
                pltpu.SemaphoreType.DMA((len(dense),)),
            ],
        ),
        out_shape=[jax.ShapeDtypeStruct(s, d) for s, d in outs],
        compiler_params=params(),
        cost_estimate=cost(1, 1),
        name="attention_backward",
    )(offsets, *ins, *dense)


def in_kernel(rows):
    return rows % 16 == 0


def weight_kernel(n_dp, n_exp, pos, *refs):
    per = 7
    sets = [refs[per * i : per * i + per] for i in range(MB)]
    outs = refs[per * MB :]
    cores = len(outs)
    shard, small = D // n_dp, D // n_dp // n_exp
    for p in range(n_dp):
        at = pl.ds(pl.multiple_of(pos[p] * shard, shard), shard)

        def product(left, right):
            total = None
            for one in sets:
                part = dot(one[left][:, at], one[right][...], 0, 0)
                total = part if total is None else total + part
            return total

        gains = sets[0][6][:, at]
        for one in sets[1:]:
            gains = gains + one[6][:, at]
        gains = jnp.concatenate(
            [jnp.zeros((EXPERTS, shard), f32), gains, jnp.zeros((120 - EXPERTS, shard), f32)], axis=0
        )
        blocks = [product(0, 1), product(4, 5) + gains.T, product(2, 3)]
        pieces = n_exp if in_kernel(small) else 1
        size = shard // pieces
        for i in range(pieces):
            rows = slice(size * i, size * i + size)
            to = pl.ds(pl.multiple_of(pos[n_dp + i] * size, size), size) if pieces > 1 else slice(None)
            offset = 0
            for value in blocks:
                width = value.shape[1]
                outs[p % cores][p // cores, to, offset : offset + width] = value[rows].astype(bf16)
                offset += width


def weight_part(pos, sets, chips, cores, n_exp):
    flat = [a for one in sets for a in one]
    n_dp = chips * cores
    shape = (chips, D // n_dp, WIDE)
    return pl.pallas_call(
        functools.partial(weight_kernel, n_dp, n_exp),
        grid_spec=pltpu.PrefetchScalarGridSpec(
            num_scalar_prefetch=1,
            grid=(1,),
            in_specs=[whole(a.shape) for a in flat],
            out_specs=[whole(shape)] * cores,
        ),
        out_shape=[jax.ShapeDtypeStruct(shape, bf16)] * cores,
        compiler_params=params(),
        cost_estimate=cost(1, 1),
        name="dense_grads",
    )(pos, *flat)


class Grid:
    def __init__(self, n_dp, n_exp):
        self.n_dp, self.n_exp = n_dp, n_exp
        self.cores = 2 if n_dp % 2 == 0 else 1
        self.chips = n_dp // self.cores
        self.major = 4
        self.minor = n_exp // self.major

    def move(self, x, axis, to):
        major, minor = (self.chips, self.cores) if axis == "dp" else (self.major, self.minor)
        pairs = []
        for i in range(major * minor):
            target = to(*divmod(i, minor))
            if target is not None:
                pairs.append((i, target[0] * minor + target[1]))
        return lax.ppermute(x, axis, pairs)

    def chip(self, x, s):
        return self.move(x, "dp", lambda a, b: ((a + s) % self.chips, b))

    def core(self, x, s):
        return self.move(x, "dp", lambda a, b: (a, (b + s) % self.cores))

    def line(self, x, s):
        return self.move(x, "expert", lambda a, b: (a, (b + s) % self.minor))

    def up(self, x, s):
        return self.move(x, "expert", lambda a, b: ((a + s) % 4, b))

    def next_up(self, x):
        return self.move(x, "expert", lambda a, b: (a + 1, b) if a < 3 else None)

    def next_down(self, x):
        return self.move(x, "expert", lambda a, b: (a - 1, b) if a > 0 else None)

    def outward(self, x):
        return self.move(x, "expert", lambda a, b: {1: (0, b), 2: (3, b)}.get(a))

    def back(self, parts):
        return [self.up(x, -k) for k, x in enumerate(parts, 1)]

    def dp_places(self):
        i = lax.axis_index("dp")
        a, b = i // self.cores, i % self.cores
        return [
            (a - s) % self.chips * self.cores + (b - c) % self.cores
            for s in range(self.chips)
            for c in range(self.cores)
        ]

    def exp_steps(self):
        i = lax.axis_index("expert")
        a, b = i // self.minor, i % self.minor
        return [
            (a - k // self.minor) % self.major * self.minor + (b - k % self.minor) % self.minor
            for k in range(self.n_exp)
        ]

    def cores_moved(self, groups):
        return [self.core(g, -c) for c, g in enumerate(groups) if c]

    def cores_added(self, groups, moved, s, a=None, b=None):
        total = groups[0][s, a:b].astype(f32)
        for part in moved:
            total = total + part[s, a:b].astype(f32)
        return total

    def major_home(self, blocks):
        total = blocks[0]
        for s in range(1, self.major):
            total = total + self.up(blocks[s].astype(bf16), -s).astype(f32)
        return total


def on_device(
    grid,
    tokens,
    parents,
    routes,
    gain_attn,
    w_query,
    key_matrix,
    value_matrix,
    w_out,
    gain_moe,
    router,
    expert_gate_up,
    expert_down,
    cotangent,
):
    n_dp, n_exp = grid.n_dp, grid.n_exp
    shard = D // n_dp
    places = grid.dp_places()
    me = lax.axis_index("expert")
    major, minor = me // grid.minor, me % grid.minor
    steps = grid.exp_steps()
    owners = [major * grid.minor + (minor - r) % grid.minor for r in range(grid.minor)]

    def pos(i, r):
        before = owners[:r] if i == 0 else (owners[1:r] if r else owners[1:])
        return jnp.stack([*places, owners[r], major, *before, jnp.int32(0)]).astype(jnp.int32)

    pos_dense = jnp.stack([*places, *steps]).astype(jnp.int32)
    chips, lines, cores = range(1, grid.chips), range(1, grid.minor), range(grid.cores)
    local = expert_gate_up.shape[0]
    cut = local - local // 2
    v = {}

    def gate(*names):
        flat, tree = jax.tree.flatten([v[name] for name in names])
        v.update(zip(names, jax.tree.unflatten(tree, lax.optimization_barrier(flat))))

    segment, position = tree_layout()
    tables = rope_tables(position)
    gain_a, gain_m = gain_attn.reshape(1, D), gain_moe.reshape(1, D)
    biases = [mask_bias(parents[i, 0], segment) for i in range(MB)]
    for i in range(MB):
        v["tok%d" % i], v["cot%d" % i] = tokens[i, 0], cotangent[i, 0]

    def pairs(a, b):
        if a == b:
            return []
        return [jnp.concatenate([expert_gate_up[a:b], expert_down[a:b].transpose(0, 2, 1)], axis=2)]

    def over_cores(arrays):
        return [[grid.core(x, c) for x in arrays] for c in cores[1:]]

    def joined(*parts):
        return [sum(held, []) for held in zip(*parts)]

    packed = jnp.concatenate(
        [w_query, key_matrix, value_matrix, router, jnp.zeros((shard, 128 - EXPERTS), bf16), w_out.T], axis=1
    )
    half = local // 2
    quarter = half // 2
    v["far"] = [grid.chip(packed, s) for s in chips]
    v["packed"] = packed
    v["wy"] = [[grid.line(w, r) for w in pairs(0, half)] for r in lines]
    v["c0a"], v["c0b"], v["c0c"] = grid.next_up(v["cot0"]), grid.up(v["cot0"], 2), grid.next_down(v["cot0"])
    v["pair"] = pairs(0, local)
    v["xa"], v["xb"], v["xc"] = pairs(0, quarter), pairs(half, local), pairs(quarter, half)
    gate("far", "packed", "wy", "c0a", "c0b", "c0c", "pair", "xa", "xb", "xc")

    v["far_core"] = [[grid.core(f, c) for c in cores[1:]] for f in v["far"]]
    v["packed_core"] = [grid.core(v["packed"], c) for c in cores[1:]]
    gate("far_core", "packed_core", "tok0", "pair", "xa", "xb", "xc", "cot1", "c0b", "wy")

    dense = [packed, *v["packed_core"]]
    for f, fs in zip(v["far"], v["far_core"]):
        dense += [f, *fs]
    offsets = (jnp.stack(places) * shard).astype(jnp.int32)

    def forward(i):
        return forward_part(
            offsets, v["tok%d" % i], biases[i], tables, gain_a, gain_m, routes[i, 0].T, dense
        )

    v["f0"] = forward(0)
    v["wxa"] = [[grid.chip(w, s) for w in v["xa"]] for s in chips]
    v["pair_core"] = over_cores(v["pair"])
    v["c0d"], v["c1b"] = grid.outward(v["c0b"]), grid.up(v["cot1"], 2)
    gate("f0", "wxa", "pair_core", "c0d", "c1b", "tok1", "xb", "xc", "wy")

    row = v["f0"][0]
    v["n0a"], v["n0b"], v["n0c"] = grid.next_up(row), grid.up(row, 2), grid.next_down(row)
    v["wxb"] = [[grid.chip(w, s) for w in v["xb"]] for s in chips]
    v["wyb"] = [[grid.line(w, r) for w in v["xb"]] for r in lines]
    v["f1"] = forward(1)
    gate("n0a", "n0b", "n0c", "wxb", "wyb", "f1", "cot1", "xc", "wy")

    v["wxc"] = [[grid.chip(w, s) for w in v["xc"]] for s in chips]
    v["wxa_core"] = [over_cores(ws) for ws in v["wxa"]]
    v["wxb_core"] = [over_cores(ws) for ws in v["wxb"]]
    v["n0d"] = grid.outward(v["n0b"])
    v["wy_core"] = [over_cores(ws) for ws in v["wy"]]
    gate("wxc", "wxa_core", "wxb_core", "wy_core", "n0d", "f1", "cot1", "wy", "wxb", "wyb")

    v["wxc_core"] = [over_cores(ws) for ws in v["wxc"]]
    v["wyb_core"] = [over_cores(ws) for ws in v["wyb"]]
    gate("wxc_core", "wyb_core", "f1", "cot1", "wy", "wxb")

    own = [tuple(v["pair"]), *[tuple(w) for w in v["pair_core"]]]
    for k in range(len(chips)):
        own.append((*v["wxa"][k], *v["wxc"][k], *v["wxb"][k]))
        own += [tuple(ws) for ws in joined(v["wxa_core"][k], v["wxc_core"][k], v["wxb_core"][k])]

    def experts(i, r, weights, before):
        name = "%d" % i
        rows = [v["f" + name][0], *[v["n" + name + k] for k in "abcd"]]
        cots = [v["cot" + name], *[v["c" + name + k] for k in "abcd"]]
        return expert_part(pos(i, r), rows, cots, weights, before, len(before) == grid.minor - 1)

    v["e00"], v["k00"] = experts(0, 0, own, [])
    row = v["f1"][0]
    v["n1a"], v["n1b"], v["n1c"] = grid.next_up(row), grid.up(row, 2), grid.next_down(row)
    v["low"] = [[[grid.chip(w, s) for w in ws] for s in chips] for ws in v["wy"]]
    v["high"] = [[[grid.line(w, r) for w in ws] for ws in v["wxb"]] for r in lines]
    gate("e00", "low", "high", "n1a", "n1b", "n1c", "f1", "cot1", "c1b", "wy", "wyb")

    v["low_core"] = [[over_cores(w) for w in ws] for ws in v["low"]]
    v["high_core"] = [[over_cores(w) for w in ws] for ws in v["high"]]
    gate("low_core", "high_core", "f1", "n1b", "e00", "cot1", "c1b")

    sets = [own]
    for i in range(len(lines)):
        parts = [(*v["wy"][i], *v["wyb"][i])]
        parts += [tuple(ws) for ws in joined(v["wy_core"][i], v["wyb_core"][i])]
        for k in range(len(chips)):
            parts.append((*v["low"][i][k], *v["high"][i][k]))
            parts += [tuple(ws) for ws in joined(v["low_core"][i][k], v["high_core"][i][k])]
        sets.append(parts)
    v["n1d"] = grid.outward(v["n1b"])
    v["c1d"] = grid.outward(v["c1b"])
    v["c1a"], v["c1c"] = grid.next_up(v["cot1"]), grid.next_down(v["cot1"])
    passed = [v["e00"]]
    for r in lines:
        out, v["k%d0" % r] = experts(0, r, sets[r], passed)
        passed.append(out)
    v["out0"] = passed[-1]
    gate("out0", "c1a", "c1c", "c1d", "n1d", "f1")

    def home(out, first, *steps):
        return [grid.up(out[first + k], -k) for k in steps]

    v["g0"] = [v["out0"][0], *home(v["out0"], 0, 1, 2)]
    passed = []
    for r in lines:
        out, v["k%d1" % r] = experts(1, r, sets[r], passed)
        passed.append(out)
    v["e1"] = passed
    v["dw_other"] = [
        expert_grads(pos_dense, [v["k%d0" % r], v["k%d1" % r]], grid.chips, grid.cores) for r in lines
    ]
    gate("dw_other", "e1", "g0", "out0")

    v["other_core"] = [grid.cores_moved(groups) for groups in v["dw_other"]]
    v["g0"] += home(v["out0"], 0, 3)
    v["m0"] = [v["out0"][4], *home(v["out0"], 4, 1)]
    v["out1"], v["k01"] = experts(1, 0, own, v["e1"])
    gate("out1", "k01", "other_core", "g0", "m0", "dw_other", "out0")

    def backward(i):
        _, hidden, q, k2, v2, mixed, gates = v["f%d" % i]
        grad_tokens, xn1, gqkv, gbr, xn2, gl, gains = backward_part(
            offsets, v["g%d" % i], tokens[i, 0], hidden, cotangent[i, 0], gates, q, k2, v2,
            biases[i], tables, gain_a, gain_m, dense,
        )
        return grad_tokens, (xn1, gqkv, gbr, mixed, xn2, gl, gains)

    def corner(a, b):
        return [
            [grid.cores_added(g, m, s, a, b).astype(bf16) for s in chips]
            for g, m in zip(v["dw_other"], v["other_core"])
        ]

    middle, top = (cut + 1) // 2, cut + (local - cut + 1) // 2
    lows = [(a, b) for a, b in ((0, middle), (middle, cut)) if a < b]
    highs = [(a, b) for a, b in ((cut, top), (top, local)) if a < b]
    v["corner_low"], v["corner_high"] = [corner(*ab) for ab in lows], [corner(*ab) for ab in highs]
    gate("corner_low", "corner_high", "out1", "k01", "g0", "out0")
    v["t_low"], v["t_high"] = [], []

    def send_corner(k):
        for ts in v["corner_low"][k : k + 1]:
            v["t_low"].append([[grid.chip(t, -s) for s, t in zip(chips, row)] for row in ts])
        for ts in v["corner_high"][k : k + 1]:
            v["t_high"].append([[grid.line(t, -r) for t in row] for r, row in zip(lines, ts)])

    send_corner(0)
    v["g1"] = [v["out1"][0], *home(v["out1"], 0, 1)]
    v["dw_own"] = expert_grads(pos_dense, [v["k00"], v["k01"]], grid.chips, grid.cores)
    gate("dw_own", "t_low", "t_high", "g1", "out1", "g0", "corner_low", "corner_high")

    send_corner(1)
    v["own_core"] = grid.cores_moved(v["dw_own"])
    v["g1"] += home(v["out1"], 0, 2)
    v["b0"] = backward(0)
    gate("b0", "own_core", "dw_own", "t_low", "t_high", "g1", "dw_other", "other_core", "out0", "out1")

    bounds = [(a, b) for a, b in ((0, cut), (cut, top), (top, local)) if a < b]
    sides = []
    for i in range(len(lines)):
        groups = [[(v["dw_other"][i][0], 0, 0)]] + [[(m, 0, 0)] for m in v["other_core"][i]]
        groups += [[(t[i][k], None, a) for t, (a, _) in zip(v["t_low"], lows)] for k in range(len(chips))]
        sides.append(groups)
    for k, s in enumerate(chips):
        groups = [[(v["dw_own"][0], s, 0)]] + [[(m, s, 0)] for m in v["own_core"]]
        if highs:
            groups += [[(t[i][k], None, a) for t, (a, _) in zip(v["t_high"], highs)] for i in range(len(lines))]
        sides.append(groups)
    sums = home_sums(sides, bounds)
    v["to_lines"], v["to_chips"] = sums[: len(lines)], sums[len(lines) :]
    v["g1"] += home(v["out1"], 0, 3)
    gate("to_lines", "to_chips", "g1", "out0", "out1")
    v["home_x"], v["home_y"] = [[] for _ in chips], [[] for _ in lines]

    def send_home(a, b):
        for s, ts, held in zip(chips, v["to_chips"], v["home_x"]):
            held += [grid.chip(t, -s) for t in ts[a:b]]
        for r, ts, held in zip(lines, v["to_lines"], v["home_y"]):
            held += [grid.line(t, -r) for t in ts[a:b]]

    send_home(0, 1)
    v["m0"] += home(v["out0"], 4, 2)
    v["m1"] = [v["out1"][4], *home(v["out1"], 4, 1)]
    v["b1"] = backward(1)
    v["dense"] = weight_part(pos_dense, [v["b0"][1], v["b1"][1]], grid.chips, grid.cores, n_exp)
    if not in_kernel(shard // n_exp):
        order = jnp.argsort(jnp.stack(steps))
        v["dense"] = [
            p.reshape(grid.chips, n_exp, shard // n_exp, WIDE)[:, order].reshape(p.shape) for p in v["dense"]
        ]
    gate("dense", "home_x", "home_y", "to_chips", "to_lines", "m0", "m1", "out0", "out1")

    v["dense_core"] = grid.cores_moved(v["dense"])
    send_home(1, 2)
    v["m1"] += home(v["out1"], 4, 3)
    gate("dense_core", "dense", "home_x", "home_y", "to_chips", "to_lines", "m1", "out0", "out1")

    split = WIDE // 2 // 128 * 128
    small = shard // n_exp
    sums = [
        grid.cores_added(v["dense"], v["dense_core"], s).reshape(grid.major, grid.minor, small, WIDE)
        for s in range(grid.chips)
    ]
    v["left"], v["right"] = [x[..., :split].astype(bf16) for x in sums], [x[..., split:].astype(bf16) for x in sums]
    v["left_far"] = [grid.chip(v["left"][s], -s) for s in chips]
    right = jnp.stack(v["right"])
    v["right_far"] = [grid.line(right[:, :, r], -r) for r in lines]
    v["m1"] += home(v["out1"], 4, 2)
    gate("left", "right", "left_far", "right_far", "m1", "to_chips", "to_lines", "out0")

    left = v["left"][0].astype(f32)
    for part in v["left_far"]:
        left = left + part.astype(f32)
    right = jnp.stack(v["right"])[:, :, 0].astype(f32)
    for part in v["right_far"]:
        right = right + part.astype(f32)
    v["left"], v["right"] = left[:, 0], right[0]
    v["left_far"] = [grid.line(left[:, r].astype(bf16), -r) for r in lines]
    v["right_far"] = [grid.chip(right[s].astype(bf16), -s) for s in chips]
    v["m0"] += home(v["out0"], 4, 3)

    def totals(k, n, held):
        groups = [[(v["dw_own"][0], 0, 0)]] + [[(m, 0, 0)] for m in v["own_core"]]
        for parts in (*v["home_y"], *v["home_x"]):
            groups.append([(parts[j], None, bounds[j][0]) for j in range(k, n)])
        return expert_totals(groups, bounds[k][0], bounds[n - 1][1], local, held)

    v["held"] = totals(0, len(bounds) - 1, []) if len(bounds) > 1 else []
    gate("left", "right", "left_far", "right_far", "to_chips", "to_lines", "m0", "held")

    left, right = v["left"], v["right"]
    for part in v["left_far"]:
        left = left + part.astype(f32)
    for part in v["right_far"]:
        right = right + part.astype(f32)
    mine = grid.major_home(jnp.concatenate([left, right], axis=-1))
    send_home(2, 3)
    outputs = []
    for i in range(MB):
        total = v["m%d" % i][0]
        for part in v["m%d" % i][1:]:
            total = total + part.astype(f32)
        outputs.append((v["f%d" % i][1] + resid_mult * total).astype(bf16))
    grad_rows = [v["b0"][0], v["b1"][0]]

    grad_gate_up, grad_down = totals(len(bounds) - 1, len(bounds), v["held"])

    return (
        jnp.stack(outputs)[:, None],
        jnp.stack(grad_rows)[:, None],
        mine[:, QKV + EXPERTS],
        mine[:, :QD],
        mine[:, QD : QD + KD],
        mine[:, QD + KD : QKV],
        mine[:, WO:].T,
        mine[:, QKV + EXPERTS + 1],
        mine[:, QKV : QKV + EXPERTS],
        grad_gate_up,
        grad_down,
    )


def solution(mesh):
    grid = Grid(mesh.shape["dp"], mesh.shape["expert"])
    in_specs = (
        P(None, ("dp", "expert"), None, None),
        P(None, ("dp", "expert"), None),
        P(None, ("dp", "expert"), None, None),
        P(),
        P("dp", None),
        P("dp", None),
        P("dp", None),
        P(None, "dp"),
        P(),
        P("dp", None),
        P("expert", "dp", None),
        P("expert", None, "dp"),
        P(None, ("dp", "expert"), None, None),
    )
    out_specs = (
        P(None, ("dp", "expert"), None, None),
        P(None, ("dp", "expert"), None, None),
        P(("dp", "expert")),
        P(("dp", "expert"), None),
        P(("dp", "expert"), None),
        P(("dp", "expert"), None),
        P(None, ("dp", "expert")),
        P(("dp", "expert")),
        P(("dp", "expert"), None),
        P("expert", "dp", None),
        P("expert", None, "dp"),
    )
    return jax.shard_map(
        functools.partial(on_device, grid), mesh=mesh, in_specs=in_specs, out_specs=out_specs, check_vma=False
    )
```
